32 devices in a mesh: vis: 8 (over z, x), tile: 4 (over y, core).
Axes of the slice: x: 2, y: 2, z: 4, core: 2. Of those that a mesh axis runs over, the one named last changes fastest.
Arguments:
- vis_data: bfloat16 [32768, 128], P(('vis', 'tile')), may hold values from -0.59765625 to 0.59765625
- u_cell: int32 [16, 32768], P(None, ('vis', 'tile')), may hold values from 0 to 25
- v_cell: int32 [16, 32768], P(None, ('vis', 'tile')), may hold values from 0 to 25
- u_frac: int32 [16, 32768], P(None, ('vis', 'tile')), may hold values from 0 to 15
- v_frac: int32 [16, 32768], P(None, ('vis', 'tile')), may hold values from 0 to 15
- w_plane: int32 [16, 32768], P(None, ('vis', 'tile')), may hold values from 0 to 7
- block_route: int32 [32768, 1], P(('vis', 'tile')), may hold values from 0 to 63; in each aligned block of 1024 rows (0 to 1023, 1024 to 2047, ...) at most 32 rows name the same one
- kernel_taps: float32 [128, 7], replicated, may hold values from 0.1 to 1
- taper_gain: float32 [32, 32], replicated, may hold values from 0.2 to 1
- sub_tile: int32 [256, 1], P(('vis', 'tile')), may hold values from 0 to 7; in each aligned block of 8 rows (0 to 7, 8 to 15, ...) at most 2 rows name the same one
- sub_anchor: int32 [256, 2], P(('vis', 'tile')), may hold values from 0 to 224
Outputs:
- grid_sum: float32 [8, 256, 2048], P('tile', 'vis')
The draws below stay inside these ranges and needn't reach their ends.
Inputs may be any that keep to these rules, and one draw needn't show every extreme that they name: `block_route`: among the rows of one device at most 32 name one uv-block, and some uv-block is named by exactly 32 of them. `sub_tile`: among the 8 uv-blocks of one device at most 2 map to one grid tile, and some grid tile gets exactly 2 of them.
All inputs are finite; a program needn't handle non-finite values.
Results may differ from the reference program's by a relative error of at most 0.008.
Values may be sent and summed in bfloat16 or wider, within the bound.
A program may use at most 128 MiB of HBM per device.

```python
import math
import jax
import jax.numpy as jnp
import numpy as np
from jax import lax

ROWS_DEV = 1024
BLK_DEV = 8
SUB = 32
CHR = 16
POLC = 8
TAPS = 7
OS = 16
WPL = 8
TS = 256
SCAP = 2
NGROUP = 64
CAP = 32
GT = 8
NROWS = 32768
NBLK = 256
N_VIS = 8
N_TILE = 4
DEVICES = 32


def place_ends(array, key, least, top_value):
    spot = [jax.random.randint(jax.random.fold_in(key, axis), (), 0, length) for axis, length in enumerate(array.shape)]
    widest = array.shape.index(max(array.shape))
    beside = spot[:widest] + [(spot[widest] + 1) % array.shape[widest]] + spot[widest + 1:]
    return array.at[tuple(spot)].set(least).at[tuple(beside)].set(top_value)


def steps_of(own_key, dims, pieces, least, high):
    level, own = 1.0, jax.random.fold_in(own_key, 6)
    for axis_at, parts in pieces:
        steps = jnp.exp(jax.random.uniform(jax.random.fold_in(own, axis_at), (parts,), jnp.float32, least / len(pieces), high / len(pieces)))
        level = level * jnp.repeat(steps, dims[axis_at] // parts).reshape([-1 if axis == axis_at else 1 for axis in range(len(dims))])
    return level


def routed_block(rng, own, number, rows, amount, top, bound, slope):
    ranking = jax.random.permutation(rng, amount)
    heavy_load, ordinary = load_shares(amount, rows * top, bound, slope, True), load_shares(amount, rows * top, bound, slope, False)
    places = jnp.arange(amount)

    def named(tallies, rotation):
        used = int((tallies > 0).sum())
        fixed = max(1, used // 4)
        shifted = fixed + (places - fixed + rotation * (used - fixed)) % max(1, amount - fixed)
        return jnp.zeros((amount,), jnp.int32).at[ranking[jnp.where(places < fixed, places, shifted)]].set(jnp.asarray(tallies, jnp.int32))

    tallies = jnp.where(number % 4 == 0, named(heavy_load, number // 4), named(ordinary, number - number // 4 - 1))
    mixed = jax.random.permutation(jax.random.fold_in(own, 3), amount)
    donor, sink = mixed[0:amount // 2 * 2:2], mixed[1:amount // 2 * 2:2]
    slack = jnp.minimum(tallies[donor] - 1, bound - tallies[sink]) // 2
    slack = jnp.where((donor == ranking[0]) | (sink == ranking[0]) | (tallies[sink] == 0), 0, jnp.maximum(slack, 0))
    shifted = jax.random.randint(jax.random.fold_in(own, 4), (amount // 2,), 0, 1 << 20) % (slack + 1)
    tallies = tallies.at[donor].add(-shifted).at[sink].add(shifted)
    items = jnp.searchsorted(jnp.cumsum(tallies), jnp.arange(rows * top), side="right").astype(jnp.int32)
    grid = items.reshape(top, rows).T
    grid = grid[jax.random.permutation(jax.random.fold_in(own, 1), rows)]
    rotation = jax.random.randint(jax.random.fold_in(own, 2), (rows, 1), 0, top)
    return jnp.take_along_axis(grid, (jnp.arange(top)[None, :] + rotation) % top, axis=1)


def load_shares(number_of, total, bound, skew, full):
    portions = [(1 << 20) // math.isqrt(standing ** skew) + 1 for standing in range(1, number_of + 1)]
    largest = bound if full else min(bound, max(-(-total // number_of), total * portions[0] // sum(portions)))
    least = 1 if total - largest >= number_of - 1 else 0
    holding, surplus = [largest] + [least] * (number_of - 1), total - largest - least * (number_of - 1)
    while surplus > 0:
        candidates = [i for i in range(1, number_of) if holding[i] < largest] or [i for i in range(1, number_of) if holding[i] < bound]
        mass, budget = sum([portions[i] for i in candidates]), surplus
        for i in candidates:
            addition = min(bound - holding[i], max(1, budget * portions[i] // mass), surplus)
            holding[i] = holding[i] + addition
            surplus = surplus - addition
    return np.array(holding)


def centred(key, shape, scale, bound, shards=(), kind=jnp.bfloat16):
    result = scale * jax.random.normal(key, shape, jnp.float32)
    if shards:
        result = result * steps_of(key, shape, shards, -0.22, 0.18)
    return jnp.clip(result, -bound, bound).astype(kind)


def setup_inputs(seed: int = 0) -> dict:
    keys = jax.random.split(jax.random.key(seed), 12)
    vis_data = centred(keys[0], (NROWS, CHR * POLC), 0.1, 0.59765625, ((0, 32),))
    u_cell = place_ends(jax.random.randint(keys[1], (CHR, NROWS), 0, SUB - TAPS + 1), jax.random.fold_in(keys[1], 1), 0, SUB - TAPS).astype(jnp.int32)
    v_cell = place_ends(jax.random.randint(keys[2], (CHR, NROWS), 0, SUB - TAPS + 1), jax.random.fold_in(keys[2], 1), 0, SUB - TAPS).astype(jnp.int32)
    u_frac = place_ends(jax.random.randint(keys[3], (CHR, NROWS), 0, OS), jax.random.fold_in(keys[3], 1), 0, OS - 1).astype(jnp.int32)
    v_frac = place_ends(jax.random.randint(keys[4], (CHR, NROWS), 0, OS), jax.random.fold_in(keys[4], 1), 0, OS - 1).astype(jnp.int32)
    w_plane = place_ends(jax.random.randint(keys[5], (CHR, NROWS), 0, WPL), jax.random.fold_in(keys[5], 1), 0, WPL - 1).astype(jnp.int32)
    block_route_keys = jax.random.split(jax.random.fold_in(keys[6], 1), NROWS // ROWS_DEV)
    block_route_turns = jax.random.permutation(jax.random.fold_in(keys[6], 3), NROWS // ROWS_DEV)
    block_route = jax.vmap(lambda own, number: routed_block(jax.random.fold_in(keys[6], 2), own, number, ROWS_DEV, NGROUP, 1, CAP, 2))(block_route_keys, block_route_turns).reshape((NROWS, 1))
    kernel_taps = jnp.clip(jax.random.uniform(keys[7], (WPL * OS, TAPS), jnp.float32, 0.1, 1.0), 0.1, 1.0)
    taper_gain = jnp.clip(jax.random.uniform(keys[8], (SUB, SUB), jnp.float32, 0.2, 1.0), 0.2, 1.0)
    sub_tile_keys = jax.random.split(jax.random.fold_in(keys[9], 1), NBLK // BLK_DEV)
    sub_tile_turns = jax.random.permutation(jax.random.fold_in(keys[9], 3), NBLK // BLK_DEV)
    sub_tile = jax.vmap(lambda own, number: routed_block(jax.random.fold_in(keys[9], 2), own, number, BLK_DEV, GT, 1, SCAP, 2))(sub_tile_keys, sub_tile_turns).reshape((NBLK, 1))
    sub_anchor = place_ends(jax.random.randint(keys[10], (NBLK, 2), 0, TS - SUB + 1), jax.random.fold_in(keys[10], 1), 0, TS - SUB).astype(jnp.int32)
    return {"vis_data": vis_data, "u_cell": u_cell, "v_cell": v_cell, "u_frac": u_frac, "v_frac": v_frac, "w_plane": w_plane, "block_route": block_route, "kernel_taps": kernel_taps, "taper_gain": taper_gain, "sub_tile": sub_tile, "sub_anchor": sub_anchor}


def spread(cell_idx, taps):
    offset = jnp.arange(SUB, dtype=jnp.int32)[None, :] - cell_idx[:, None]
    spread_sum = jnp.zeros((cell_idx.shape[0], SUB), jnp.float32)
    for tap_index in range(TAPS):
        spread_sum = spread_sum + jnp.where(offset == tap_index, taps[:, tap_index:tap_index + 1], 0.0)
    return spread_sum.astype(jnp.bfloat16)


def grid_block(samples, code_rows, kernel_taps, taper_gain):
    taps_u = kernel_taps[code_rows[2]]
    taps_v = kernel_taps[code_rows[3]]
    weight_u = spread(code_rows[0], taps_u)
    weight_v = spread(code_rows[1], taps_v)
    weighted = (weight_u.astype(jnp.float32)[:, :, None] * samples.astype(jnp.float32)[:, None, :]).astype(jnp.bfloat16)
    weighted = weighted.reshape(samples.shape[0], SUB * POLC)
    subgrid = jnp.dot(weight_v.T, weighted, preferred_element_type=jnp.float32)
    return subgrid * jnp.repeat(taper_gain, POLC, axis=1)


def place_tiles(canvas, sub_grids, tile_ids, anchors, first_tile):
    tile_count = canvas.shape[0]

    def add_one(slot_index, canvas):
        target = (tile_ids[slot_index] - first_tile).astype(jnp.int32)
        inside = (target >= 0) & (target < tile_count)
        target = jnp.clip(target, 0, tile_count - 1).astype(jnp.int32)
        corner = (target, anchors[slot_index, 0].astype(jnp.int32), (anchors[slot_index, 1] * POLC).astype(jnp.int32))
        window = lax.dynamic_slice(canvas, corner, (1, SUB, SUB * POLC))
        addend = jnp.where(inside, sub_grids[slot_index], 0.0)[None]
        return lax.dynamic_update_slice(canvas, window + addend, corner)

    return lax.fori_loop(0, sub_grids.shape[0], add_one, canvas)


def rank_rows(row_route):
    onehot = (row_route[:, None] == jnp.arange(NGROUP, dtype=jnp.int32)[None, :]).astype(jnp.int32)
    before = jnp.cumsum(onehot, axis=0) - onehot
    return jnp.sum(before * onehot, axis=1).astype(jnp.int32)


def reference(vis_data, u_cell, v_cell, u_frac, v_frac, w_plane, block_route, kernel_taps, taper_gain, sub_tile, sub_anchor):
    flat_route = block_route[:, 0].astype(jnp.int32)
    row_rank = lax.map(rank_rows, flat_route.reshape(DEVICES, ROWS_DEV)).reshape(-1)
    device = jnp.arange(NROWS, dtype=jnp.int32) // ROWS_DEV
    vis_index = device // N_TILE
    tile_index = device % N_TILE
    block_id = ((flat_route // BLK_DEV) * N_TILE + tile_index) * BLK_DEV + flat_route % BLK_DEV
    slot_id = vis_index * CAP + row_rank
    slot_table = jnp.full((NBLK, N_VIS * CAP), -1, jnp.int32).at[block_id, slot_id].set(jnp.arange(NROWS, dtype=jnp.int32))
    table_u = w_plane * OS + u_frac
    table_v = w_plane * OS + v_frac
    codes_all = jnp.stack([u_cell.T, v_cell.T, table_u.T, table_v.T], axis=1).astype(jnp.int32)

    def grid_one(slot_rows):
        is_live = slot_rows >= 0
        safe_rows = jnp.maximum(slot_rows, 0)
        samples = jnp.where(is_live[:, None], vis_data[safe_rows], jnp.zeros((), jnp.bfloat16))
        samples = samples.reshape(-1, POLC)
        code_rows = jnp.transpose(codes_all[safe_rows], (1, 0, 2)).reshape(4, -1)
        return grid_block(samples, code_rows, kernel_taps, taper_gain)

    subgrids = lax.map(grid_one, slot_table)
    canvas = jnp.zeros((GT, TS, TS * POLC), jnp.float32)
    return place_tiles(canvas, subgrids, sub_tile[:, 0].astype(jnp.int32), sub_anchor, 0)
```

```python
import functools

import jax
import jax.numpy as jnp
from jax import lax
from jax.experimental import pallas as pl
from jax.experimental.pallas import tpu as pltpu
from jax.sharding import PartitionSpec as P

BLK_DEV = 8
SUB = 32
POLC = 8
TAPS = 7
OS = 16
TS = 256
GT = 8
SCAP = 2
LANES = 128
ROWS = 8
GROUP = 4
FAR = 1 << 20
MESH = pl.DeviceIdType.MESH
NT = (((1,), (1,)), ((), ()))


def dispatch_kernel(
    slot_cap, regroup, vis, u_cell, v_cell, u_frac, v_frac, w_plane, route, taps, gain, out, table, taper, feat, dest
):
    rows = vis.shape[0]
    columns = vis.shape[1]
    channels = u_cell.shape[0]
    owners, _, chunk = out.shape
    groups = owners * BLK_DEV
    feat[pl.ds(0, columns), :] = vis[...].astype(jnp.float32).T.astype(jnp.bfloat16)
    plane = w_plane[...] * OS
    codes = (u_cell[...], v_cell[...], plane + u_frac[...], plane + v_frac[...])
    codes = jnp.concatenate(codes, axis=0).astype(jnp.float32).astype(jnp.bfloat16)
    if regroup:
        count = 4 * channels
        width = channels // GROUP
        to = lax.broadcasted_iota(jnp.int32, (count, count), 0)
        quarter, rest = to // (4 * width), to % (4 * width)
        source = rest // width * channels + quarter * width + rest % width
        turn = source == lax.broadcasted_iota(jnp.int32, (count, count), 1)
        codes = jnp.dot(
            jnp.where(turn, 1.0, 0.0).astype(jnp.bfloat16), codes, preferred_element_type=jnp.float32
        ).astype(jnp.bfloat16)
    feat[pl.ds(columns, 4 * channels), :] = codes
    names = route[...]
    mine = lax.broadcasted_iota(jnp.int32, (groups, rows), 0) == names
    onehot = jnp.where(mine, 1.0, 0.0)
    earlier = lax.broadcasted_iota(jnp.int32, (rows, rows), 0) < lax.broadcasted_iota(
        jnp.int32, (rows, rows), 1
    )
    before = jnp.dot(
        onehot.astype(jnp.bfloat16),
        jnp.where(earlier, 1.0, 0.0).astype(jnp.bfloat16),
        preferred_element_type=jnp.float32,
    )
    rank = jnp.sum(onehot * before, axis=0, keepdims=True).astype(jnp.int32)
    dest[...] = names * slot_cap + rank

    table[...] = jnp.zeros_like(table)
    table[pl.ds(0, TAPS), :] = taps[...].astype(jnp.bfloat16).astype(jnp.float32)
    cells = lax.broadcasted_iota(jnp.int32, (SUB, SUB * POLC), 0)
    repeat = cells == lax.broadcasted_iota(jnp.int32, (SUB, SUB * POLC), 1) // POLC
    taper[...] = jnp.dot(
        gain[...],
        jnp.where(repeat, 1.0, 0.0),
        precision=lax.Precision.HIGHEST,
        preferred_element_type=jnp.float32,
    )

    def send(owner, _):
        slots = lax.broadcasted_iota(jnp.int32, (chunk, rows), 0) + owner * chunk
        pick = jnp.where(slots == dest[...], 1.0, 0.0).astype(jnp.bfloat16)
        out[owner] = lax.dot_general(
            feat[...], pick, NT, preferred_element_type=jnp.float32
        ).astype(jnp.bfloat16)
        return 0

    lax.fori_loop(0, owners, send, 0)


def spread(cell, taps):
    rows = lax.broadcasted_iota(jnp.int32, taps.shape, 0) - cell
    parts = []
    for start in range(0, SUB, ROWS):
        delta = rows + start
        weight = jnp.take_along_axis(taps, delta & (ROWS - 1), axis=0)
        parts.append(jnp.where((delta >= 0) & (delta < ROWS), weight, 0.0))
    return jnp.concatenate(parts, axis=0)


def grid_chunk(slot_cap, chunk, channels, lane, feat, table, total, left, right):
    covered = min(BLK_DEV, LANES // slot_cap)
    first = lane % chunk // slot_cap
    columns = channels * POLC
    lanes = lax.broadcasted_iota(jnp.int32, (SUB, LANES), 1)
    block = (lane + lanes) % chunk // slot_cap - first
    samples = feat[:columns, :].astype(jnp.float32)
    codes = feat[columns:, :].astype(jnp.float32).astype(jnp.int32)
    lookup = table[...]
    part = jnp.zeros((covered * SUB, SUB * POLC), jnp.float32)
    for h in range(channels):
        sample = samples[h * POLC : (h + 1) * POLC, :]
        cell_u = codes[h : h + 1, :]
        cell_v = codes[channels + h : channels + h + 1, :]
        row_u = codes[2 * channels + h : 2 * channels + h + 1, :]
        row_v = codes[3 * channels + h : 3 * channels + h + 1, :]
        taps_u = jnp.take_along_axis(lookup, jnp.broadcast_to(row_u, (8, LANES)), axis=1)
        taps_v = jnp.take_along_axis(lookup, jnp.broadcast_to(row_v, (8, LANES)), axis=1)
        weight_u = spread(cell_u, taps_u)
        weight_v = spread(cell_v, taps_v)
        here = pl.ds(h * LANES, LANES)
        weighted = weight_u[:, None, :] * sample[None, :, :]
        right[:, here] = weighted.reshape(SUB * POLC, LANES).astype(jnp.bfloat16)
        for b in range(covered):
            left[pl.ds(b * SUB, SUB), here] = jnp.where(block == b, weight_v, 0.0).astype(
                jnp.bfloat16
            )
        if (h + 1) % GROUP == 0:
            group = pl.ds((h + 1 - GROUP) * LANES, GROUP * LANES)
            part = part + lax.dot_general(
                left[:, group], right[:, group], NT, preferred_element_type=jnp.float32
            )
    place = pl.ds(pl.multiple_of(first * SUB, SUB), covered * SUB)
    total[place, :] = total[place, :] + part


def grid_kernel(slot_cap, chunk, channels, feat, table, taper, out, total, left, right):
    step = pl.program_id(0)

    @pl.when(step == 0)
    def _():
        total[...] = jnp.zeros_like(total)

    grid_chunk(
        slot_cap, chunk, channels, step * LANES, feat[0], table, total, left, right
    )

    @pl.when(step == pl.num_programs(0) - 1)
    def _():
        for b in range(BLK_DEV):
            out[b] = (total[pl.ds(b * SUB, SUB), :] * taper[...]).astype(jnp.bfloat16)


def swap(first, second, width):
    low = lax.broadcasted_iota(jnp.int32, first.shape, 1) // width % 2 == 0
    return (
        jnp.where(low, first, pltpu.roll(second, width, 1)),
        jnp.where(low, pltpu.roll(first, LANES - width, 1), second),
    )


def regroup_lanes(parts):
    quarter = LANES // GROUP
    first, second = swap(parts[0], parts[1], quarter)
    third, fourth = swap(parts[2], parts[3], quarter)
    first, third = swap(first, third, 2 * quarter)
    second, fourth = swap(second, fourth, 2 * quarter)
    return first, second, third, fourth


def weights(cell, taps):
    delta = lax.broadcasted_iota(jnp.int32, taps.shape, 0) - cell
    turned = jnp.take_along_axis(taps, delta & (ROWS - 1), axis=0)
    octave = delta >> 3
    return [jnp.where(octave == -g, turned, 0.0) for g in range(SUB // ROWS)]


def grid_part(channels, features, table, left, right, spare):
    width = channels // GROUP
    columns = channels * POLC
    span = width * POLC
    samples = regroup_lanes([features[q * span : (q + 1) * span] for q in range(GROUP)])
    start = [columns + q * 4 * width for q in range(GROUP)]
    codes = regroup_lanes([features[at : at + 4 * width] for at in start])
    lookup = table[...]
    parts = []
    for b in range(GROUP):
        code = codes[b].astype(jnp.int32)
        for g in range(width):
            sample = samples[b][g * POLC : (g + 1) * POLC, :]
            cell_u, cell_v, row_u, row_v = [
                code[kind * width + g : kind * width + g + 1, :] for kind in range(4)
            ]
            taps_u = jnp.take_along_axis(lookup, jnp.broadcast_to(row_u, (8, LANES)), axis=1)
            taps_v = jnp.take_along_axis(lookup, jnp.broadcast_to(row_v, (8, LANES)), axis=1)
            here = pl.ds(g * LANES, LANES)
            for place, weight in enumerate(weights(cell_u, taps_u)):
                spare[g, pl.ds(place * ROWS, ROWS), :] = weight
            for u in range(0, SUB, 2):
                pair = [spare[g, pl.ds(u + i, POLC, stride=0), :] * sample for i in range(2)]
                right[b, pl.ds(u * POLC, 2 * POLC), here] = jnp.concatenate(pair, axis=0).astype(
                    jnp.bfloat16
                )
            left[b, :, here] = jnp.concatenate(weights(cell_v, taps_v), axis=0).astype(jnp.bfloat16)
        parts.append(
            lax.dot_general(left[b], right[b], NT, preferred_element_type=jnp.float32)
        )
    return parts


def move_grid_kernel(
    channels, send, table, taper, out, moved, total, left, right, spare, own_sem, to_sem, at_sem
):
    count, features, chunk = send.shape
    v, t = lax.axis_index("vis"), lax.axis_index("tile")
    barrier = pltpu.get_barrier_semaphore()
    for k in range(1, count):
        pl.semaphore_signal(barrier, inc=1, device_id=((v + k) % count, t), device_id_type=MESH)
    pl.semaphore_wait(barrier, count - 1)

    def copy(k):
        return pltpu.make_async_remote_copy(
            src_ref=send.at[(v + k) % count],
            dst_ref=moved.at[v],
            send_sem=to_sem.at[k],
            recv_sem=at_sem.at[k],
            device_id=((v + k) % count, t),
            device_id_type=MESH,
        )

    own = pltpu.make_async_copy(send.at[v], moved.at[v], own_sem.at[0])
    own.start()
    for k in range(1, count):
        copy(k).start()
    total[...] = jnp.zeros_like(total)
    own.wait()

    def source(k, _):
        @pl.when(k > 0)
        def _():
            copy(k).wait_recv()

        origin = (v + count - k) % count

        for piece in range(chunk // LANES):
            features = moved[origin, :, pl.ds(piece * LANES, LANES)].astype(jnp.float32)
            parts = grid_part(channels, features, table, left, right, spare)
            for b, part in enumerate(parts):
                here = pl.ds((piece * GROUP + b) * SUB, SUB)
                total[here, :] = total[here, :] + part
        return 0

    lax.fori_loop(0, count, source, 0)
    for b in range(BLK_DEV):
        out[b] = (total[pl.ds(b * SUB, SUB), :] * taper[...]).astype(jnp.bfloat16)
    for k in range(1, count):
        copy(k).wait_send()


def slot_kernel(tiles, anchors, subs, out, meta):
    slots = out.shape[0]
    out[...] = jnp.zeros_like(out)
    lanes = lax.broadcasted_iota(jnp.int32, meta.shape, 1)
    places = jnp.full(meta.shape, -FAR, jnp.int32)
    for b in range(BLK_DEV):
        slot = tiles[0, b] * SCAP
        for before in range(b):
            slot = slot + jnp.where(tiles[0, before] == tiles[0, b], 1, 0)
        out[slot] = subs[b]
        places = jnp.where(lanes == slot, anchors[0, b], places)
        places = jnp.where(lanes == slots + slot, anchors[1, b], places)
    meta[...] = places


def gather_kernel(subs, meta, out, meta_out, own_sem, near_send, near_recv, far_send, far_recv):
    count = out.shape[0]
    width = out.shape[1]
    v, t = lax.axis_index("vis"), lax.axis_index("tile")
    half = count // 2
    spot = v // 2 * (1 - v % 2) + (count - 1 - v // 2) * (v % 2)

    def member(position):
        position = (position + 2 * count) % count
        back = position // half
        return (1 - back) * 2 * position + back * (2 * (count - 1 - position) + 1)

    barrier = pltpu.get_barrier_semaphore()
    for side in (1, -1):
        pl.semaphore_signal(
            barrier, inc=1, device_id=(member(spot + side), t), device_id_type=MESH
        )
    for k in range(1, width):
        pl.semaphore_signal(barrier, inc=1, device_id=(v, (t + k) % width), device_id_type=MESH)
    pl.semaphore_wait(barrier, 1 + width)

    def near(k):
        chunk = pl.ds((t + k) % width, 1)
        pairs = ((subs.at[chunk], out.at[v, pl.ds(t, 1)]), (meta, meta_out.at[v, t]))
        return [
            pltpu.make_async_remote_copy(
                src_ref=src,
                dst_ref=dst,
                send_sem=near_send.at[2 * k + i],
                recv_sem=near_recv.at[2 * k + i],
                device_id=(v, (t + k) % width),
                device_id_type=MESH,
            )
            for i, (src, dst) in enumerate(pairs)
        ]

    def own():
        pairs = ((subs.at[pl.ds(t, 1)], out.at[v, pl.ds(t, 1)]), (meta, meta_out.at[v, t]))
        return [
            pltpu.make_async_copy(src, dst, own_sem.at[i]) for i, (src, dst) in enumerate(pairs)
        ]

    def far(k, step):
        source = (t + width - k) % width
        cut = out.shape[2] // 2
        copies = []
        for i in range(3):
            side = 1 - 2 * (i % 2)
            origin = member(spot - side * step)
            if i < 2:
                ref = out.at[origin, source, pl.ds(i * cut, cut)]
            else:
                ref = meta_out.at[origin, source]
            copies.append(
                pltpu.make_async_remote_copy(
                    src_ref=ref,
                    dst_ref=ref,
                    send_sem=far_send.at[(step * width + k) * 3 + i],
                    recv_sem=far_recv.at[(step * width + k) * 3 + i],
                    device_id=(member(spot + side), t),
                    device_id_type=MESH,
                )
            )
        return copies

    for copy in own():
        copy.start()
    for k in range(1, width):
        for copy in near(k):
            copy.start()
    for copy in own():
        copy.wait()
    for k in range(width):
        if k:
            for copy in near(k):
                copy.wait_recv()
        for copy in far(k, 0):
            copy.start()

    def forward(step, _):
        for k in range(width):
            for landed, copy in zip(far(k, step - 1), far(k, step)):
                landed.wait_recv()
                copy.start()
        return 0

    lax.fori_loop(1, count - 1, forward, 0)
    for k in range(width):
        for copy in far(k, count - 2):
            copy.wait_recv()
    for k in range(1, width):
        for copy in near(k):
            copy.wait_send()

    def sent(step, _):
        for k in range(width):
            for copy in far(k, step):
                copy.wait_send()
        return 0

    lax.fori_loop(0, count - 1, sent, 0)


def place_kernel(tile_slots, meta, subs, out, canvas):
    v, t = lax.axis_index("vis"), lax.axis_index("tile")
    step = pl.program_id(0)
    slots = subs.shape[1]
    height = out.shape[1]
    width = out.shape[2]
    span = SUB * POLC

    @pl.when(step == 0)
    def _():
        canvas[...] = jnp.zeros_like(canvas)

    def add_source(near, _):
        source = step * (slots // tile_slots) + near
        for slot in range(tile_slots):
            lane = t * tile_slots + slot
            low = meta[source, lane] - v * height + SUB
            column = meta[source, slots + lane] * POLC

            @pl.when((low > 0) & (low < height + SUB))
            def _():
                sub = subs[0, near * tile_slots + slot].astype(jnp.float32)
                sub = jnp.concatenate([sub, jnp.zeros((SUB, LANES), jnp.float32)], axis=1)
                sub = pltpu.roll(sub, column % LANES, 1)
                sub = jnp.concatenate([sub, jnp.zeros((ROWS, span + LANES), jnp.float32)], axis=0)
                sub = pltpu.roll(sub, low % ROWS, 0)
                top = pl.multiple_of(low // ROWS * ROWS, ROWS)
                base = pl.multiple_of(column // LANES * LANES, LANES)
                here = (slot // SCAP, pl.ds(top, SUB + ROWS), pl.ds(base, span + LANES))
                canvas[here] = canvas[here] + sub

        return 0

    lax.fori_loop(0, slots // tile_slots, add_source, 0)

    @pl.when(step == pl.num_programs(0) - 1)
    def _():
        out[...] = canvas[:, pl.ds(SUB, height), pl.ds(0, width)]


def on_device(
    vis_data,
    u_cell,
    v_cell,
    u_frac,
    v_frac,
    w_plane,
    block_route,
    kernel_taps,
    taper_gain,
    sub_tile,
    sub_anchor,
):
    vis_count = lax.axis_size("vis")
    tile_width = lax.axis_size("tile")
    gt_dev = GT // tile_width
    rows, columns = vis_data.shape
    channels = u_cell.shape[0]
    slot_cap = max(2, 2 * rows // (BLK_DEV * vis_count))
    chunk = BLK_DEV * slot_cap
    grouped = slot_cap * GROUP == LANES and channels % GROUP == 0
    features = columns + 4 * channels
    per_owner = gt_dev * SCAP
    slots = tile_width * per_owner
    height = TS // vis_count
    width = TS * POLC

    send, table, taper = pl.pallas_call(
        functools.partial(dispatch_kernel, slot_cap, grouped),
        out_shape=[
            jax.ShapeDtypeStruct((vis_count, features, chunk), jnp.bfloat16),
            jax.ShapeDtypeStruct((ROWS, LANES), jnp.float32),
            jax.ShapeDtypeStruct((SUB, SUB * POLC), jnp.float32),
        ],
        scratch_shapes=[
            pltpu.VMEM((features, rows), jnp.bfloat16),
            pltpu.VMEM((1, rows), jnp.int32),
        ],
        name="dispatch",
    )(
        vis_data,
        u_cell,
        v_cell,
        u_frac,
        v_frac,
        w_plane,
        block_route.reshape(1, rows),
        kernel_taps.T,
        taper_gain,
    )
    covered = min(BLK_DEV, LANES // slot_cap)
    vmem = pl.BlockSpec(memory_space=pltpu.VMEM)
    work = [
        pltpu.VMEM((BLK_DEV * SUB, SUB * POLC), jnp.float32),
        pltpu.VMEM((covered * SUB, channels * LANES), jnp.bfloat16),
        pltpu.VMEM((SUB * POLC, channels * LANES), jnp.bfloat16),
    ]
    gridded = jax.ShapeDtypeStruct((BLK_DEV, SUB, SUB * POLC), jnp.bfloat16)
    if grouped:
        subs = pl.pallas_call(
            functools.partial(move_grid_kernel, channels),
            in_specs=[vmem, vmem, vmem],
            out_specs=vmem,
            out_shape=gridded,
            scratch_shapes=[pltpu.VMEM(send.shape, jnp.bfloat16)]
            + [
                work[0],
                pltpu.VMEM((GROUP, SUB, channels // GROUP * LANES), jnp.bfloat16),
                pltpu.VMEM((GROUP, SUB * POLC, channels // GROUP * LANES), jnp.bfloat16),
                pltpu.VMEM((channels // GROUP, SUB, LANES), jnp.float32),
                pltpu.SemaphoreType.DMA((1,)),
                pltpu.SemaphoreType.DMA((vis_count,)),
                pltpu.SemaphoreType.DMA((vis_count,)),
            ],
            compiler_params=pltpu.CompilerParams(collective_id=1, has_side_effects=True),
            name="move_grid",
        )(send, table, taper)
    else:
        moved = lax.all_to_all(send, "vis", split_axis=0, concat_axis=0, tiled=True)
        moved = jnp.transpose(moved, (1, 0, 2)).reshape(1, features, vis_count * chunk)
        subs = pl.pallas_call(
            functools.partial(grid_kernel, slot_cap, chunk, channels),
            grid=(moved.shape[2] // LANES,),
            in_specs=[
                pl.BlockSpec((1, features, LANES), lambda s: (0, 0, s)),
                pl.BlockSpec(table.shape, lambda s: (0, 0)),
                pl.BlockSpec(taper.shape, lambda s: (0, 0)),
            ],
            out_specs=pl.BlockSpec(gridded.shape, lambda s: (0, 0, 0)),
            out_shape=gridded,
            scratch_shapes=work,
            name="grid",
        )(moved, table, taper)
    scalars = pl.BlockSpec(memory_space=pltpu.SMEM)
    subs, meta = pl.pallas_call(
        slot_kernel,
        in_specs=[scalars, scalars, vmem],
        out_specs=[vmem, vmem],
        out_shape=[
            jax.ShapeDtypeStruct((slots, SUB, SUB * POLC), jnp.bfloat16),
            jax.ShapeDtypeStruct((1, LANES), jnp.int32),
        ],
        name="slot",
    )(sub_tile.reshape(1, BLK_DEV), sub_anchor.T, subs)
    hops = (vis_count - 1) * tile_width * 3
    subs, meta = pl.pallas_call(
        gather_kernel,
        in_specs=[vmem, vmem],
        out_specs=[vmem, vmem],
        out_shape=[
            jax.ShapeDtypeStruct(
                (vis_count, tile_width, per_owner, SUB, SUB * POLC), jnp.bfloat16
            ),
            jax.ShapeDtypeStruct((vis_count, tile_width, 1, LANES), jnp.int32),
        ],
        scratch_shapes=[
            pltpu.SemaphoreType.DMA((2,)),
            pltpu.SemaphoreType.DMA((2 * tile_width,)),
            pltpu.SemaphoreType.DMA((2 * tile_width,)),
            pltpu.SemaphoreType.DMA((hops,)),
            pltpu.SemaphoreType.DMA((hops,)),
        ],
        compiler_params=pltpu.CompilerParams(collective_id=0, has_side_effects=True),
        name="gather",
    )(subs.reshape(tile_width, per_owner, SUB, SUB * POLC), meta)
    subs = subs.reshape(vis_count, slots, SUB, SUB * POLC)
    meta = meta.reshape(vis_count * tile_width, LANES)
    return pl.pallas_call(
        functools.partial(place_kernel, per_owner),
        grid_spec=pltpu.PrefetchScalarGridSpec(
            num_scalar_prefetch=1,
            grid=(vis_count,),
            in_specs=[pl.BlockSpec((1, slots, SUB, SUB * POLC), lambda s, *_: (s, 0, 0, 0))],
            out_specs=pl.BlockSpec((gt_dev, height, width), lambda s, *_: (0, 0, 0)),
            scratch_shapes=[
                pltpu.VMEM((gt_dev, -(-height // ROWS) * ROWS + 2 * SUB + ROWS, width + LANES), jnp.float32),
            ],
        ),
        out_shape=jax.ShapeDtypeStruct((gt_dev, height, width), jnp.float32),
        name="place",
    )(meta, subs)


def solution(mesh):
    placed = (
        P(("vis", "tile"), None),
        P(None, ("vis", "tile")),
        P(None, ("vis", "tile")),
        P(None, ("vis", "tile")),
        P(None, ("vis", "tile")),
        P(None, ("vis", "tile")),
        P(("vis", "tile"), None),
        P(),
        P(),
        P(("vis", "tile"), None),
        P(("vis", "tile"), None),
    )
    return jax.shard_map(
        on_device, mesh=mesh, in_specs=placed, out_specs=P("tile", "vis", None), check_vma=False
    )
```

```python
import functools

import jax
import jax.numpy as jnp
from jax import lax
from jax.experimental import pallas as pl
from jax.experimental.pallas import tpu as pltpu
from jax.sharding import PartitionSpec as P

BLK_DEV = 8
SUB = 32
POLC = 8
TAPS = 7
OS = 16
TS = 256
GT = 8
SCAP = 2
LANES = 128
ROWS = 8
GROUP = 4
PIECES = 2
VMEM_BYTES = 40 << 20
FAR = 1 << 20
MESH = pl.DeviceIdType.MESH
NT = (((1,), (1,)), ((), ()))


def dispatch_kernel(
    slot_cap, vis, u_cell, v_cell, u_frac, v_frac, w_plane, route, taps, gain, out, table, taper, feat, dest
):
    rows = vis.shape[0]
    columns = vis.shape[1]
    channels = u_cell.shape[0]
    owners, _, chunk = out.shape
    groups = owners * BLK_DEV
    feat[pl.ds(0, columns), :] = vis[...].astype(jnp.float32).T.astype(jnp.bfloat16)
    plane = w_plane[...] * OS
    codes = (u_cell[...], v_cell[...], plane + u_frac[...], plane + v_frac[...])
    codes = jnp.concatenate(codes, axis=0).astype(jnp.float32).astype(jnp.bfloat16)
    feat[pl.ds(columns, 4 * channels), :] = codes
    names = route[...]
    mine = lax.broadcasted_iota(jnp.int32, (groups, rows), 0) == names
    onehot = jnp.where(mine, 1.0, 0.0)
    earlier = lax.broadcasted_iota(jnp.int32, (rows, rows), 0) < lax.broadcasted_iota(
        jnp.int32, (rows, rows), 1
    )
    before = jnp.dot(
        onehot.astype(jnp.bfloat16),
        jnp.where(earlier, 1.0, 0.0).astype(jnp.bfloat16),
        preferred_element_type=jnp.float32,
    )
    rank = jnp.sum(onehot * before, axis=0, keepdims=True).astype(jnp.int32)
    dest[...] = names * slot_cap + rank

    table[...] = jnp.zeros_like(table)
    table[pl.ds(0, TAPS), :] = taps[...].astype(jnp.bfloat16).astype(jnp.float32)
    cells = lax.broadcasted_iota(jnp.int32, (SUB, SUB * POLC), 0)
    repeat = cells == lax.broadcasted_iota(jnp.int32, (SUB, SUB * POLC), 1) // POLC
    taper[...] = jnp.dot(
        gain[...],
        jnp.where(repeat, 1.0, 0.0),
        precision=lax.Precision.HIGHEST,
        preferred_element_type=jnp.float32,
    )

    def send(owner, _):
        slots = lax.broadcasted_iota(jnp.int32, (chunk, rows), 0) + owner * chunk
        pick = jnp.where(slots == dest[...], 1.0, 0.0).astype(jnp.bfloat16)
        out[owner] = lax.dot_general(
            feat[...], pick, NT, preferred_element_type=jnp.float32
        ).astype(jnp.bfloat16)
        return 0

    lax.fori_loop(0, owners, send, 0)


def spread(cell, taps):
    rows = lax.broadcasted_iota(jnp.int32, taps.shape, 0) - cell
    parts = []
    for start in range(0, SUB, ROWS):
        delta = rows + start
        weight = jnp.take_along_axis(taps, delta & (ROWS - 1), axis=0)
        parts.append(jnp.where((delta >= 0) & (delta < ROWS), weight, 0.0))
    return jnp.concatenate(parts, axis=0)


def grid_chunk(slot_cap, chunk, channels, lane, feat, table, total, left, right):
    covered = min(BLK_DEV, LANES // slot_cap)
    first = lane % chunk // slot_cap
    columns = channels * POLC
    lanes = lax.broadcasted_iota(jnp.int32, (SUB, LANES), 1)
    block = (lane + lanes) % chunk // slot_cap - first
    samples = feat[:columns, :].astype(jnp.float32)
    codes = feat[columns:, :].astype(jnp.float32).astype(jnp.int32)
    lookup = table[...]
    part = jnp.zeros((covered * SUB, SUB * POLC), jnp.float32)
    for h in range(channels):
        sample = samples[h * POLC : (h + 1) * POLC, :]
        cell_u = codes[h : h + 1, :]
        cell_v = codes[channels + h : channels + h + 1, :]
        row_u = codes[2 * channels + h : 2 * channels + h + 1, :]
        row_v = codes[3 * channels + h : 3 * channels + h + 1, :]
        taps_u = jnp.take_along_axis(lookup, jnp.broadcast_to(row_u, (8, LANES)), axis=1)
        taps_v = jnp.take_along_axis(lookup, jnp.broadcast_to(row_v, (8, LANES)), axis=1)
        weight_u = spread(cell_u, taps_u)
        weight_v = spread(cell_v, taps_v)
        here = pl.ds(h * LANES, LANES)
        weighted = weight_u[:, None, :] * sample[None, :, :]
        right[:, here] = weighted.reshape(SUB * POLC, LANES).astype(jnp.bfloat16)
        for b in range(covered):
            left[pl.ds(b * SUB, SUB), here] = jnp.where(block == b, weight_v, 0.0).astype(
                jnp.bfloat16
            )
        if (h + 1) % GROUP == 0:
            group = pl.ds((h + 1 - GROUP) * LANES, GROUP * LANES)
            part = part + lax.dot_general(
                left[:, group], right[:, group], NT, preferred_element_type=jnp.float32
            )
    place = pl.ds(pl.multiple_of(first * SUB, SUB), covered * SUB)
    total[place, :] = total[place, :] + part


def grid_kernel(slot_cap, chunk, channels, feat, table, taper, out, total, left, right):
    step = pl.program_id(0)

    @pl.when(step == 0)
    def _():
        total[...] = jnp.zeros_like(total)

    grid_chunk(
        slot_cap, chunk, channels, step * LANES, feat[0], table, total, left, right
    )

    @pl.when(step == pl.num_programs(0) - 1)
    def _():
        for b in range(BLK_DEV):
            out[b] = (total[pl.ds(b * SUB, SUB), :] * taper[...]).astype(jnp.bfloat16)


def swap(first, second, width):
    low = lax.broadcasted_iota(jnp.int32, first.shape, 1) // width % 2 == 0
    return (
        jnp.where(low, first, pltpu.roll(second, width, 1)),
        jnp.where(low, pltpu.roll(first, LANES - width, 1), second),
    )


def regroup_lanes(parts):
    quarter = LANES // GROUP
    first, second = swap(parts[0], parts[1], quarter)
    third, fourth = swap(parts[2], parts[3], quarter)
    first, third = swap(first, third, 2 * quarter)
    second, fourth = swap(second, fourth, 2 * quarter)
    return first, second, third, fourth


def weights(cell, taps):
    delta = lax.broadcasted_iota(jnp.int32, taps.shape, 0) - cell
    turned = jnp.take_along_axis(taps, delta & (ROWS - 1), axis=0)
    octave = delta >> 3
    return [jnp.where(octave == -g, turned, 0.0) for g in range(SUB // ROWS)]


def grid_part(channels, features, table, left, right, spare):
    width = channels // GROUP
    columns = channels * POLC
    span = width * POLC
    samples = regroup_lanes([features[q * span : (q + 1) * span] for q in range(GROUP)])
    start = [columns + q * 4 * width for q in range(GROUP)]
    codes = regroup_lanes([features[at : at + 4 * width] for at in start])
    lookup = table[...]
    parts = []
    for b in range(GROUP):
        code = codes[b].astype(jnp.int32)
        for g in range(width):
            sample = samples[b][g * POLC : (g + 1) * POLC, :]
            cell_u, cell_v, row_u, row_v = [
                code[kind * width + g : kind * width + g + 1, :] for kind in range(4)
            ]
            taps_u = jnp.take_along_axis(lookup, jnp.broadcast_to(row_u, (8, LANES)), axis=1)
            taps_v = jnp.take_along_axis(lookup, jnp.broadcast_to(row_v, (8, LANES)), axis=1)
            here = pl.ds(g * LANES, LANES)
            for place, weight in enumerate(weights(cell_u, taps_u)):
                spare[g, pl.ds(place * ROWS, ROWS), :] = weight
            for u in range(0, SUB, 2):
                pair = [spare[g, pl.ds(u + i, POLC, stride=0), :] * sample for i in range(2)]
                right[b, pl.ds(u * POLC, 2 * POLC), here] = jnp.concatenate(pair, axis=0).astype(
                    jnp.bfloat16
                )
            left[b, :, here] = jnp.concatenate(weights(cell_v, taps_v), axis=0).astype(jnp.bfloat16)
        parts.append(
            lax.dot_general(left[b], right[b], NT, preferred_element_type=jnp.float32)
        )
    return parts


def ring(count):
    v = lax.axis_index("vis")
    half = count // 2
    spot = v // 2 * (1 - v % 2) + (count - 1 - v // 2) * (v % 2)

    def member(position):
        position = (position + 2 * count) % count
        back = position // half
        return (1 - back) * 2 * position + back * (2 * (count - 1 - position) + 1)

    return spot, member


def prepare(slot_cap, groups, vis, codes, route, feat, dest):
    rows, columns = vis.shape
    feat[pl.ds(0, columns), :] = vis[...].astype(jnp.float32).T.astype(jnp.bfloat16)
    u_cell, v_cell, u_frac, v_frac, w_plane = codes
    channels = u_cell.shape[0]
    plane = w_plane[...] * OS
    codes = (u_cell[...], v_cell[...], plane + u_frac[...], plane + v_frac[...])
    codes = jnp.concatenate(codes, axis=0).astype(jnp.float32).astype(jnp.bfloat16)
    count = 4 * channels
    width = channels // GROUP
    to = lax.broadcasted_iota(jnp.int32, (count, count), 0)
    quarter, rest = to // (4 * width), to % (4 * width)
    source = rest // width * channels + quarter * width + rest % width
    turn = source == lax.broadcasted_iota(jnp.int32, (count, count), 1)
    feat[pl.ds(columns, count), :] = jnp.dot(
        jnp.where(turn, 1.0, 0.0).astype(jnp.bfloat16), codes, preferred_element_type=jnp.float32
    ).astype(jnp.bfloat16)
    earlier = lax.broadcasted_iota(jnp.int32, (LANES, LANES), 0) < lax.broadcasted_iota(
        jnp.int32, (LANES, LANES), 1
    )
    earlier = jnp.where(earlier, 1.0, 0.0).astype(jnp.bfloat16)
    seen = jnp.zeros((groups, 1), jnp.float32)
    for start in range(0, rows, LANES):
        names = route[:, pl.ds(start, LANES)]
        mine = lax.broadcasted_iota(jnp.int32, (groups, LANES), 0) == names
        onehot = jnp.where(mine, 1.0, 0.0)
        before = seen + jnp.dot(
            onehot.astype(jnp.bfloat16), earlier, preferred_element_type=jnp.float32
        )
        rank = jnp.sum(onehot * before, axis=0, keepdims=True).astype(jnp.int32)
        dest[:, pl.ds(start, LANES)] = names * slot_cap + rank
        seen = seen + jnp.sum(onehot, axis=1, keepdims=True)


def reduce_kernel(
    slot_cap,
    vis,
    u_cell,
    v_cell,
    u_frac,
    v_frac,
    w_plane,
    route,
    taps,
    gain,
    tiles,
    anchors,
    out,
    meta_out,
    table,
    taper,
    feat,
    dest,
    left,
    right,
    spare,
    partial,
    sent,
    landed,
    meta,
    meta_send,
    meta_recv,
    sum_send,
    sum_recv,
    far_send,
    far_recv,
):
    count = out.shape[0]
    rows = vis.shape[0]
    channels = u_cell.shape[0]
    chunk = BLK_DEV * slot_cap
    v, t = lax.axis_index("vis"), lax.axis_index("tile")
    spot, member = ring(count)
    sides = (1, -1)
    each = GROUP // PIECES

    barrier = pltpu.get_barrier_semaphore()
    for k in range(1, count):
        pl.semaphore_signal(barrier, inc=1, device_id=((v + k) % count, t), device_id_type=MESH)

    meta[...] = jnp.zeros_like(meta)
    meta[pl.ds(0, 1), pl.ds(0, BLK_DEV)] = tiles[...]
    meta[pl.ds(1, 2), pl.ds(0, BLK_DEV)] = anchors[...]
    table[...] = jnp.zeros_like(table)
    table[pl.ds(0, TAPS), :] = taps[...].astype(jnp.bfloat16).astype(jnp.float32)
    cells = lax.broadcasted_iota(jnp.int32, (SUB, SUB * POLC), 0)
    repeat = cells == lax.broadcasted_iota(jnp.int32, (SUB, SUB * POLC), 1) // POLC
    taper[...] = jnp.dot(
        gain[...],
        jnp.where(repeat, 1.0, 0.0),
        precision=lax.Precision.HIGHEST,
        preferred_element_type=jnp.float32,
    )
    prepare(
        slot_cap,
        count * BLK_DEV,
        vis,
        (u_cell, v_cell, u_frac, v_frac, w_plane),
        route,
        feat,
        dest,
    )
    pl.semaphore_wait(barrier, count - 1)

    def tell(k):
        return pltpu.make_async_remote_copy(
            src_ref=meta,
            dst_ref=meta_out.at[v],
            send_sem=meta_send.at[k],
            recv_sem=meta_recv.at[k],
            device_id=((v + k) % count, t),
            device_id_type=MESH,
        )

    for k in range(1, count):
        tell(k).start()
    meta_out[v] = meta[...]

    def add(step, d, i):
        here = (step, d, pl.ds(i * each, each))
        return pltpu.make_async_remote_copy(
            src_ref=sent.at[here],
            dst_ref=landed.at[here],
            send_sem=sum_send.at[(step * 2 + d) * PIECES + i],
            recv_sem=sum_recv.at[(step * 2 + d) * PIECES + i],
            device_id=(member(spot + sides[d]), t),
            device_id_type=MESH,
        )

    def far(step, d, i):
        ref = out.at[member(spot - sides[d] * step), pl.ds(d * GROUP + i * each, each)]
        return pltpu.make_async_remote_copy(
            src_ref=ref,
            dst_ref=ref,
            send_sem=far_send.at[(step * 2 + d) * PIECES + i],
            recv_sem=far_recv.at[(step * 2 + d) * PIECES + i],
            device_id=(member(spot + sides[d]), t),
            device_id_type=MESH,
        )

    pieces = [(d, i) for i in range(PIECES) for d in range(2)]

    def grid_step(step, _):
        slots = lax.broadcasted_iota(jnp.int32, (chunk, rows), 0)
        owner = jnp.where(slots < LANES, member(spot - 1 - step), member(spot + 1 + step))
        pick = jnp.where(slots + owner * chunk == dest[...], 1.0, 0.0).astype(jnp.bfloat16)
        features = lax.dot_general(feat[...], pick, NT, preferred_element_type=jnp.float32)
        for d in range(2):
            grids = grid_part(
                channels, features[:, d * LANES : (d + 1) * LANES], table, left, right, spare
            )
            for b, part in enumerate(grids):
                partial[d, b] = part
        for d, i in pieces:
            here = pl.ds(i * each, each)

            @pl.when(step > 0)
            def _():
                add(step - 1, d, i).wait_recv()
                partial[d, here] = partial[d, here] + landed[step - 1, d, here].astype(jnp.float32)

            @pl.when(step < count - 1)
            def _():
                sent[step, d, here] = partial[d, here].astype(jnp.bfloat16)
                add(step, d, i).start()

        return 0

    lax.fori_loop(0, count, grid_step, 0)
    for d, i in pieces:
        for b in range(i * each, (i + 1) * each):
            out[v, d * GROUP + b] = (partial[d, b] * taper[...]).astype(jnp.bfloat16)
        far(0, d, i).start()

    def forward(step, _):
        for d, i in pieces:
            far(step - 1, d, i).wait_recv()
            far(step, d, i).start()
        return 0

    lax.fori_loop(1, count - 1, forward, 0)
    for d, i in pieces:
        far(count - 2, d, i).wait_recv()
    for k in range(1, count):
        tell(k).wait_recv()

    def finish(step, _):
        for d, i in pieces:
            add(step, d, i).wait_send()
            far(step, d, i).wait_send()
        return 0

    lax.fori_loop(0, count - 1, finish, 0)
    for k in range(1, count):
        tell(k).wait_send()


def canvas_kernel(meta, subs, out, canvas):
    v = lax.axis_index("vis")
    tiles, height, width = out.shape
    span = SUB * POLC
    canvas[:, pl.ds(SUB, height), :] = jnp.zeros((tiles, height, width + LANES), jnp.float32)

    def add_source(source, _):
        for b in range(BLK_DEV):
            tile = meta[source * ROWS, b]
            low = meta[source * ROWS + 1, b] - v * height + SUB
            column = meta[source * ROWS + 2, b] * POLC

            @pl.when((low > 0) & (low < height + SUB))
            def _():
                sub = subs[source, b].astype(jnp.float32)
                sub = jnp.concatenate([sub, jnp.zeros((SUB, LANES), jnp.float32)], axis=1)
                sub = pltpu.roll(sub, column % LANES, 1)
                sub = jnp.concatenate([sub, jnp.zeros((ROWS, span + LANES), jnp.float32)], axis=0)
                sub = pltpu.roll(sub, low % ROWS, 0)
                top = pl.multiple_of(low // ROWS * ROWS, ROWS)
                base = pl.multiple_of(column // LANES * LANES, LANES)
                here = (tile, pl.ds(top, SUB + ROWS), pl.ds(base, span + LANES))
                canvas[here] = canvas[here] + sub

        return 0

    lax.fori_loop(0, subs.shape[0], add_source, 0)
    out[...] = canvas[:, pl.ds(SUB, height), pl.ds(0, width)].astype(jnp.bfloat16)


def fold_kernel(
    canvas, own, far_out, near, middle, near_send, near_recv, far_send, far_recv
):
    tiles, height, width = own.shape
    v, t = lax.axis_index("vis"), lax.axis_index("tile")
    beside = t + 1 - 2 * (t % 2)
    across = (t + 2) % 4
    corner = (beside + 2) % 4
    cut = height // 2
    barrier = pltpu.get_barrier_semaphore()
    for other in (beside, across):
        pl.semaphore_signal(barrier, inc=1, device_id=(v, other), device_id_type=MESH)
    pl.semaphore_wait(barrier, 2)
    pieces = [(g, i) for g in range(tiles) for i in range(2)]

    def to_beside(part, g, i):
        here = pl.ds(i * cut, cut)
        return pltpu.make_async_remote_copy(
            src_ref=canvas.at[(corner, beside)[part] * tiles + g, here],
            dst_ref=near.at[part, g, here],
            send_sem=near_send.at[(part * tiles + g) * 2 + i],
            recv_sem=near_recv.at[(part * tiles + g) * 2 + i],
            device_id=(v, beside),
            device_id_type=MESH,
        )

    def to_across(g, i):
        here = pl.ds(i * cut, cut)
        return pltpu.make_async_remote_copy(
            src_ref=middle.at[g, here],
            dst_ref=far_out.at[g, here],
            send_sem=far_send.at[g * 2 + i],
            recv_sem=far_recv.at[g * 2 + i],
            device_id=(v, across),
            device_id_type=MESH,
        )

    for part in range(2):
        for g, i in pieces:
            to_beside(part, g, i).start()
    for g, i in pieces:
        here = pl.ds(i * cut, cut)
        to_beside(0, g, i).wait_recv()
        middle[g, here] = (
            canvas[across * tiles + g, here].astype(jnp.float32)
            + near[0, g, here].astype(jnp.float32)
        ).astype(jnp.bfloat16)
        to_across(g, i).start()
    for g, i in pieces:
        here = pl.ds(i * cut, cut)
        to_beside(1, g, i).wait_recv()
        own[g, here] = canvas[t * tiles + g, here].astype(jnp.float32) + near[1, g, here].astype(
            jnp.float32
        )
    for g, i in pieces:
        to_across(g, i).wait_recv()
    for g, i in pieces:
        for part in range(2):
            to_beside(part, g, i).wait_send()
        to_across(g, i).wait_send()


def slot_kernel(tiles, anchors, subs, out, meta):
    slots = out.shape[0]
    out[...] = jnp.zeros_like(out)
    lanes = lax.broadcasted_iota(jnp.int32, meta.shape, 1)
    places = jnp.full(meta.shape, -FAR, jnp.int32)
    for b in range(BLK_DEV):
        slot = tiles[0, b] * SCAP
        for before in range(b):
            slot = slot + jnp.where(tiles[0, before] == tiles[0, b], 1, 0)
        out[slot] = subs[b]
        places = jnp.where(lanes == slot, anchors[0, b], places)
        places = jnp.where(lanes == slots + slot, anchors[1, b], places)
    meta[...] = places


def gather_kernel(subs, meta, out, meta_out, own_sem, near_send, near_recv, far_send, far_recv):
    count = out.shape[0]
    width = out.shape[1]
    v, t = lax.axis_index("vis"), lax.axis_index("tile")
    half = count // 2
    spot = v // 2 * (1 - v % 2) + (count - 1 - v // 2) * (v % 2)

    def member(position):
        position = (position + 2 * count) % count
        back = position // half
        return (1 - back) * 2 * position + back * (2 * (count - 1 - position) + 1)

    barrier = pltpu.get_barrier_semaphore()
    for side in (1, -1):
        pl.semaphore_signal(
            barrier, inc=1, device_id=(member(spot + side), t), device_id_type=MESH
        )
    for k in range(1, width):
        pl.semaphore_signal(barrier, inc=1, device_id=(v, (t + k) % width), device_id_type=MESH)
    pl.semaphore_wait(barrier, 1 + width)

    def near(k):
        chunk = pl.ds((t + k) % width, 1)
        pairs = ((subs.at[chunk], out.at[v, pl.ds(t, 1)]), (meta, meta_out.at[v, t]))
        return [
            pltpu.make_async_remote_copy(
                src_ref=src,
                dst_ref=dst,
                send_sem=near_send.at[2 * k + i],
                recv_sem=near_recv.at[2 * k + i],
                device_id=(v, (t + k) % width),
                device_id_type=MESH,
            )
            for i, (src, dst) in enumerate(pairs)
        ]

    def own():
        pairs = ((subs.at[pl.ds(t, 1)], out.at[v, pl.ds(t, 1)]), (meta, meta_out.at[v, t]))
        return [
            pltpu.make_async_copy(src, dst, own_sem.at[i]) for i, (src, dst) in enumerate(pairs)
        ]

    def far(k, step):
        source = (t + width - k) % width
        cut = out.shape[2] // 2
        copies = []
        for i in range(3):
            side = 1 - 2 * (i % 2)
            origin = member(spot - side * step)
            if i < 2:
                ref = out.at[origin, source, pl.ds(i * cut, cut)]
            else:
                ref = meta_out.at[origin, source]
            copies.append(
                pltpu.make_async_remote_copy(
                    src_ref=ref,
                    dst_ref=ref,
                    send_sem=far_send.at[(step * width + k) * 3 + i],
                    recv_sem=far_recv.at[(step * width + k) * 3 + i],
                    device_id=(member(spot + side), t),
                    device_id_type=MESH,
                )
            )
        return copies

    for copy in own():
        copy.start()
    for k in range(1, width):
        for copy in near(k):
            copy.start()
    for copy in own():
        copy.wait()
    for k in range(width):
        if k:
            for copy in near(k):
                copy.wait_recv()
        for copy in far(k, 0):
            copy.start()

    def forward(step, _):
        for k in range(width):
            for landed, copy in zip(far(k, step - 1), far(k, step)):
                landed.wait_recv()
                copy.start()
        return 0

    lax.fori_loop(1, count - 1, forward, 0)
    for k in range(width):
        for copy in far(k, count - 2):
            copy.wait_recv()
    for k in range(1, width):
        for copy in near(k):
            copy.wait_send()

    def sent(step, _):
        for k in range(width):
            for copy in far(k, step):
                copy.wait_send()
        return 0

    lax.fori_loop(0, count - 1, sent, 0)


def place_kernel(tile_slots, meta, subs, out, canvas):
    v, t = lax.axis_index("vis"), lax.axis_index("tile")
    step = pl.program_id(0)
    slots = subs.shape[1]
    height = out.shape[1]
    width = out.shape[2]
    span = SUB * POLC

    @pl.when(step == 0)
    def _():
        canvas[...] = jnp.zeros_like(canvas)

    def add_source(near, _):
        source = step * (slots // tile_slots) + near
        for slot in range(tile_slots):
            lane = t * tile_slots + slot
            low = meta[source, lane] - v * height + SUB
            column = meta[source, slots + lane] * POLC

            @pl.when((low > 0) & (low < height + SUB))
            def _():
                sub = subs[0, near * tile_slots + slot].astype(jnp.float32)
                sub = jnp.concatenate([sub, jnp.zeros((SUB, LANES), jnp.float32)], axis=1)
                sub = pltpu.roll(sub, column % LANES, 1)
                sub = jnp.concatenate([sub, jnp.zeros((ROWS, span + LANES), jnp.float32)], axis=0)
                sub = pltpu.roll(sub, low % ROWS, 0)
                top = pl.multiple_of(low // ROWS * ROWS, ROWS)
                base = pl.multiple_of(column // LANES * LANES, LANES)
                here = (slot // SCAP, pl.ds(top, SUB + ROWS), pl.ds(base, span + LANES))
                canvas[here] = canvas[here] + sub

        return 0

    lax.fori_loop(0, slots // tile_slots, add_source, 0)

    @pl.when(step == pl.num_programs(0) - 1)
    def _():
        out[...] = canvas[:, pl.ds(SUB, height), pl.ds(0, width)]


def on_device(
    vis_data,
    u_cell,
    v_cell,
    u_frac,
    v_frac,
    w_plane,
    block_route,
    kernel_taps,
    taper_gain,
    sub_tile,
    sub_anchor,
):
    vis_count = lax.axis_size("vis")
    tile_width = lax.axis_size("tile")
    gt_dev = GT // tile_width
    rows, columns = vis_data.shape
    channels = u_cell.shape[0]
    slot_cap = max(2, 2 * rows // (BLK_DEV * vis_count))
    chunk = BLK_DEV * slot_cap
    grouped = (
        slot_cap * GROUP == LANES
        and channels % GROUP == 0
        and vis_count % 2 == 0
        and tile_width == 4
        and TS // vis_count % 32 == 0
    )
    features = columns + 4 * channels
    per_owner = gt_dev * SCAP
    slots = tile_width * per_owner
    height = TS // vis_count
    width = TS * POLC

    vmem = pl.BlockSpec(memory_space=pltpu.VMEM)
    if grouped:
        stages = vis_count - 1
        lots = stages * 2 * PIECES
        block = (SUB, SUB * POLC)
        lanes = channels // GROUP * LANES
        subs, meta = pl.pallas_call(
            functools.partial(reduce_kernel, slot_cap),
            in_specs=[vmem] * 11,
            out_specs=[vmem] * 2,
            out_shape=[
                jax.ShapeDtypeStruct((vis_count, BLK_DEV) + block, jnp.bfloat16),
                jax.ShapeDtypeStruct((vis_count, ROWS, LANES), jnp.int32),
            ],
            scratch_shapes=[
                pltpu.VMEM((ROWS, LANES), jnp.float32),
                pltpu.VMEM(block, jnp.float32),
                pltpu.VMEM((features, rows), jnp.bfloat16),
                pltpu.VMEM((1, rows), jnp.int32),
                pltpu.VMEM((GROUP, SUB, lanes), jnp.bfloat16),
                pltpu.VMEM((GROUP, SUB * POLC, lanes), jnp.bfloat16),
                pltpu.VMEM((channels // GROUP, SUB, LANES), jnp.float32),
                pltpu.VMEM((2, GROUP) + block, jnp.float32),
                pltpu.VMEM((stages, 2, GROUP) + block, jnp.bfloat16),
                pltpu.VMEM((stages, 2, GROUP) + block, jnp.bfloat16),
                pltpu.VMEM((ROWS, LANES), jnp.int32),
                pltpu.SemaphoreType.DMA((vis_count,)),
                pltpu.SemaphoreType.DMA((vis_count,)),
            ]
            + [pltpu.SemaphoreType.DMA((lots,))] * 4,
            compiler_params=pltpu.CompilerParams(
                collective_id=1, has_side_effects=True, vmem_limit_bytes=VMEM_BYTES
            ),
            name="reduce",
        )(
            vis_data,
            u_cell,
            v_cell,
            u_frac,
            v_frac,
            w_plane,
            block_route.reshape(1, rows),
            kernel_taps.T,
            taper_gain,
            sub_tile.reshape(1, BLK_DEV),
            sub_anchor.T,
        )
        canvas = pl.pallas_call(
            canvas_kernel,
            grid_spec=pltpu.PrefetchScalarGridSpec(
                num_scalar_prefetch=1,
                grid=(1,),
                in_specs=[vmem],
                out_specs=vmem,
                scratch_shapes=[
                    pltpu.VMEM((GT, height + 2 * SUB + ROWS, width + LANES), jnp.float32),
                ],
            ),
            out_shape=jax.ShapeDtypeStruct((GT, height, width), jnp.bfloat16),
            compiler_params=pltpu.CompilerParams(vmem_limit_bytes=VMEM_BYTES),
            name="canvas",
        )(meta.reshape(vis_count * ROWS, LANES), subs)
        portion = (gt_dev, height, width)
        own, other = pl.pallas_call(
            fold_kernel,
            in_specs=[vmem],
            out_specs=[vmem] * 2,
            out_shape=[
                jax.ShapeDtypeStruct(portion, jnp.float32),
                jax.ShapeDtypeStruct(portion, jnp.bfloat16),
            ],
            scratch_shapes=[
                pltpu.VMEM((2,) + portion, jnp.bfloat16),
                pltpu.VMEM(portion, jnp.bfloat16),
                pltpu.SemaphoreType.DMA((4 * gt_dev,)),
                pltpu.SemaphoreType.DMA((4 * gt_dev,)),
                pltpu.SemaphoreType.DMA((2 * gt_dev,)),
                pltpu.SemaphoreType.DMA((2 * gt_dev,)),
            ],
            compiler_params=pltpu.CompilerParams(
                collective_id=0, has_side_effects=True, vmem_limit_bytes=VMEM_BYTES
            ),
            name="fold",
        )(canvas)
        return own + other.astype(jnp.float32)

    send, table, taper = pl.pallas_call(
        functools.partial(dispatch_kernel, slot_cap),
        out_shape=[
            jax.ShapeDtypeStruct((vis_count, features, chunk), jnp.bfloat16),
            jax.ShapeDtypeStruct((ROWS, LANES), jnp.float32),
            jax.ShapeDtypeStruct((SUB, SUB * POLC), jnp.float32),
        ],
        scratch_shapes=[
            pltpu.VMEM((features, rows), jnp.bfloat16),
            pltpu.VMEM((1, rows), jnp.int32),
        ],
        name="dispatch",
    )(
        vis_data,
        u_cell,
        v_cell,
        u_frac,
        v_frac,
        w_plane,
        block_route.reshape(1, rows),
        kernel_taps.T,
        taper_gain,
    )
    covered = min(BLK_DEV, LANES // slot_cap)
    work = [
        pltpu.VMEM((BLK_DEV * SUB, SUB * POLC), jnp.float32),
        pltpu.VMEM((covered * SUB, channels * LANES), jnp.bfloat16),
        pltpu.VMEM((SUB * POLC, channels * LANES), jnp.bfloat16),
    ]
    gridded = jax.ShapeDtypeStruct((BLK_DEV, SUB, SUB * POLC), jnp.bfloat16)
    moved = lax.all_to_all(send, "vis", split_axis=0, concat_axis=0, tiled=True)
    moved = jnp.transpose(moved, (1, 0, 2)).reshape(1, features, vis_count * chunk)
    subs = pl.pallas_call(
        functools.partial(grid_kernel, slot_cap, chunk, channels),
        grid=(moved.shape[2] // LANES,),
        in_specs=[
            pl.BlockSpec((1, features, LANES), lambda s: (0, 0, s)),
            pl.BlockSpec(table.shape, lambda s: (0, 0)),
            pl.BlockSpec(taper.shape, lambda s: (0, 0)),
        ],
        out_specs=pl.BlockSpec(gridded.shape, lambda s: (0, 0, 0)),
        out_shape=gridded,
        scratch_shapes=work,
        name="grid",
    )(moved, table, taper)
    scalars = pl.BlockSpec(memory_space=pltpu.SMEM)
    subs, meta = pl.pallas_call(
        slot_kernel,
        in_specs=[scalars, scalars, vmem],
        out_specs=[vmem, vmem],
        out_shape=[
            jax.ShapeDtypeStruct((slots, SUB, SUB * POLC), jnp.bfloat16),
            jax.ShapeDtypeStruct((1, LANES), jnp.int32),
        ],
        name="slot",
    )(sub_tile.reshape(1, BLK_DEV), sub_anchor.T, subs)
    hops = (vis_count - 1) * tile_width * 3
    subs, meta = pl.pallas_call(
        gather_kernel,
        in_specs=[vmem, vmem],
        out_specs=[vmem, vmem],
        out_shape=[
            jax.ShapeDtypeStruct(
                (vis_count, tile_width, per_owner, SUB, SUB * POLC), jnp.bfloat16
            ),
            jax.ShapeDtypeStruct((vis_count, tile_width, 1, LANES), jnp.int32),
        ],
        scratch_shapes=[
            pltpu.SemaphoreType.DMA((2,)),
            pltpu.SemaphoreType.DMA((2 * tile_width,)),
            pltpu.SemaphoreType.DMA((2 * tile_width,)),
            pltpu.SemaphoreType.DMA((hops,)),
            pltpu.SemaphoreType.DMA((hops,)),
        ],
        compiler_params=pltpu.CompilerParams(collective_id=0, has_side_effects=True),
        name="gather",
    )(subs.reshape(tile_width, per_owner, SUB, SUB * POLC), meta)
    subs = subs.reshape(vis_count, slots, SUB, SUB * POLC)
    meta = meta.reshape(vis_count * tile_width, LANES)
    return pl.pallas_call(
        functools.partial(place_kernel, per_owner),
        grid_spec=pltpu.PrefetchScalarGridSpec(
            num_scalar_prefetch=1,
            grid=(vis_count,),
            in_specs=[pl.BlockSpec((1, slots, SUB, SUB * POLC), lambda s, *_: (s, 0, 0, 0))],
            out_specs=pl.BlockSpec((gt_dev, height, width), lambda s, *_: (0, 0, 0)),
            scratch_shapes=[
                pltpu.VMEM((gt_dev, -(-height // ROWS) * ROWS + 2 * SUB + ROWS, width + LANES), jnp.float32),
            ],
        ),
        out_shape=jax.ShapeDtypeStruct((gt_dev, height, width), jnp.float32),
        name="place",
    )(meta, subs)


def solution(mesh):
    placed = (
        P(("vis", "tile"), None),
        P(None, ("vis", "tile")),
        P(None, ("vis", "tile")),
        P(None, ("vis", "tile")),
        P(None, ("vis", "tile")),
        P(None, ("vis", "tile")),
        P(("vis", "tile"), None),
        P(),
        P(),
        P(("vis", "tile"), None),
        P(("vis", "tile"), None),
    )
    return jax.shard_map(
        on_device, mesh=mesh, in_specs=placed, out_specs=P("tile", "vis", None), check_vma=False
    )
```

```python
import functools

import jax
import jax.numpy as jnp
from jax import lax
from jax.experimental import pallas as pl
from jax.experimental.pallas import tpu as pltpu
from jax.sharding import PartitionSpec as P

BLK_DEV = 8
SUB = 32
POLC = 8
TAPS = 7
OS = 16
TS = 256
GT = 8
SCAP = 2
LANES = 128
ROWS = 8
GROUP = 4
PIECES = 4
VMEM_BYTES = 24 << 20
FAR = 1 << 20
MESH = pl.DeviceIdType.MESH
NT = (((1,), (1,)), ((), ()))


def dispatch_kernel(
    slot_cap, vis, u_cell, v_cell, u_frac, v_frac, w_plane, route, taps, gain, out, table, taper, feat, dest
):
    rows = vis.shape[0]
    columns = vis.shape[1]
    channels = u_cell.shape[0]
    owners, _, chunk = out.shape
    groups = owners * BLK_DEV
    feat[pl.ds(0, columns), :] = vis[...].astype(jnp.float32).T.astype(jnp.bfloat16)
    plane = w_plane[...] * OS
    codes = (u_cell[...], v_cell[...], plane + u_frac[...], plane + v_frac[...])
    codes = jnp.concatenate(codes, axis=0).astype(jnp.float32).astype(jnp.bfloat16)
    feat[pl.ds(columns, 4 * channels), :] = codes
    names = route[...]
    mine = lax.broadcasted_iota(jnp.int32, (groups, rows), 0) == names
    onehot = jnp.where(mine, 1.0, 0.0)
    earlier = lax.broadcasted_iota(jnp.int32, (rows, rows), 0) < lax.broadcasted_iota(
        jnp.int32, (rows, rows), 1
    )
    before = jnp.dot(
        onehot.astype(jnp.bfloat16),
        jnp.where(earlier, 1.0, 0.0).astype(jnp.bfloat16),
        preferred_element_type=jnp.float32,
    )
    rank = jnp.sum(onehot * before, axis=0, keepdims=True).astype(jnp.int32)
    dest[...] = names * slot_cap + rank

    table[...] = jnp.zeros_like(table)
    table[pl.ds(0, TAPS), :] = taps[...].astype(jnp.bfloat16).astype(jnp.float32)
    cells = lax.broadcasted_iota(jnp.int32, (SUB, SUB * POLC), 0)
    repeat = cells == lax.broadcasted_iota(jnp.int32, (SUB, SUB * POLC), 1) // POLC
    taper[...] = jnp.dot(
        gain[...],
        jnp.where(repeat, 1.0, 0.0),
        precision=lax.Precision.HIGHEST,
        preferred_element_type=jnp.float32,
    )

    def send(owner, _):
        slots = lax.broadcasted_iota(jnp.int32, (chunk, rows), 0) + owner * chunk
        pick = jnp.where(slots == dest[...], 1.0, 0.0).astype(jnp.bfloat16)
        out[owner] = lax.dot_general(
            feat[...], pick, NT, preferred_element_type=jnp.float32
        ).astype(jnp.bfloat16)
        return 0

    lax.fori_loop(0, owners, send, 0)


def spread(cell, taps):
    rows = lax.broadcasted_iota(jnp.int32, taps.shape, 0) - cell
    parts = []
    for start in range(0, SUB, ROWS):
        delta = rows + start
        weight = jnp.take_along_axis(taps, delta & (ROWS - 1), axis=0)
        parts.append(jnp.where((delta >= 0) & (delta < ROWS), weight, 0.0))
    return jnp.concatenate(parts, axis=0)


def grid_chunk(slot_cap, chunk, channels, lane, feat, table, total, left, right):
    covered = min(BLK_DEV, LANES // slot_cap)
    first = lane % chunk // slot_cap
    columns = channels * POLC
    lanes = lax.broadcasted_iota(jnp.int32, (SUB, LANES), 1)
    block = (lane + lanes) % chunk // slot_cap - first
    samples = feat[:columns, :].astype(jnp.float32)
    codes = feat[columns:, :].astype(jnp.float32).astype(jnp.int32)
    lookup = table[...]
    part = jnp.zeros((covered * SUB, SUB * POLC), jnp.float32)
    for h in range(channels):
        sample = samples[h * POLC : (h + 1) * POLC, :]
        cell_u = codes[h : h + 1, :]
        cell_v = codes[channels + h : channels + h + 1, :]
        row_u = codes[2 * channels + h : 2 * channels + h + 1, :]
        row_v = codes[3 * channels + h : 3 * channels + h + 1, :]
        taps_u = jnp.take_along_axis(lookup, jnp.broadcast_to(row_u, (8, LANES)), axis=1)
        taps_v = jnp.take_along_axis(lookup, jnp.broadcast_to(row_v, (8, LANES)), axis=1)
        weight_u = spread(cell_u, taps_u)
        weight_v = spread(cell_v, taps_v)
        here = pl.ds(h * LANES, LANES)
        weighted = weight_u[:, None, :] * sample[None, :, :]
        right[:, here] = weighted.reshape(SUB * POLC, LANES).astype(jnp.bfloat16)
        for b in range(covered):
            left[pl.ds(b * SUB, SUB), here] = jnp.where(block == b, weight_v, 0.0).astype(
                jnp.bfloat16
            )
        if (h + 1) % GROUP == 0:
            group = pl.ds((h + 1 - GROUP) * LANES, GROUP * LANES)
            part = part + lax.dot_general(
                left[:, group], right[:, group], NT, preferred_element_type=jnp.float32
            )
    place = pl.ds(pl.multiple_of(first * SUB, SUB), covered * SUB)
    total[place, :] = total[place, :] + part


def grid_kernel(slot_cap, chunk, channels, feat, table, taper, out, total, left, right):
    step = pl.program_id(0)

    @pl.when(step == 0)
    def _():
        total[...] = jnp.zeros_like(total)

    grid_chunk(
        slot_cap, chunk, channels, step * LANES, feat[0], table, total, left, right
    )

    @pl.when(step == pl.num_programs(0) - 1)
    def _():
        for b in range(BLK_DEV):
            out[b] = (total[pl.ds(b * SUB, SUB), :] * taper[...]).astype(jnp.bfloat16)


def swap(first, second, width):
    low = lax.broadcasted_iota(jnp.int32, first.shape, 1) // width % 2 == 0
    return (
        jnp.where(low, first, pltpu.roll(second, width, 1)),
        jnp.where(low, pltpu.roll(first, LANES - width, 1), second),
    )


def regroup_lanes(parts):
    quarter = LANES // GROUP
    first, second = swap(parts[0], parts[1], quarter)
    third, fourth = swap(parts[2], parts[3], quarter)
    first, third = swap(first, third, 2 * quarter)
    second, fourth = swap(second, fourth, 2 * quarter)
    return first, second, third, fourth


def weights(cell, taps):
    delta = lax.broadcasted_iota(jnp.int32, taps.shape, 0) - cell
    turned = jnp.take_along_axis(taps, delta & (ROWS - 1), axis=0)
    octave = delta >> 3
    return [jnp.where(octave == -g, turned, 0.0) for g in range(SUB // ROWS)]


def grid_part(channels, features, table, left, right, spare):
    width = channels // GROUP
    columns = channels * POLC
    span = width * POLC
    samples = regroup_lanes([features[q * span : (q + 1) * span] for q in range(GROUP)])
    start = [columns + q * 4 * width for q in range(GROUP)]
    codes = regroup_lanes([features[at : at + 4 * width] for at in start])
    lookup = table[...]
    parts = []
    for b in range(GROUP):
        code = codes[b].astype(jnp.int32)
        for g in range(width):
            sample = samples[b][g * POLC : (g + 1) * POLC, :]
            cell_u, cell_v, row_u, row_v = [
                code[kind * width + g : kind * width + g + 1, :] for kind in range(4)
            ]
            taps_u = jnp.take_along_axis(lookup, jnp.broadcast_to(row_u, (8, LANES)), axis=1)
            taps_v = jnp.take_along_axis(lookup, jnp.broadcast_to(row_v, (8, LANES)), axis=1)
            here = pl.ds(g * LANES, LANES)
            for place, weight in enumerate(weights(cell_u, taps_u)):
                spare[g, pl.ds(place * ROWS, ROWS), :] = weight
            for u in range(0, SUB, 2):
                pair = [spare[g, pl.ds(u + i, POLC, stride=0), :] * sample for i in range(2)]
                right[b, pl.ds(u * POLC, 2 * POLC), here] = jnp.concatenate(pair, axis=0).astype(
                    jnp.bfloat16
                )
            left[b, :, here] = jnp.concatenate(weights(cell_v, taps_v), axis=0).astype(jnp.bfloat16)
        parts.append(
            lax.dot_general(left[b], right[b], NT, preferred_element_type=jnp.float32)
        )
    return parts


def prepare(slot_cap, groups, vis, codes, route, feat, dest):
    rows, columns = vis.shape
    feat[pl.ds(0, columns), :] = vis[...].astype(jnp.float32).T.astype(jnp.bfloat16)
    u_cell, v_cell, u_frac, v_frac, w_plane = codes
    channels = u_cell.shape[0]
    plane = w_plane[...] * OS
    codes = (u_cell[...], v_cell[...], plane + u_frac[...], plane + v_frac[...])
    codes = jnp.concatenate(codes, axis=0).astype(jnp.float32).astype(jnp.bfloat16)
    count = 4 * channels
    width = channels // GROUP
    to = lax.broadcasted_iota(jnp.int32, (count, count), 0)
    quarter, rest = to // (4 * width), to % (4 * width)
    source = rest // width * channels + quarter * width + rest % width
    turn = source == lax.broadcasted_iota(jnp.int32, (count, count), 1)
    feat[pl.ds(columns, count), :] = jnp.dot(
        jnp.where(turn, 1.0, 0.0).astype(jnp.bfloat16), codes, preferred_element_type=jnp.float32
    ).astype(jnp.bfloat16)
    earlier = lax.broadcasted_iota(jnp.int32, (LANES, LANES), 0) < lax.broadcasted_iota(
        jnp.int32, (LANES, LANES), 1
    )
    earlier = jnp.where(earlier, 1.0, 0.0).astype(jnp.bfloat16)
    seen = jnp.zeros((groups, 1), jnp.float32)
    for start in range(0, rows, LANES):
        names = route[:, pl.ds(start, LANES)]
        mine = lax.broadcasted_iota(jnp.int32, (groups, LANES), 0) == names
        onehot = jnp.where(mine, 1.0, 0.0)
        before = seen + jnp.dot(
            onehot.astype(jnp.bfloat16), earlier, preferred_element_type=jnp.float32
        )
        rank = jnp.sum(onehot * before, axis=0, keepdims=True).astype(jnp.int32)
        dest[:, pl.ds(start, LANES)] = names * slot_cap + rank
        seen = seen + jnp.sum(onehot, axis=1, keepdims=True)


def reduce_kernel(
    slot_cap,
    vis_hbm,
    u_cell_hbm,
    v_cell_hbm,
    u_frac_hbm,
    v_frac_hbm,
    w_plane_hbm,
    route_hbm,
    taps_hbm,
    gain_hbm,
    tiles_hbm,
    anchors_hbm,
    out,
    meta_out,
    vis,
    u_cell,
    v_cell,
    u_frac,
    v_frac,
    w_plane,
    route,
    taps,
    gain,
    tiles,
    anchors,
    table,
    taper,
    feat,
    dest,
    left,
    right,
    spare,
    partial,
    x_sent,
    x_landed,
    z_sent,
    z_landed,
    meta,
    in_sem,
    meta_send,
    meta_recv,
    x_send,
    x_recv,
    z_send,
    z_recv,
    to_z_send,
    to_z_recv,
    to_x_send,
    to_x_recv,
):
    count = out.shape[0]
    height = count // 2
    rows = vis.shape[0]
    channels = u_cell.shape[0]
    chunk = BLK_DEV * slot_cap
    v, t = lax.axis_index("vis"), lax.axis_index("tile")
    z, x = v // 2, v % 2
    each = BLK_DEV // PIECES
    remote = functools.partial(pltpu.make_async_remote_copy, device_id_type=MESH)

    barrier = pltpu.get_barrier_semaphore()
    for k in range(1, count):
        pl.semaphore_signal(barrier, inc=1, device_id=((v + k) % count, t), device_id_type=MESH)
    pairs = (
        (vis_hbm, vis),
        (u_cell_hbm, u_cell),
        (v_cell_hbm, v_cell),
        (u_frac_hbm, u_frac),
        (v_frac_hbm, v_frac),
        (w_plane_hbm, w_plane),
        (route_hbm, route),
        (taps_hbm, taps),
        (gain_hbm, gain),
        (tiles_hbm, tiles),
        (anchors_hbm, anchors),
    )
    loads = [pltpu.make_async_copy(src, dst, in_sem.at[i]) for i, (src, dst) in enumerate(pairs)]
    for load in loads:
        load.start()
    meta[...] = jnp.zeros_like(meta)
    table[...] = jnp.zeros_like(table)
    for load in loads:
        load.wait()

    meta[pl.ds(0, 1), pl.ds(0, BLK_DEV)] = tiles[...]
    meta[pl.ds(1, 2), pl.ds(0, BLK_DEV)] = anchors[...]
    table[pl.ds(0, TAPS), :] = taps[...].astype(jnp.bfloat16).astype(jnp.float32)
    cells = lax.broadcasted_iota(jnp.int32, (SUB, SUB * POLC), 0)
    repeat = cells == lax.broadcasted_iota(jnp.int32, (SUB, SUB * POLC), 1) // POLC
    taper[...] = jnp.dot(
        gain[...],
        jnp.where(repeat, 1.0, 0.0),
        precision=lax.Precision.HIGHEST,
        preferred_element_type=jnp.float32,
    )
    prepare(
        slot_cap,
        count * BLK_DEV,
        vis,
        (u_cell, v_cell, u_frac, v_frac, w_plane),
        route,
        feat,
        dest,
    )
    pl.semaphore_wait(barrier, count - 1)

    def piece(i):
        return pl.ds(i * each, each)

    def tell(k):
        return remote(
            src_ref=meta,
            dst_ref=meta_out.at[v],
            send_sem=meta_send.at[k],
            recv_sem=meta_recv.at[k],
            device_id=((v + k) % count, t),
        )

    def add_x(j, i):
        return remote(
            src_ref=x_sent.at[j, piece(i)],
            dst_ref=x_landed.at[j, piece(i)],
            send_sem=x_send.at[j * PIECES + i],
            recv_sem=x_recv.at[j * PIECES + i],
            device_id=(z * 2 + 1 - x, t),
        )

    def add_z(j, i):
        return remote(
            src_ref=z_sent.at[j - 1, piece(i)],
            dst_ref=z_landed.at[j - 1, piece(i)],
            send_sem=z_send.at[(j - 1) * PIECES + i],
            recv_sem=z_recv.at[(j - 1) * PIECES + i],
            device_id=((z + j) % height * 2 + x, t),
        )

    def give_z(j, i):
        return remote(
            src_ref=out.at[v, piece(i)],
            dst_ref=out.at[v, piece(i)],
            send_sem=to_z_send.at[(j - 1) * PIECES + i],
            recv_sem=to_z_recv.at[(j - 1) * PIECES + i],
            device_id=((z + j) % height * 2 + x, t),
        )

    def give_x(j, i):
        ref = out.at[(z + height - j) % height * 2 + x, piece(i)]
        return remote(
            src_ref=ref,
            dst_ref=ref,
            send_sem=to_x_send.at[j * PIECES + i],
            recv_sem=to_x_recv.at[j * PIECES + i],
            device_id=(z * 2 + 1 - x, t),
        )

    for k in range(1, count):
        tell(k).start()
    meta_out[v] = meta[...]

    def grid_step(step, _):
        last = step == count - 1
        mine = jnp.logical_or(jnp.logical_and(step > 0, step % 2 == 0), last)
        j = jnp.where(last, 0, jnp.where(mine, step // 2, (step + 3) // 2 % height))
        owner = (z + j) % height * 2 + jnp.where(mine, x, 1 - x)
        slots = lax.broadcasted_iota(jnp.int32, (chunk, rows), 0) + owner * chunk
        pick = jnp.where(slots == dest[...], 1.0, 0.0).astype(jnp.bfloat16)
        features = lax.dot_general(feat[...], pick, NT, preferred_element_type=jnp.float32)
        for d in range(chunk // LANES):
            grids = grid_part(
                channels, features[:, d * LANES : (d + 1) * LANES], table, left, right, spare
            )
            for b, part in enumerate(grids):
                partial[d * GROUP + b] = part

        @pl.when(jnp.logical_not(mine))
        def _():
            for i in range(PIECES):
                x_sent[j, piece(i)] = partial[piece(i)].astype(jnp.bfloat16)
                add_x(j, i).start()

        @pl.when(mine)
        def _():
            for i in range(PIECES):
                add_x(j, i).wait_recv()
                partial[piece(i)] = partial[piece(i)] + x_landed[j, piece(i)].astype(jnp.float32)

                @pl.when(j > 0)
                def _():
                    z_sent[j - 1, piece(i)] = partial[piece(i)].astype(jnp.bfloat16)
                    add_z(j, i).start()

        return 0

    lax.fori_loop(0, count, grid_step, 0)
    for i in range(PIECES):
        whole = partial[piece(i)]
        for j in range(1, height):
            add_z(j, i).wait_recv()
            whole = whole + z_landed[j - 1, piece(i)].astype(jnp.float32)
        out[v, piece(i)] = (whole * taper[...][None]).astype(jnp.bfloat16)
        for j in range(1, height):
            give_z(j, i).start()
        give_x(0, i).start()
    for i in range(PIECES):
        for j in range(1, height):
            give_z(j, i).wait_recv()
            give_x(j, i).start()
    for i in range(PIECES):
        for j in range(height):
            give_x(j, i).wait_recv()
    for k in range(1, count):
        tell(k).wait_recv()
    for k in range(1, count):
        tell(k).wait_send()
    for i in range(PIECES):
        for j in range(height):
            add_x(j, i).wait_send()
            give_x(j, i).wait_send()
        for j in range(1, height):
            add_z(j, i).wait_send()
            give_z(j, i).wait_send()


def canvas_kernel(meta, subs, out, canvas):
    v = lax.axis_index("vis")
    tiles, height, width = out.shape
    span = SUB * POLC
    canvas[:, pl.ds(SUB, height), :] = jnp.zeros((tiles, height, width + LANES), jnp.float32)

    def add_source(source, _):
        for b in range(BLK_DEV):
            tile = meta[source * ROWS, b]
            low = meta[source * ROWS + 1, b] - v * height + SUB
            column = meta[source * ROWS + 2, b] * POLC

            @pl.when((low > 0) & (low < height + SUB))
            def _():
                sub = subs[source, b].astype(jnp.float32)
                sub = jnp.concatenate([sub, jnp.zeros((SUB, LANES), jnp.float32)], axis=1)
                sub = pltpu.roll(sub, column % LANES, 1)
                sub = jnp.concatenate([sub, jnp.zeros((ROWS, span + LANES), jnp.float32)], axis=0)
                sub = pltpu.roll(sub, low % ROWS, 0)
                top = pl.multiple_of(low // ROWS * ROWS, ROWS)
                base = pl.multiple_of(column // LANES * LANES, LANES)
                here = (tile, pl.ds(top, SUB + ROWS), pl.ds(base, span + LANES))
                canvas[here] = canvas[here] + sub

        return 0

    lax.fori_loop(0, subs.shape[0], add_source, 0)
    out[...] = canvas[:, pl.ds(SUB, height), pl.ds(0, width)].astype(jnp.bfloat16)


def fold_kernel(
    canvas, own, far_out, near, middle, near_send, near_recv, far_send, far_recv
):
    tiles, height, width = own.shape
    v, t = lax.axis_index("vis"), lax.axis_index("tile")
    beside = t + 1 - 2 * (t % 2)
    across = (t + 2) % 4
    corner = (beside + 2) % 4
    cut = height // 2
    barrier = pltpu.get_barrier_semaphore()
    for other in (beside, across):
        pl.semaphore_signal(barrier, inc=1, device_id=(v, other), device_id_type=MESH)
    pl.semaphore_wait(barrier, 2)
    pieces = [(g, i) for g in range(tiles) for i in range(2)]

    def to_beside(part, g, i):
        here = pl.ds(i * cut, cut)
        return pltpu.make_async_remote_copy(
            src_ref=canvas.at[(corner, beside)[part] * tiles + g, here],
            dst_ref=near.at[part, g, here],
            send_sem=near_send.at[(part * tiles + g) * 2 + i],
            recv_sem=near_recv.at[(part * tiles + g) * 2 + i],
            device_id=(v, beside),
            device_id_type=MESH,
        )

    def to_across(g, i):
        here = pl.ds(i * cut, cut)
        return pltpu.make_async_remote_copy(
            src_ref=middle.at[g, here],
            dst_ref=far_out.at[g, here],
            send_sem=far_send.at[g * 2 + i],
            recv_sem=far_recv.at[g * 2 + i],
            device_id=(v, across),
            device_id_type=MESH,
        )

    for part in range(2):
        for g, i in pieces:
            to_beside(part, g, i).start()
    for g, i in pieces:
        here = pl.ds(i * cut, cut)
        to_beside(0, g, i).wait_recv()
        middle[g, here] = (
            canvas[across * tiles + g, here].astype(jnp.float32)
            + near[0, g, here].astype(jnp.float32)
        ).astype(jnp.bfloat16)
        to_across(g, i).start()
    for g, i in pieces:
        here = pl.ds(i * cut, cut)
        to_beside(1, g, i).wait_recv()
        own[g, here] = canvas[t * tiles + g, here].astype(jnp.float32) + near[1, g, here].astype(
            jnp.float32
        )
    for g, i in pieces:
        to_across(g, i).wait_recv()
    for g, i in pieces:
        for part in range(2):
            to_beside(part, g, i).wait_send()
        to_across(g, i).wait_send()


def slot_kernel(tiles, anchors, subs, out, meta):
    slots = out.shape[0]
    out[...] = jnp.zeros_like(out)
    lanes = lax.broadcasted_iota(jnp.int32, meta.shape, 1)
    places = jnp.full(meta.shape, -FAR, jnp.int32)
    for b in range(BLK_DEV):
        slot = tiles[0, b] * SCAP
        for before in range(b):
            slot = slot + jnp.where(tiles[0, before] == tiles[0, b], 1, 0)
        out[slot] = subs[b]
        places = jnp.where(lanes == slot, anchors[0, b], places)
        places = jnp.where(lanes == slots + slot, anchors[1, b], places)
    meta[...] = places


def gather_kernel(subs, meta, out, meta_out, own_sem, near_send, near_recv, far_send, far_recv):
    count = out.shape[0]
    width = out.shape[1]
    v, t = lax.axis_index("vis"), lax.axis_index("tile")
    half = count // 2
    spot = v // 2 * (1 - v % 2) + (count - 1 - v // 2) * (v % 2)

    def member(position):
        position = (position + 2 * count) % count
        back = position // half
        return (1 - back) * 2 * position + back * (2 * (count - 1 - position) + 1)

    barrier = pltpu.get_barrier_semaphore()
    for side in (1, -1):
        pl.semaphore_signal(
            barrier, inc=1, device_id=(member(spot + side), t), device_id_type=MESH
        )
    for k in range(1, width):
        pl.semaphore_signal(barrier, inc=1, device_id=(v, (t + k) % width), device_id_type=MESH)
    pl.semaphore_wait(barrier, 1 + width)

    def near(k):
        chunk = pl.ds((t + k) % width, 1)
        pairs = ((subs.at[chunk], out.at[v, pl.ds(t, 1)]), (meta, meta_out.at[v, t]))
        return [
            pltpu.make_async_remote_copy(
                src_ref=src,
                dst_ref=dst,
                send_sem=near_send.at[2 * k + i],
                recv_sem=near_recv.at[2 * k + i],
                device_id=(v, (t + k) % width),
                device_id_type=MESH,
            )
            for i, (src, dst) in enumerate(pairs)
        ]

    def own():
        pairs = ((subs.at[pl.ds(t, 1)], out.at[v, pl.ds(t, 1)]), (meta, meta_out.at[v, t]))
        return [
            pltpu.make_async_copy(src, dst, own_sem.at[i]) for i, (src, dst) in enumerate(pairs)
        ]

    def far(k, step):
        source = (t + width - k) % width
        cut = out.shape[2] // 2
        copies = []
        for i in range(3):
            side = 1 - 2 * (i % 2)
            origin = member(spot - side * step)
            if i < 2:
                ref = out.at[origin, source, pl.ds(i * cut, cut)]
            else:
                ref = meta_out.at[origin, source]
            copies.append(
                pltpu.make_async_remote_copy(
                    src_ref=ref,
                    dst_ref=ref,
                    send_sem=far_send.at[(step * width + k) * 3 + i],
                    recv_sem=far_recv.at[(step * width + k) * 3 + i],
                    device_id=(member(spot + side), t),
                    device_id_type=MESH,
                )
            )
        return copies

    for copy in own():
        copy.start()
    for k in range(1, width):
        for copy in near(k):
            copy.start()
    for copy in own():
        copy.wait()
    for k in range(width):
        if k:
            for copy in near(k):
                copy.wait_recv()
        for copy in far(k, 0):
            copy.start()

    def forward(step, _):
        for k in range(width):
            for landed, copy in zip(far(k, step - 1), far(k, step)):
                landed.wait_recv()
                copy.start()
        return 0

    lax.fori_loop(1, count - 1, forward, 0)
    for k in range(width):
        for copy in far(k, count - 2):
            copy.wait_recv()
    for k in range(1, width):
        for copy in near(k):
            copy.wait_send()

    def sent(step, _):
        for k in range(width):
            for copy in far(k, step):
                copy.wait_send()
        return 0

    lax.fori_loop(0, count - 1, sent, 0)


def place_kernel(tile_slots, meta, subs, out, canvas):
    v, t = lax.axis_index("vis"), lax.axis_index("tile")
    step = pl.program_id(0)
    slots = subs.shape[1]
    height = out.shape[1]
    width = out.shape[2]
    span = SUB * POLC

    @pl.when(step == 0)
    def _():
        canvas[...] = jnp.zeros_like(canvas)

    def add_source(near, _):
        source = step * (slots // tile_slots) + near
        for slot in range(tile_slots):
            lane = t * tile_slots + slot
            low = meta[source, lane] - v * height + SUB
            column = meta[source, slots + lane] * POLC

            @pl.when((low > 0) & (low < height + SUB))
            def _():
                sub = subs[0, near * tile_slots + slot].astype(jnp.float32)
                sub = jnp.concatenate([sub, jnp.zeros((SUB, LANES), jnp.float32)], axis=1)
                sub = pltpu.roll(sub, column % LANES, 1)
                sub = jnp.concatenate([sub, jnp.zeros((ROWS, span + LANES), jnp.float32)], axis=0)
                sub = pltpu.roll(sub, low % ROWS, 0)
                top = pl.multiple_of(low // ROWS * ROWS, ROWS)
                base = pl.multiple_of(column // LANES * LANES, LANES)
                here = (slot // SCAP, pl.ds(top, SUB + ROWS), pl.ds(base, span + LANES))
                canvas[here] = canvas[here] + sub

        return 0

    lax.fori_loop(0, slots // tile_slots, add_source, 0)

    @pl.when(step == pl.num_programs(0) - 1)
    def _():
        out[...] = canvas[:, pl.ds(SUB, height), pl.ds(0, width)]


def on_device(
    vis_data,
    u_cell,
    v_cell,
    u_frac,
    v_frac,
    w_plane,
    block_route,
    kernel_taps,
    taper_gain,
    sub_tile,
    sub_anchor,
):
    vis_count = lax.axis_size("vis")
    tile_width = lax.axis_size("tile")
    gt_dev = GT // tile_width
    rows, columns = vis_data.shape
    channels = u_cell.shape[0]
    slot_cap = max(2, 2 * rows // (BLK_DEV * vis_count))
    chunk = BLK_DEV * slot_cap
    grouped = (
        slot_cap * GROUP == LANES
        and channels % GROUP == 0
        and vis_count % 2 == 0
        and vis_count > 2
        and tile_width == 4
        and TS // vis_count % 32 == 0
    )
    features = columns + 4 * channels
    per_owner = gt_dev * SCAP
    slots = tile_width * per_owner
    height = TS // vis_count
    width = TS * POLC

    vmem = pl.BlockSpec(memory_space=pltpu.VMEM)
    if grouped:
        layers = vis_count // 2
        block = (SUB, SUB * POLC)
        lanes = channels // GROUP * LANES
        operands = (
            vis_data,
            u_cell,
            v_cell,
            u_frac,
            v_frac,
            w_plane,
            block_route.reshape(1, rows),
            kernel_taps.T,
            taper_gain,
            sub_tile.reshape(1, BLK_DEV),
            sub_anchor.T,
        )
        subs, meta = pl.pallas_call(
            functools.partial(reduce_kernel, slot_cap),
            in_specs=[pl.BlockSpec(memory_space=pltpu.HBM)] * len(operands),
            out_specs=[vmem] * 2,
            out_shape=[
                jax.ShapeDtypeStruct((vis_count, BLK_DEV) + block, jnp.bfloat16),
                jax.ShapeDtypeStruct((vis_count, ROWS, LANES), jnp.int32),
            ],
            scratch_shapes=[pltpu.VMEM(operand.shape, operand.dtype) for operand in operands]
            + [
                pltpu.VMEM((ROWS, LANES), jnp.float32),
                pltpu.VMEM(block, jnp.float32),
                pltpu.VMEM((features, rows), jnp.bfloat16),
                pltpu.VMEM((1, rows), jnp.int32),
                pltpu.VMEM((GROUP, SUB, lanes), jnp.bfloat16),
                pltpu.VMEM((GROUP, SUB * POLC, lanes), jnp.bfloat16),
                pltpu.VMEM((channels // GROUP, SUB, LANES), jnp.float32),
                pltpu.VMEM((BLK_DEV,) + block, jnp.float32),
                pltpu.VMEM((layers, BLK_DEV) + block, jnp.bfloat16),
                pltpu.VMEM((layers, BLK_DEV) + block, jnp.bfloat16),
                pltpu.VMEM((layers - 1, BLK_DEV) + block, jnp.bfloat16),
                pltpu.VMEM((layers - 1, BLK_DEV) + block, jnp.bfloat16),
                pltpu.VMEM((ROWS, LANES), jnp.int32),
                pltpu.SemaphoreType.DMA((len(operands),)),
            ]
            + [
                pltpu.SemaphoreType.DMA((lots,))
                for lots in [vis_count] * 2
                + [layers * PIECES] * 2
                + [(layers - 1) * PIECES] * 4
                + [layers * PIECES] * 2
            ],
            compiler_params=pltpu.CompilerParams(
                collective_id=1, has_side_effects=True, vmem_limit_bytes=VMEM_BYTES
            ),
            name="reduce",
        )(*[pltpu.with_memory_space_constraint(operand, pltpu.HBM) for operand in operands])
        canvas = pl.pallas_call(
            canvas_kernel,
            grid_spec=pltpu.PrefetchScalarGridSpec(
                num_scalar_prefetch=1,
                grid=(1,),
                in_specs=[vmem],
                out_specs=vmem,
                scratch_shapes=[
                    pltpu.VMEM((GT, height + 2 * SUB + ROWS, width + LANES), jnp.float32),
                ],
            ),
            out_shape=jax.ShapeDtypeStruct((GT, height, width), jnp.bfloat16),
            compiler_params=pltpu.CompilerParams(vmem_limit_bytes=VMEM_BYTES),
            name="canvas",
        )(meta.reshape(vis_count * ROWS, LANES), subs)
        portion = (gt_dev, height, width)
        own, other = pl.pallas_call(
            fold_kernel,
            in_specs=[vmem],
            out_specs=[vmem] * 2,
            out_shape=[
                jax.ShapeDtypeStruct(portion, jnp.float32),
                jax.ShapeDtypeStruct(portion, jnp.bfloat16),
            ],
            scratch_shapes=[
                pltpu.VMEM((2,) + portion, jnp.bfloat16),
                pltpu.VMEM(portion, jnp.bfloat16),
                pltpu.SemaphoreType.DMA((4 * gt_dev,)),
                pltpu.SemaphoreType.DMA((4 * gt_dev,)),
                pltpu.SemaphoreType.DMA((2 * gt_dev,)),
                pltpu.SemaphoreType.DMA((2 * gt_dev,)),
            ],
            compiler_params=pltpu.CompilerParams(
                collective_id=0, has_side_effects=True, vmem_limit_bytes=VMEM_BYTES
            ),
            name="fold",
        )(canvas)
        return own + other.astype(jnp.float32)

    send, table, taper = pl.pallas_call(
        functools.partial(dispatch_kernel, slot_cap),
        out_shape=[
            jax.ShapeDtypeStruct((vis_count, features, chunk), jnp.bfloat16),
            jax.ShapeDtypeStruct((ROWS, LANES), jnp.float32),
            jax.ShapeDtypeStruct((SUB, SUB * POLC), jnp.float32),
        ],
        scratch_shapes=[
            pltpu.VMEM((features, rows), jnp.bfloat16),
            pltpu.VMEM((1, rows), jnp.int32),
        ],
        name="dispatch",
    )(
        vis_data,
        u_cell,
        v_cell,
        u_frac,
        v_frac,
        w_plane,
        block_route.reshape(1, rows),
        kernel_taps.T,
        taper_gain,
    )
    covered = min(BLK_DEV, LANES // slot_cap)
    work = [
        pltpu.VMEM((BLK_DEV * SUB, SUB * POLC), jnp.float32),
        pltpu.VMEM((covered * SUB, channels * LANES), jnp.bfloat16),
        pltpu.VMEM((SUB * POLC, channels * LANES), jnp.bfloat16),
    ]
    gridded = jax.ShapeDtypeStruct((BLK_DEV, SUB, SUB * POLC), jnp.bfloat16)
    moved = lax.all_to_all(send, "vis", split_axis=0, concat_axis=0, tiled=True)
    moved = jnp.transpose(moved, (1, 0, 2)).reshape(1, features, vis_count * chunk)
    subs = pl.pallas_call(
        functools.partial(grid_kernel, slot_cap, chunk, channels),
        grid=(moved.shape[2] // LANES,),
        in_specs=[
            pl.BlockSpec((1, features, LANES), lambda s: (0, 0, s)),
            pl.BlockSpec(table.shape, lambda s: (0, 0)),
            pl.BlockSpec(taper.shape, lambda s: (0, 0)),
        ],
        out_specs=pl.BlockSpec(gridded.shape, lambda s: (0, 0, 0)),
        out_shape=gridded,
        scratch_shapes=work,
        name="grid",
    )(moved, table, taper)
    scalars = pl.BlockSpec(memory_space=pltpu.SMEM)
    subs, meta = pl.pallas_call(
        slot_kernel,
        in_specs=[scalars, scalars, vmem],
        out_specs=[vmem, vmem],
        out_shape=[
            jax.ShapeDtypeStruct((slots, SUB, SUB * POLC), jnp.bfloat16),
            jax.ShapeDtypeStruct((1, LANES), jnp.int32),
        ],
        name="slot",
    )(sub_tile.reshape(1, BLK_DEV), sub_anchor.T, subs)
    hops = (vis_count - 1) * tile_width * 3
    subs, meta = pl.pallas_call(
        gather_kernel,
        in_specs=[vmem, vmem],
        out_specs=[vmem, vmem],
        out_shape=[
            jax.ShapeDtypeStruct(
                (vis_count, tile_width, per_owner, SUB, SUB * POLC), jnp.bfloat16
            ),
            jax.ShapeDtypeStruct((vis_count, tile_width, 1, LANES), jnp.int32),
        ],
        scratch_shapes=[
            pltpu.SemaphoreType.DMA((2,)),
            pltpu.SemaphoreType.DMA((2 * tile_width,)),
            pltpu.SemaphoreType.DMA((2 * tile_width,)),
            pltpu.SemaphoreType.DMA((hops,)),
            pltpu.SemaphoreType.DMA((hops,)),
        ],
        compiler_params=pltpu.CompilerParams(collective_id=0, has_side_effects=True),
        name="gather",
    )(subs.reshape(tile_width, per_owner, SUB, SUB * POLC), meta)
    subs = subs.reshape(vis_count, slots, SUB, SUB * POLC)
    meta = meta.reshape(vis_count * tile_width, LANES)
    return pl.pallas_call(
        functools.partial(place_kernel, per_owner),
        grid_spec=pltpu.PrefetchScalarGridSpec(
            num_scalar_prefetch=1,
            grid=(vis_count,),
            in_specs=[pl.BlockSpec((1, slots, SUB, SUB * POLC), lambda s, *_: (s, 0, 0, 0))],
            out_specs=pl.BlockSpec((gt_dev, height, width), lambda s, *_: (0, 0, 0)),
            scratch_shapes=[
                pltpu.VMEM((gt_dev, -(-height // ROWS) * ROWS + 2 * SUB + ROWS, width + LANES), jnp.float32),
            ],
        ),
        out_shape=jax.ShapeDtypeStruct((gt_dev, height, width), jnp.float32),
        name="place",
    )(meta, subs)


def solution(mesh):
    placed = (
        P(("vis", "tile"), None),
        P(None, ("vis", "tile")),
        P(None, ("vis", "tile")),
        P(None, ("vis", "tile")),
        P(None, ("vis", "tile")),
        P(None, ("vis", "tile")),
        P(("vis", "tile"), None),
        P(),
        P(),
        P(("vis", "tile"), None),
        P(("vis", "tile"), None),
    )
    return jax.shard_map(
        on_device, mesh=mesh, in_specs=placed, out_specs=P("tile", "vis", None), check_vma=False
    )
```

```python
import functools

import jax
import jax.numpy as jnp
from jax import lax
from jax.experimental import pallas as pl
from jax.experimental.pallas import tpu as pltpu
from jax.sharding import PartitionSpec as P

BLK_DEV = 8
SUB = 32
POLC = 8
TAPS = 7
OS = 16
TS = 256
GT = 8
SCAP = 2
LANES = 128
ROWS = 8
GROUP = 4
PIECES = 4
VMEM_BYTES = 24 << 20
FAR = 1 << 20
MESH = pl.DeviceIdType.MESH
NT = (((1,), (1,)), ((), ()))


def dispatch_kernel(
    slot_cap, vis, u_cell, v_cell, u_frac, v_frac, w_plane, route, taps, gain, out, table, taper, feat, dest
):
    rows = vis.shape[0]
    columns = vis.shape[1]
    channels = u_cell.shape[0]
    owners, _, chunk = out.shape
    groups = owners * BLK_DEV
    feat[pl.ds(0, columns), :] = vis[...].astype(jnp.float32).T.astype(jnp.bfloat16)
    plane = w_plane[...] * OS
    codes = (u_cell[...], v_cell[...], plane + u_frac[...], plane + v_frac[...])
    codes = jnp.concatenate(codes, axis=0).astype(jnp.float32).astype(jnp.bfloat16)
    feat[pl.ds(columns, 4 * channels), :] = codes
    names = route[...]
    mine = lax.broadcasted_iota(jnp.int32, (groups, rows), 0) == names
    onehot = jnp.where(mine, 1.0, 0.0)
    earlier = lax.broadcasted_iota(jnp.int32, (rows, rows), 0) < lax.broadcasted_iota(
        jnp.int32, (rows, rows), 1
    )
    before = jnp.dot(
        onehot.astype(jnp.bfloat16),
        jnp.where(earlier, 1.0, 0.0).astype(jnp.bfloat16),
        preferred_element_type=jnp.float32,
    )
    rank = jnp.sum(onehot * before, axis=0, keepdims=True).astype(jnp.int32)
    dest[...] = names * slot_cap + rank

    table[...] = jnp.zeros_like(table)
    table[pl.ds(0, TAPS), :] = taps[...].astype(jnp.bfloat16).astype(jnp.float32)
    cells = lax.broadcasted_iota(jnp.int32, (SUB, SUB * POLC), 0)
    repeat = cells == lax.broadcasted_iota(jnp.int32, (SUB, SUB * POLC), 1) // POLC
    taper[...] = jnp.dot(
        gain[...],
        jnp.where(repeat, 1.0, 0.0),
        precision=lax.Precision.HIGHEST,
        preferred_element_type=jnp.float32,
    )

    def send(owner, _):
        slots = lax.broadcasted_iota(jnp.int32, (chunk, rows), 0) + owner * chunk
        pick = jnp.where(slots == dest[...], 1.0, 0.0).astype(jnp.bfloat16)
        out[owner] = lax.dot_general(
            feat[...], pick, NT, preferred_element_type=jnp.float32
        ).astype(jnp.bfloat16)
        return 0

    lax.fori_loop(0, owners, send, 0)


def spread(cell, taps):
    rows = lax.broadcasted_iota(jnp.int32, taps.shape, 0) - cell
    parts = []
    for start in range(0, SUB, ROWS):
        delta = rows + start
        weight = jnp.take_along_axis(taps, delta & (ROWS - 1), axis=0)
        parts.append(jnp.where((delta >= 0) & (delta < ROWS), weight, 0.0))
    return jnp.concatenate(parts, axis=0)


def grid_chunk(slot_cap, chunk, channels, lane, feat, table, total, left, right):
    covered = min(BLK_DEV, LANES // slot_cap)
    first = lane % chunk // slot_cap
    columns = channels * POLC
    lanes = lax.broadcasted_iota(jnp.int32, (SUB, LANES), 1)
    block = (lane + lanes) % chunk // slot_cap - first
    samples = feat[:columns, :].astype(jnp.float32)
    codes = feat[columns:, :].astype(jnp.float32).astype(jnp.int32)
    lookup = table[...]
    part = jnp.zeros((covered * SUB, SUB * POLC), jnp.float32)
    for h in range(channels):
        sample = samples[h * POLC : (h + 1) * POLC, :]
        cell_u = codes[h : h + 1, :]
        cell_v = codes[channels + h : channels + h + 1, :]
        row_u = codes[2 * channels + h : 2 * channels + h + 1, :]
        row_v = codes[3 * channels + h : 3 * channels + h + 1, :]
        taps_u = jnp.take_along_axis(lookup, jnp.broadcast_to(row_u, (8, LANES)), axis=1)
        taps_v = jnp.take_along_axis(lookup, jnp.broadcast_to(row_v, (8, LANES)), axis=1)
        weight_u = spread(cell_u, taps_u)
        weight_v = spread(cell_v, taps_v)
        here = pl.ds(h * LANES, LANES)
        weighted = weight_u[:, None, :] * sample[None, :, :]
        right[:, here] = weighted.reshape(SUB * POLC, LANES).astype(jnp.bfloat16)
        for b in range(covered):
            left[pl.ds(b * SUB, SUB), here] = jnp.where(block == b, weight_v, 0.0).astype(
                jnp.bfloat16
            )
        if (h + 1) % GROUP == 0:
            group = pl.ds((h + 1 - GROUP) * LANES, GROUP * LANES)
            part = part + lax.dot_general(
                left[:, group], right[:, group], NT, preferred_element_type=jnp.float32
            )
    place = pl.ds(pl.multiple_of(first * SUB, SUB), covered * SUB)
    total[place, :] = total[place, :] + part


def grid_kernel(slot_cap, chunk, channels, feat, table, taper, out, total, left, right):
    step = pl.program_id(0)

    @pl.when(step == 0)
    def _():
        total[...] = jnp.zeros_like(total)

    grid_chunk(
        slot_cap, chunk, channels, step * LANES, feat[0], table, total, left, right
    )

    @pl.when(step == pl.num_programs(0) - 1)
    def _():
        for b in range(BLK_DEV):
            out[b] = (total[pl.ds(b * SUB, SUB), :] * taper[...]).astype(jnp.bfloat16)


def swap(first, second, width):
    low = lax.broadcasted_iota(jnp.int32, first.shape, 1) // width % 2 == 0
    return (
        jnp.where(low, first, pltpu.roll(second, width, 1)),
        jnp.where(low, pltpu.roll(first, LANES - width, 1), second),
    )


def regroup_lanes(parts):
    quarter = LANES // GROUP
    first, second = swap(parts[0], parts[1], quarter)
    third, fourth = swap(parts[2], parts[3], quarter)
    first, third = swap(first, third, 2 * quarter)
    second, fourth = swap(second, fourth, 2 * quarter)
    return first, second, third, fourth


def weights(cell, taps):
    delta = lax.broadcasted_iota(jnp.int32, taps.shape, 0) - cell
    turned = jnp.take_along_axis(taps, delta & (ROWS - 1), axis=0)
    octave = delta >> 3
    return [jnp.where(octave == -g, turned, 0.0) for g in range(SUB // ROWS)]


def grid_part(channels, features, table, left, right, spare):
    width = channels // GROUP
    columns = channels * POLC
    span = width * POLC
    samples = regroup_lanes([features[q * span : (q + 1) * span] for q in range(GROUP)])
    start = [columns + q * 4 * width for q in range(GROUP)]
    codes = regroup_lanes([features[at : at + 4 * width] for at in start])
    lookup = table[...]
    parts = []
    for b in range(GROUP):
        code = codes[b].astype(jnp.int32)
        for g in range(width):
            sample = samples[b][g * POLC : (g + 1) * POLC, :]
            cell_u, cell_v, row_u, row_v = [
                code[kind * width + g : kind * width + g + 1, :] for kind in range(4)
            ]
            taps_u = jnp.take_along_axis(lookup, jnp.broadcast_to(row_u, (8, LANES)), axis=1)
            taps_v = jnp.take_along_axis(lookup, jnp.broadcast_to(row_v, (8, LANES)), axis=1)
            here = pl.ds(g * LANES, LANES)
            for place, weight in enumerate(weights(cell_u, taps_u)):
                spare[g, pl.ds(place * ROWS, ROWS), :] = weight
            for u in range(0, SUB, 2):
                pair = [spare[g, pl.ds(u + i, POLC, stride=0), :] * sample for i in range(2)]
                right[b, pl.ds(u * POLC, 2 * POLC), here] = jnp.concatenate(pair, axis=0).astype(
                    jnp.bfloat16
                )
            left[b, :, here] = jnp.concatenate(weights(cell_v, taps_v), axis=0).astype(jnp.bfloat16)
        parts.append(
            lax.dot_general(left[b], right[b], NT, preferred_element_type=jnp.float32)
        )
    return parts


def prepare(slot_cap, groups, vis, codes, route, feat, dest):
    rows, columns = vis.shape
    feat[pl.ds(0, columns), :] = vis[...].astype(jnp.float32).T.astype(jnp.bfloat16)
    u_cell, v_cell, u_frac, v_frac, w_plane = codes
    channels = u_cell.shape[0]
    plane = w_plane[...] * OS
    codes = (u_cell[...], v_cell[...], plane + u_frac[...], plane + v_frac[...])
    codes = jnp.concatenate(codes, axis=0).astype(jnp.float32).astype(jnp.bfloat16)
    count = 4 * channels
    width = channels // GROUP
    to = lax.broadcasted_iota(jnp.int32, (count, count), 0)
    quarter, rest = to // (4 * width), to % (4 * width)
    source = rest // width * channels + quarter * width + rest % width
    turn = source == lax.broadcasted_iota(jnp.int32, (count, count), 1)
    feat[pl.ds(columns, count), :] = jnp.dot(
        jnp.where(turn, 1.0, 0.0).astype(jnp.bfloat16), codes, preferred_element_type=jnp.float32
    ).astype(jnp.bfloat16)
    earlier = lax.broadcasted_iota(jnp.int32, (LANES, LANES), 0) < lax.broadcasted_iota(
        jnp.int32, (LANES, LANES), 1
    )
    earlier = jnp.where(earlier, 1.0, 0.0).astype(jnp.bfloat16)
    seen = jnp.zeros((groups, 1), jnp.float32)
    for start in range(0, rows, LANES):
        names = route[:, pl.ds(start, LANES)]
        mine = lax.broadcasted_iota(jnp.int32, (groups, LANES), 0) == names
        onehot = jnp.where(mine, 1.0, 0.0)
        before = seen + jnp.dot(
            onehot.astype(jnp.bfloat16), earlier, preferred_element_type=jnp.float32
        )
        rank = jnp.sum(onehot * before, axis=0, keepdims=True).astype(jnp.int32)
        dest[:, pl.ds(start, LANES)] = names * slot_cap + rank
        seen = seen + jnp.sum(onehot, axis=1, keepdims=True)


def reduce_kernel(
    slot_cap,
    vis_hbm,
    u_cell_hbm,
    v_cell_hbm,
    u_frac_hbm,
    v_frac_hbm,
    w_plane_hbm,
    route_hbm,
    taps_hbm,
    gain_hbm,
    tiles_hbm,
    anchors_hbm,
    out,
    meta_out,
    vis,
    u_cell,
    v_cell,
    u_frac,
    v_frac,
    w_plane,
    route,
    taps,
    gain,
    tiles,
    anchors,
    table,
    taper,
    feat,
    dest,
    ordered,
    left,
    right,
    spare,
    partial,
    x_sent,
    x_landed,
    z_sent,
    z_landed,
    meta,
    in_sem,
    meta_send,
    meta_recv,
    x_send,
    x_recv,
    z_send,
    z_recv,
    to_z_send,
    to_z_recv,
    to_x_send,
    to_x_recv,
):
    count = out.shape[0]
    height = count // 2
    rows = vis.shape[0]
    channels = u_cell.shape[0]
    chunk = BLK_DEV * slot_cap
    v, t = lax.axis_index("vis"), lax.axis_index("tile")
    z, x = v // 2, v % 2
    each = BLK_DEV // PIECES
    remote = functools.partial(pltpu.make_async_remote_copy, device_id_type=MESH)

    barrier = pltpu.get_barrier_semaphore()
    for k in range(1, count):
        pl.semaphore_signal(barrier, inc=1, device_id=((v + k) % count, t), device_id_type=MESH)
    pairs = (
        (vis_hbm, vis),
        (u_cell_hbm, u_cell),
        (v_cell_hbm, v_cell),
        (u_frac_hbm, u_frac),
        (v_frac_hbm, v_frac),
        (w_plane_hbm, w_plane),
        (route_hbm, route),
        (taps_hbm, taps),
        (gain_hbm, gain),
        (tiles_hbm, tiles),
        (anchors_hbm, anchors),
    )
    loads = [pltpu.make_async_copy(src, dst, in_sem.at[i]) for i, (src, dst) in enumerate(pairs)]
    for load in loads:
        load.start()
    meta[...] = jnp.zeros_like(meta)
    table[...] = jnp.zeros_like(table)
    for load in loads:
        load.wait()

    meta[pl.ds(0, 1), pl.ds(0, BLK_DEV)] = tiles[...]
    meta[pl.ds(1, 2), pl.ds(0, BLK_DEV)] = anchors[...]
    table[pl.ds(0, TAPS), :] = taps[...].astype(jnp.bfloat16).astype(jnp.float32)
    cells = lax.broadcasted_iota(jnp.int32, (SUB, SUB * POLC), 0)
    repeat = cells == lax.broadcasted_iota(jnp.int32, (SUB, SUB * POLC), 1) // POLC
    taper[...] = jnp.dot(
        gain[...],
        jnp.where(repeat, 1.0, 0.0),
        precision=lax.Precision.HIGHEST,
        preferred_element_type=jnp.float32,
    )
    prepare(
        slot_cap,
        count * BLK_DEV,
        vis,
        (u_cell, v_cell, u_frac, v_frac, w_plane),
        route,
        feat,
        dest,
    )
    pl.semaphore_wait(barrier, count - 1)

    def piece(i):
        return pl.ds(i * each, each)

    def tell(k):
        return remote(
            src_ref=meta,
            dst_ref=meta_out.at[v],
            send_sem=meta_send.at[k],
            recv_sem=meta_recv.at[k],
            device_id=((v + k) % count, t),
        )

    def add_x(j, i):
        return remote(
            src_ref=x_sent.at[j, piece(i)],
            dst_ref=x_landed.at[j, piece(i)],
            send_sem=x_send.at[j * PIECES + i],
            recv_sem=x_recv.at[j * PIECES + i],
            device_id=(z * 2 + 1 - x, t),
        )

    def add_z(j, i):
        return remote(
            src_ref=z_sent.at[j - 1, piece(i)],
            dst_ref=z_landed.at[j - 1, piece(i)],
            send_sem=z_send.at[(j - 1) * PIECES + i],
            recv_sem=z_recv.at[(j - 1) * PIECES + i],
            device_id=((z + j) % height * 2 + x, t),
        )

    def hand_z(source, side, i):
        ref = out.at[source * 2 + x, piece(i)]
        return remote(
            src_ref=ref,
            dst_ref=ref,
            send_sem=to_z_send.at[((1 + side) // 2 * height + source) * PIECES + i],
            recv_sem=to_z_recv.at[source * PIECES + i],
            device_id=((z + side) * 2 + x, t),
        )

    def give_x(j, i):
        ref = out.at[j * 2 + x, piece(i)]
        return remote(
            src_ref=ref,
            dst_ref=ref,
            send_sem=to_x_send.at[j * PIECES + i],
            recv_sem=to_x_recv.at[j * PIECES + i],
            device_id=(z * 2 + 1 - x, t),
        )

    for k in range(1, count):
        tell(k).start()
    meta_out[v] = meta[...]

    cells = lax.broadcasted_iota(jnp.int32, (chunk, rows), 0).astype(jnp.float32)
    cells = cells.astype(jnp.bfloat16)

    def plan(step):
        last = step == count - 1
        mine = jnp.logical_or(jnp.logical_and(step > 0, step % 2 == 0), last)
        j = jnp.where(last, 0, jnp.where(mine, step // 2, (step + 3) // 2 % height))
        return mine, j

    def sort(step, slot):
        mine, j = plan(step)
        owner = (z + j) % height * 2 + jnp.where(mine, x, 1 - x)
        slots = jnp.clip(dest[...] - owner * chunk, -1, chunk).astype(jnp.float32)
        pick = jnp.where(cells == slots.astype(jnp.bfloat16), 1.0, 0.0).astype(jnp.bfloat16)
        ordered[slot] = lax.dot_general(feat[...], pick, NT, preferred_element_type=jnp.float32)

    def grid_step(step, slot):
        mine, j = plan(step)
        sort(step + 1, 1 - slot)
        for d in range(chunk // LANES):
            features = ordered[slot, :, pl.ds(d * LANES, LANES)]
            grids = grid_part(channels, features, table, left, right, spare)
            for b, part in enumerate(grids):
                partial[d * GROUP + b] = part

        @pl.when(jnp.logical_not(mine))
        def _():
            for i in range(PIECES):
                x_sent[j, piece(i)] = partial[piece(i)].astype(jnp.bfloat16)
                add_x(j, i).start()

        @pl.when(mine)
        def _():
            for i in range(PIECES):
                add_x(j, i).wait_recv()
                partial[piece(i)] = partial[piece(i)] + x_landed[j, piece(i)].astype(jnp.float32)

                @pl.when(j > 0)
                def _():
                    z_sent[j - 1, piece(i)] = partial[piece(i)].astype(jnp.bfloat16)
                    add_z(j, i).start()

    def two_steps(half, _):
        grid_step(2 * half, 0)
        grid_step(2 * half + 1, 1)
        return 0

    sort(0, 0)
    lax.fori_loop(0, height, two_steps, 0)
    for i in range(PIECES):
        whole = partial[piece(i)]
        for j in range(1, height):
            add_z(j, i).wait_recv()
            whole = whole + z_landed[j - 1, piece(i)].astype(jnp.float32)
        out[v, piece(i)] = (whole * taper[...][None]).astype(jnp.bfloat16)
        @pl.when(z > 0)
        def _():
            hand_z(z, -1, i).start()

        @pl.when(z < height - 1)
        def _():
            hand_z(z, 1, i).start()

        give_x(z, i).start()
    for gap in range(1, height):
        for i in range(PIECES):
            for side in (1, -1):
                origin = z - side * gap

                @pl.when((origin >= 0) & (origin < height))
                def _():
                    hand_z(origin, side, i).wait_recv()
                    give_x(origin, i).start()

                    @pl.when((z + side >= 0) & (z + side < height))
                    def _():
                        hand_z(origin, side, i).start()

    for i in range(PIECES):
        for j in range(height):
            give_x(j, i).wait_recv()
    for k in range(1, count):
        tell(k).wait_recv()
    for k in range(1, count):
        tell(k).wait_send()
    for i in range(PIECES):
        for j in range(height):
            add_x(j, i).wait_send()
            give_x(j, i).wait_send()
        for j in range(1, height):
            add_z(j, i).wait_send()
        for j in range(height):

            @pl.when((j <= z) & (z < height - 1))
            def _():
                hand_z(j, 1, i).wait_send()

            @pl.when((j >= z) & (z > 0))
            def _():
                hand_z(j, -1, i).wait_send()


def canvas_kernel(meta, subs, out, canvas):
    v = lax.axis_index("vis")
    tiles, height, width = out.shape
    span = SUB * POLC
    canvas[:, pl.ds(SUB, height), :] = jnp.zeros((tiles, height, width + LANES), jnp.float32)

    def add_source(source, _):
        for b in range(BLK_DEV):
            tile = meta[source * ROWS, b]
            low = meta[source * ROWS + 1, b] - v * height + SUB
            column = meta[source * ROWS + 2, b] * POLC

            @pl.when((low > 0) & (low < height + SUB))
            def _():
                sub = subs[source, b].astype(jnp.float32)
                sub = jnp.concatenate([sub, jnp.zeros((SUB, LANES), jnp.float32)], axis=1)
                sub = pltpu.roll(sub, column % LANES, 1)
                sub = jnp.concatenate([sub, jnp.zeros((ROWS, span + LANES), jnp.float32)], axis=0)
                sub = pltpu.roll(sub, low % ROWS, 0)
                top = pl.multiple_of(low // ROWS * ROWS, ROWS)
                base = pl.multiple_of(column // LANES * LANES, LANES)
                here = (tile, pl.ds(top, SUB + ROWS), pl.ds(base, span + LANES))
                canvas[here] = canvas[here] + sub

        return 0

    lax.fori_loop(0, subs.shape[0], add_source, 0)
    out[...] = canvas[:, pl.ds(SUB, height), pl.ds(0, width)].astype(jnp.bfloat16)


def fold_kernel(
    canvas, own, far_out, near, middle, near_send, near_recv, far_send, far_recv
):
    tiles, height, width = own.shape
    v, t = lax.axis_index("vis"), lax.axis_index("tile")
    beside = t + 1 - 2 * (t % 2)
    across = (t + 2) % 4
    corner = (beside + 2) % 4
    cut = height // 2
    barrier = pltpu.get_barrier_semaphore()
    for other in (beside, across):
        pl.semaphore_signal(barrier, inc=1, device_id=(v, other), device_id_type=MESH)
    pl.semaphore_wait(barrier, 2)
    pieces = [(g, i) for g in range(tiles) for i in range(2)]

    def to_beside(part, g, i):
        here = pl.ds(i * cut, cut)
        return pltpu.make_async_remote_copy(
            src_ref=canvas.at[(corner, beside)[part] * tiles + g, here],
            dst_ref=near.at[part, g, here],
            send_sem=near_send.at[(part * tiles + g) * 2 + i],
            recv_sem=near_recv.at[(part * tiles + g) * 2 + i],
            device_id=(v, beside),
            device_id_type=MESH,
        )

    def to_across(g, i):
        here = pl.ds(i * cut, cut)
        return pltpu.make_async_remote_copy(
            src_ref=middle.at[g, here],
            dst_ref=far_out.at[g, here],
            send_sem=far_send.at[g * 2 + i],
            recv_sem=far_recv.at[g * 2 + i],
            device_id=(v, across),
            device_id_type=MESH,
        )

    for part in range(2):
        for g, i in pieces:
            to_beside(part, g, i).start()
    for g, i in pieces:
        here = pl.ds(i * cut, cut)
        to_beside(0, g, i).wait_recv()
        middle[g, here] = (
            canvas[across * tiles + g, here].astype(jnp.float32)
            + near[0, g, here].astype(jnp.float32)
        ).astype(jnp.bfloat16)
        to_across(g, i).start()
    for g, i in pieces:
        here = pl.ds(i * cut, cut)
        to_beside(1, g, i).wait_recv()
        own[g, here] = canvas[t * tiles + g, here].astype(jnp.float32) + near[1, g, here].astype(
            jnp.float32
        )
    for g, i in pieces:
        to_across(g, i).wait_recv()
    for g, i in pieces:
        for part in range(2):
            to_beside(part, g, i).wait_send()
        to_across(g, i).wait_send()


def slot_kernel(tiles, anchors, subs, out, meta):
    slots = out.shape[0]
    out[...] = jnp.zeros_like(out)
    lanes = lax.broadcasted_iota(jnp.int32, meta.shape, 1)
    places = jnp.full(meta.shape, -FAR, jnp.int32)
    for b in range(BLK_DEV):
        slot = tiles[0, b] * SCAP
        for before in range(b):
            slot = slot + jnp.where(tiles[0, before] == tiles[0, b], 1, 0)
        out[slot] = subs[b]
        places = jnp.where(lanes == slot, anchors[0, b], places)
        places = jnp.where(lanes == slots + slot, anchors[1, b], places)
    meta[...] = places


def gather_kernel(subs, meta, out, meta_out, own_sem, near_send, near_recv, far_send, far_recv):
    count = out.shape[0]
    width = out.shape[1]
    v, t = lax.axis_index("vis"), lax.axis_index("tile")
    half = count // 2
    spot = v // 2 * (1 - v % 2) + (count - 1 - v // 2) * (v % 2)

    def member(position):
        position = (position + 2 * count) % count
        back = position // half
        return (1 - back) * 2 * position + back * (2 * (count - 1 - position) + 1)

    barrier = pltpu.get_barrier_semaphore()
    for side in (1, -1):
        pl.semaphore_signal(
            barrier, inc=1, device_id=(member(spot + side), t), device_id_type=MESH
        )
    for k in range(1, width):
        pl.semaphore_signal(barrier, inc=1, device_id=(v, (t + k) % width), device_id_type=MESH)
    pl.semaphore_wait(barrier, 1 + width)

    def near(k):
        chunk = pl.ds((t + k) % width, 1)
        pairs = ((subs.at[chunk], out.at[v, pl.ds(t, 1)]), (meta, meta_out.at[v, t]))
        return [
            pltpu.make_async_remote_copy(
                src_ref=src,
                dst_ref=dst,
                send_sem=near_send.at[2 * k + i],
                recv_sem=near_recv.at[2 * k + i],
                device_id=(v, (t + k) % width),
                device_id_type=MESH,
            )
            for i, (src, dst) in enumerate(pairs)
        ]

    def own():
        pairs = ((subs.at[pl.ds(t, 1)], out.at[v, pl.ds(t, 1)]), (meta, meta_out.at[v, t]))
        return [
            pltpu.make_async_copy(src, dst, own_sem.at[i]) for i, (src, dst) in enumerate(pairs)
        ]

    def far(k, step):
        source = (t + width - k) % width
        cut = out.shape[2] // 2
        copies = []
        for i in range(3):
            side = 1 - 2 * (i % 2)
            origin = member(spot - side * step)
            if i < 2:
                ref = out.at[origin, source, pl.ds(i * cut, cut)]
            else:
                ref = meta_out.at[origin, source]
            copies.append(
                pltpu.make_async_remote_copy(
                    src_ref=ref,
                    dst_ref=ref,
                    send_sem=far_send.at[(step * width + k) * 3 + i],
                    recv_sem=far_recv.at[(step * width + k) * 3 + i],
                    device_id=(member(spot + side), t),
                    device_id_type=MESH,
                )
            )
        return copies

    for copy in own():
        copy.start()
    for k in range(1, width):
        for copy in near(k):
            copy.start()
    for copy in own():
        copy.wait()
    for k in range(width):
        if k:
            for copy in near(k):
                copy.wait_recv()
        for copy in far(k, 0):
            copy.start()

    def forward(step, _):
        for k in range(width):
            for landed, copy in zip(far(k, step - 1), far(k, step)):
                landed.wait_recv()
                copy.start()
        return 0

    lax.fori_loop(1, count - 1, forward, 0)
    for k in range(width):
        for copy in far(k, count - 2):
            copy.wait_recv()
    for k in range(1, width):
        for copy in near(k):
            copy.wait_send()

    def sent(step, _):
        for k in range(width):
            for copy in far(k, step):
                copy.wait_send()
        return 0

    lax.fori_loop(0, count - 1, sent, 0)


def place_kernel(tile_slots, meta, subs, out, canvas):
    v, t = lax.axis_index("vis"), lax.axis_index("tile")
    step = pl.program_id(0)
    slots = subs.shape[1]
    height = out.shape[1]
    width = out.shape[2]
    span = SUB * POLC

    @pl.when(step == 0)
    def _():
        canvas[...] = jnp.zeros_like(canvas)

    def add_source(near, _):
        source = step * (slots // tile_slots) + near
        for slot in range(tile_slots):
            lane = t * tile_slots + slot
            low = meta[source, lane] - v * height + SUB
            column = meta[source, slots + lane] * POLC

            @pl.when((low > 0) & (low < height + SUB))
            def _():
                sub = subs[0, near * tile_slots + slot].astype(jnp.float32)
                sub = jnp.concatenate([sub, jnp.zeros((SUB, LANES), jnp.float32)], axis=1)
                sub = pltpu.roll(sub, column % LANES, 1)
                sub = jnp.concatenate([sub, jnp.zeros((ROWS, span + LANES), jnp.float32)], axis=0)
                sub = pltpu.roll(sub, low % ROWS, 0)
                top = pl.multiple_of(low // ROWS * ROWS, ROWS)
                base = pl.multiple_of(column // LANES * LANES, LANES)
                here = (slot // SCAP, pl.ds(top, SUB + ROWS), pl.ds(base, span + LANES))
                canvas[here] = canvas[here] + sub

        return 0

    lax.fori_loop(0, slots // tile_slots, add_source, 0)

    @pl.when(step == pl.num_programs(0) - 1)
    def _():
        out[...] = canvas[:, pl.ds(SUB, height), pl.ds(0, width)]


def on_device(
    vis_data,
    u_cell,
    v_cell,
    u_frac,
    v_frac,
    w_plane,
    block_route,
    kernel_taps,
    taper_gain,
    sub_tile,
    sub_anchor,
):
    vis_count = lax.axis_size("vis")
    tile_width = lax.axis_size("tile")
    gt_dev = GT // tile_width
    rows, columns = vis_data.shape
    channels = u_cell.shape[0]
    slot_cap = max(2, 2 * rows // (BLK_DEV * vis_count))
    chunk = BLK_DEV * slot_cap
    grouped = (
        slot_cap * GROUP == LANES
        and channels % GROUP == 0
        and vis_count % 2 == 0
        and vis_count > 2
        and tile_width == 4
        and TS // vis_count % 32 == 0
    )
    features = columns + 4 * channels
    per_owner = gt_dev * SCAP
    slots = tile_width * per_owner
    height = TS // vis_count
    width = TS * POLC

    vmem = pl.BlockSpec(memory_space=pltpu.VMEM)
    if grouped:
        layers = vis_count // 2
        block = (SUB, SUB * POLC)
        lanes = channels // GROUP * LANES
        operands = (
            vis_data,
            u_cell,
            v_cell,
            u_frac,
            v_frac,
            w_plane,
            block_route.reshape(1, rows),
            kernel_taps.T,
            taper_gain,
            sub_tile.reshape(1, BLK_DEV),
            sub_anchor.T,
        )
        subs, meta = pl.pallas_call(
            functools.partial(reduce_kernel, slot_cap),
            in_specs=[pl.BlockSpec(memory_space=pltpu.HBM)] * len(operands),
            out_specs=[vmem] * 2,
            out_shape=[
                jax.ShapeDtypeStruct((vis_count, BLK_DEV) + block, jnp.bfloat16),
                jax.ShapeDtypeStruct((vis_count, ROWS, LANES), jnp.int32),
            ],
            scratch_shapes=[pltpu.VMEM(operand.shape, operand.dtype) for operand in operands]
            + [
                pltpu.VMEM((ROWS, LANES), jnp.float32),
                pltpu.VMEM(block, jnp.float32),
                pltpu.VMEM((features, rows), jnp.bfloat16),
                pltpu.VMEM((1, rows), jnp.int32),
                pltpu.VMEM((2, features, chunk), jnp.float32),
                pltpu.VMEM((GROUP, SUB, lanes), jnp.bfloat16),
                pltpu.VMEM((GROUP, SUB * POLC, lanes), jnp.bfloat16),
                pltpu.VMEM((channels // GROUP, SUB, LANES), jnp.float32),
                pltpu.VMEM((BLK_DEV,) + block, jnp.float32),
                pltpu.VMEM((layers, BLK_DEV) + block, jnp.bfloat16),
                pltpu.VMEM((layers, BLK_DEV) + block, jnp.bfloat16),
                pltpu.VMEM((layers - 1, BLK_DEV) + block, jnp.bfloat16),
                pltpu.VMEM((layers - 1, BLK_DEV) + block, jnp.bfloat16),
                pltpu.VMEM((ROWS, LANES), jnp.int32),
                pltpu.SemaphoreType.DMA((len(operands),)),
            ]
            + [
                pltpu.SemaphoreType.DMA((lots,))
                for lots in [vis_count] * 2
                + [layers * PIECES] * 2
                + [(layers - 1) * PIECES] * 2
                + [2 * layers * PIECES]
                + [layers * PIECES] * 3
            ],
            compiler_params=pltpu.CompilerParams(
                collective_id=1, has_side_effects=True, vmem_limit_bytes=VMEM_BYTES
            ),
            name="reduce",
        )(*[pltpu.with_memory_space_constraint(operand, pltpu.HBM) for operand in operands])
        canvas = pl.pallas_call(
            canvas_kernel,
            grid_spec=pltpu.PrefetchScalarGridSpec(
                num_scalar_prefetch=1,
                grid=(1,),
                in_specs=[vmem],
                out_specs=vmem,
                scratch_shapes=[
                    pltpu.VMEM((GT, height + 2 * SUB + ROWS, width + LANES), jnp.float32),
                ],
            ),
            out_shape=jax.ShapeDtypeStruct((GT, height, width), jnp.bfloat16),
            compiler_params=pltpu.CompilerParams(vmem_limit_bytes=VMEM_BYTES),
            name="canvas",
        )(meta.reshape(vis_count * ROWS, LANES), subs)
        portion = (gt_dev, height, width)
        own, other = pl.pallas_call(
            fold_kernel,
            in_specs=[vmem],
            out_specs=[vmem] * 2,
            out_shape=[
                jax.ShapeDtypeStruct(portion, jnp.float32),
                jax.ShapeDtypeStruct(portion, jnp.bfloat16),
            ],
            scratch_shapes=[
                pltpu.VMEM((2,) + portion, jnp.bfloat16),
                pltpu.VMEM(portion, jnp.bfloat16),
                pltpu.SemaphoreType.DMA((4 * gt_dev,)),
                pltpu.SemaphoreType.DMA((4 * gt_dev,)),
                pltpu.SemaphoreType.DMA((2 * gt_dev,)),
                pltpu.SemaphoreType.DMA((2 * gt_dev,)),
            ],
            compiler_params=pltpu.CompilerParams(
                collective_id=0, has_side_effects=True, vmem_limit_bytes=VMEM_BYTES
            ),
            name="fold",
        )(canvas)
        return own + other.astype(jnp.float32)

    send, table, taper = pl.pallas_call(
        functools.partial(dispatch_kernel, slot_cap),
        out_shape=[
            jax.ShapeDtypeStruct((vis_count, features, chunk), jnp.bfloat16),
            jax.ShapeDtypeStruct((ROWS, LANES), jnp.float32),
            jax.ShapeDtypeStruct((SUB, SUB * POLC), jnp.float32),
        ],
        scratch_shapes=[
            pltpu.VMEM((features, rows), jnp.bfloat16),
            pltpu.VMEM((1, rows), jnp.int32),
        ],
        name="dispatch",
    )(
        vis_data,
        u_cell,
        v_cell,
        u_frac,
        v_frac,
        w_plane,
        block_route.reshape(1, rows),
        kernel_taps.T,
        taper_gain,
    )
    covered = min(BLK_DEV, LANES // slot_cap)
    work = [
        pltpu.VMEM((BLK_DEV * SUB, SUB * POLC), jnp.float32),
        pltpu.VMEM((covered * SUB, channels * LANES), jnp.bfloat16),
        pltpu.VMEM((SUB * POLC, channels * LANES), jnp.bfloat16),
    ]
    gridded = jax.ShapeDtypeStruct((BLK_DEV, SUB, SUB * POLC), jnp.bfloat16)
    moved = lax.all_to_all(send, "vis", split_axis=0, concat_axis=0, tiled=True)
    moved = jnp.transpose(moved, (1, 0, 2)).reshape(1, features, vis_count * chunk)
    subs = pl.pallas_call(
        functools.partial(grid_kernel, slot_cap, chunk, channels),
        grid=(moved.shape[2] // LANES,),
        in_specs=[
            pl.BlockSpec((1, features, LANES), lambda s: (0, 0, s)),
            pl.BlockSpec(table.shape, lambda s: (0, 0)),
            pl.BlockSpec(taper.shape, lambda s: (0, 0)),
        ],
        out_specs=pl.BlockSpec(gridded.shape, lambda s: (0, 0, 0)),
        out_shape=gridded,
        scratch_shapes=work,
        name="grid",
    )(moved, table, taper)
    scalars = pl.BlockSpec(memory_space=pltpu.SMEM)
    subs, meta = pl.pallas_call(
        slot_kernel,
        in_specs=[scalars, scalars, vmem],
        out_specs=[vmem, vmem],
        out_shape=[
            jax.ShapeDtypeStruct((slots, SUB, SUB * POLC), jnp.bfloat16),
            jax.ShapeDtypeStruct((1, LANES), jnp.int32),
        ],
        name="slot",
    )(sub_tile.reshape(1, BLK_DEV), sub_anchor.T, subs)
    hops = (vis_count - 1) * tile_width * 3
    subs, meta = pl.pallas_call(
        gather_kernel,
        in_specs=[vmem, vmem],
        out_specs=[vmem, vmem],
        out_shape=[
            jax.ShapeDtypeStruct(
                (vis_count, tile_width, per_owner, SUB, SUB * POLC), jnp.bfloat16
            ),
            jax.ShapeDtypeStruct((vis_count, tile_width, 1, LANES), jnp.int32),
        ],
        scratch_shapes=[
            pltpu.SemaphoreType.DMA((2,)),
            pltpu.SemaphoreType.DMA((2 * tile_width,)),
            pltpu.SemaphoreType.DMA((2 * tile_width,)),
            pltpu.SemaphoreType.DMA((hops,)),
            pltpu.SemaphoreType.DMA((hops,)),
        ],
        compiler_params=pltpu.CompilerParams(collective_id=0, has_side_effects=True),
        name="gather",
    )(subs.reshape(tile_width, per_owner, SUB, SUB * POLC), meta)
    subs = subs.reshape(vis_count, slots, SUB, SUB * POLC)
    meta = meta.reshape(vis_count * tile_width, LANES)
    return pl.pallas_call(
        functools.partial(place_kernel, per_owner),
        grid_spec=pltpu.PrefetchScalarGridSpec(
            num_scalar_prefetch=1,
            grid=(vis_count,),
            in_specs=[pl.BlockSpec((1, slots, SUB, SUB * POLC), lambda s, *_: (s, 0, 0, 0))],
            out_specs=pl.BlockSpec((gt_dev, height, width), lambda s, *_: (0, 0, 0)),
            scratch_shapes=[
                pltpu.VMEM((gt_dev, -(-height // ROWS) * ROWS + 2 * SUB + ROWS, width + LANES), jnp.float32),
            ],
        ),
        out_shape=jax.ShapeDtypeStruct((gt_dev, height, width), jnp.float32),
        name="place",
    )(meta, subs)


def solution(mesh):
    placed = (
        P(("vis", "tile"), None),
        P(None, ("vis", "tile")),
        P(None, ("vis", "tile")),
        P(None, ("vis", "tile")),
        P(None, ("vis", "tile")),
        P(None, ("vis", "tile")),
        P(("vis", "tile"), None),
        P(),
        P(),
        P(("vis", "tile"), None),
        P(("vis", "tile"), None),
    )
    return jax.shard_map(
        on_device, mesh=mesh, in_specs=placed, out_specs=P("tile", "vis", None), check_vma=False
    )
```

```python
import functools

import jax
import jax.numpy as jnp
from jax import lax
from jax.experimental import pallas as pl
from jax.experimental.pallas import tpu as pltpu
from jax.sharding import PartitionSpec as P

BLK_DEV = 8
SUB = 32
POLC = 8
TAPS = 7
OS = 16
TS = 256
GT = 8
SCAP = 2
LANES = 128
ROWS = 8
GROUP = 4
PIECES = 4
LUMPS = 4
VMEM_BYTES = 24 << 20
FAR = 1 << 20
MESH = pl.DeviceIdType.MESH
NT = (((1,), (1,)), ((), ()))


def dispatch_kernel(
    slot_cap, vis, u_cell, v_cell, u_frac, v_frac, w_plane, route, taps, gain, out, table, taper, feat, dest
):
    rows = vis.shape[0]
    columns = vis.shape[1]
    channels = u_cell.shape[0]
    owners, _, chunk = out.shape
    groups = owners * BLK_DEV
    feat[pl.ds(0, columns), :] = vis[...].astype(jnp.float32).T.astype(jnp.bfloat16)
    plane = w_plane[...] * OS
    codes = (u_cell[...], v_cell[...], plane + u_frac[...], plane + v_frac[...])
    codes = jnp.concatenate(codes, axis=0).astype(jnp.float32).astype(jnp.bfloat16)
    feat[pl.ds(columns, 4 * channels), :] = codes
    names = route[...]
    mine = lax.broadcasted_iota(jnp.int32, (groups, rows), 0) == names
    onehot = jnp.where(mine, 1.0, 0.0)
    earlier = lax.broadcasted_iota(jnp.int32, (rows, rows), 0) < lax.broadcasted_iota(
        jnp.int32, (rows, rows), 1
    )
    before = jnp.dot(
        onehot.astype(jnp.bfloat16),
        jnp.where(earlier, 1.0, 0.0).astype(jnp.bfloat16),
        preferred_element_type=jnp.float32,
    )
    rank = jnp.sum(onehot * before, axis=0, keepdims=True).astype(jnp.int32)
    dest[...] = names * slot_cap + rank

    table[...] = jnp.zeros_like(table)
    table[pl.ds(0, TAPS), :] = taps[...].astype(jnp.bfloat16).astype(jnp.float32)
    cells = lax.broadcasted_iota(jnp.int32, (SUB, SUB * POLC), 0)
    repeat = cells == lax.broadcasted_iota(jnp.int32, (SUB, SUB * POLC), 1) // POLC
    taper[...] = jnp.dot(
        gain[...],
        jnp.where(repeat, 1.0, 0.0),
        precision=lax.Precision.HIGHEST,
        preferred_element_type=jnp.float32,
    )

    def send(owner, _):
        slots = lax.broadcasted_iota(jnp.int32, (chunk, rows), 0) + owner * chunk
        pick = jnp.where(slots == dest[...], 1.0, 0.0).astype(jnp.bfloat16)
        out[owner] = lax.dot_general(
            feat[...], pick, NT, preferred_element_type=jnp.float32
        ).astype(jnp.bfloat16)
        return 0

    lax.fori_loop(0, owners, send, 0)


def spread(cell, taps):
    rows = lax.broadcasted_iota(jnp.int32, taps.shape, 0) - cell
    parts = []
    for start in range(0, SUB, ROWS):
        delta = rows + start
        weight = jnp.take_along_axis(taps, delta & (ROWS - 1), axis=0)
        parts.append(jnp.where((delta >= 0) & (delta < ROWS), weight, 0.0))
    return jnp.concatenate(parts, axis=0)


def grid_chunk(slot_cap, chunk, channels, lane, feat, table, total, left, right):
    covered = min(BLK_DEV, LANES // slot_cap)
    first = lane % chunk // slot_cap
    columns = channels * POLC
    lanes = lax.broadcasted_iota(jnp.int32, (SUB, LANES), 1)
    block = (lane + lanes) % chunk // slot_cap - first
    samples = feat[:columns, :].astype(jnp.float32)
    codes = feat[columns:, :].astype(jnp.float32).astype(jnp.int32)
    lookup = table[...]
    part = jnp.zeros((covered * SUB, SUB * POLC), jnp.float32)
    for h in range(channels):
        sample = samples[h * POLC : (h + 1) * POLC, :]
        cell_u = codes[h : h + 1, :]
        cell_v = codes[channels + h : channels + h + 1, :]
        row_u = codes[2 * channels + h : 2 * channels + h + 1, :]
        row_v = codes[3 * channels + h : 3 * channels + h + 1, :]
        taps_u = jnp.take_along_axis(lookup, jnp.broadcast_to(row_u, (8, LANES)), axis=1)
        taps_v = jnp.take_along_axis(lookup, jnp.broadcast_to(row_v, (8, LANES)), axis=1)
        weight_u = spread(cell_u, taps_u)
        weight_v = spread(cell_v, taps_v)
        here = pl.ds(h * LANES, LANES)
        weighted = weight_u[:, None, :] * sample[None, :, :]
        right[:, here] = weighted.reshape(SUB * POLC, LANES).astype(jnp.bfloat16)
        for b in range(covered):
            left[pl.ds(b * SUB, SUB), here] = jnp.where(block == b, weight_v, 0.0).astype(
                jnp.bfloat16
            )
        if (h + 1) % GROUP == 0:
            group = pl.ds((h + 1 - GROUP) * LANES, GROUP * LANES)
            part = part + lax.dot_general(
                left[:, group], right[:, group], NT, preferred_element_type=jnp.float32
            )
    place = pl.ds(pl.multiple_of(first * SUB, SUB), covered * SUB)
    total[place, :] = total[place, :] + part


def grid_kernel(slot_cap, chunk, channels, feat, table, taper, out, total, left, right):
    step = pl.program_id(0)

    @pl.when(step == 0)
    def _():
        total[...] = jnp.zeros_like(total)

    grid_chunk(
        slot_cap, chunk, channels, step * LANES, feat[0], table, total, left, right
    )

    @pl.when(step == pl.num_programs(0) - 1)
    def _():
        for b in range(BLK_DEV):
            out[b] = (total[pl.ds(b * SUB, SUB), :] * taper[...]).astype(jnp.bfloat16)


def swap(first, second, width):
    low = lax.broadcasted_iota(jnp.int32, first.shape, 1) // width % 2 == 0
    return (
        jnp.where(low, first, pltpu.roll(second, width, 1)),
        jnp.where(low, pltpu.roll(first, LANES - width, 1), second),
    )


def regroup_lanes(parts):
    quarter = LANES // GROUP
    first, second = swap(parts[0], parts[1], quarter)
    third, fourth = swap(parts[2], parts[3], quarter)
    first, third = swap(first, third, 2 * quarter)
    second, fourth = swap(second, fourth, 2 * quarter)
    return first, second, third, fourth


def weights(cell, taps):
    delta = lax.broadcasted_iota(jnp.int32, taps.shape, 0) - cell
    turned = jnp.take_along_axis(taps, delta & (ROWS - 1), axis=0)
    octave = delta >> 3
    return [jnp.where(octave == -g, turned, 0.0) for g in range(SUB // ROWS)]


def grid_part(channels, features, table, left, right, spare):
    width = channels // GROUP
    columns = channels * POLC
    span = width * POLC
    samples = regroup_lanes([features[q * span : (q + 1) * span] for q in range(GROUP)])
    start = [columns + q * 4 * width for q in range(GROUP)]
    codes = regroup_lanes([features[at : at + 4 * width] for at in start])
    lookup = table[...]
    parts = []
    for b in range(GROUP):
        code = codes[b].astype(jnp.int32)
        for g in range(width):
            sample = samples[b][g * POLC : (g + 1) * POLC, :]
            cell_u, cell_v, row_u, row_v = [
                code[kind * width + g : kind * width + g + 1, :] for kind in range(4)
            ]
            taps_u = jnp.take_along_axis(lookup, jnp.broadcast_to(row_u, (8, LANES)), axis=1)
            taps_v = jnp.take_along_axis(lookup, jnp.broadcast_to(row_v, (8, LANES)), axis=1)
            here = pl.ds(g * LANES, LANES)
            for place, weight in enumerate(weights(cell_u, taps_u)):
                spare[g, pl.ds(place * ROWS, ROWS), :] = weight
            for u in range(0, SUB, 2):
                pair = [spare[g, pl.ds(u + i, POLC, stride=0), :] * sample for i in range(2)]
                right[b, pl.ds(u * POLC, 2 * POLC), here] = jnp.concatenate(pair, axis=0).astype(
                    jnp.bfloat16
                )
            left[b, :, here] = jnp.concatenate(weights(cell_v, taps_v), axis=0).astype(jnp.bfloat16)
        parts.append(
            lax.dot_general(left[b], right[b], NT, preferred_element_type=jnp.float32)
        )
    return parts


def rank_rows(slot_cap, groups, route, dest):
    rows = route.shape[1]
    earlier = lax.broadcasted_iota(jnp.int32, (LANES, LANES), 0) < lax.broadcasted_iota(
        jnp.int32, (LANES, LANES), 1
    )
    earlier = jnp.where(earlier, 1.0, 0.0).astype(jnp.bfloat16)
    seen = jnp.zeros((groups, 1), jnp.float32)
    for start in range(0, rows, LANES):
        names = route[:, pl.ds(start, LANES)]
        mine = lax.broadcasted_iota(jnp.int32, (groups, LANES), 0) == names
        onehot = jnp.where(mine, 1.0, 0.0)
        before = seen + jnp.dot(
            onehot.astype(jnp.bfloat16), earlier, preferred_element_type=jnp.float32
        )
        rank = jnp.sum(onehot * before, axis=0, keepdims=True).astype(jnp.int32)
        dest[:, pl.ds(start, LANES)] = names * slot_cap + rank
        seen = seen + jnp.sum(onehot, axis=1, keepdims=True)


def stack_features(vis, codes, feat):
    columns = vis.shape[1]
    feat[pl.ds(0, columns), :] = vis[...].astype(jnp.float32).T.astype(jnp.bfloat16)
    u_cell, v_cell, u_frac, v_frac, w_plane = codes
    channels = u_cell.shape[0]
    plane = w_plane[...] * OS
    codes = (u_cell[...], v_cell[...], plane + u_frac[...], plane + v_frac[...])
    codes = jnp.concatenate(codes, axis=0).astype(jnp.float32).astype(jnp.bfloat16)
    count = 4 * channels
    width = channels // GROUP
    to = lax.broadcasted_iota(jnp.int32, (count, count), 0)
    quarter, rest = to // (4 * width), to % (4 * width)
    source = rest // width * channels + quarter * width + rest % width
    turn = source == lax.broadcasted_iota(jnp.int32, (count, count), 1)
    feat[pl.ds(columns, count), :] = jnp.dot(
        jnp.where(turn, 1.0, 0.0).astype(jnp.bfloat16), codes, preferred_element_type=jnp.float32
    ).astype(jnp.bfloat16)


def placement(facts, height, v, t):
    tiles = GT // 4
    lanes = lax.broadcasted_iota(jnp.int32, facts.shape, 1) // BLK_DEV
    low = facts - v * height + SUB
    low = jnp.where((low > 0) & (low < height + SUB), low, 0)
    group = pltpu.roll(facts, BLK_DEV, 1) // tiles
    own = jnp.where(group == t, low, 0)
    across = pltpu.roll(jnp.where(group == (t + 2) % 4, low, 0), 2 * BLK_DEV, 1)
    facts = jnp.where(lanes == 0, facts % tiles, facts * POLC)
    return jnp.where(lanes == 1, own, jnp.where(lanes == 3, across, facts))


def reduce_kernel(
    slot_cap,
    tile_rows,
    vis_hbm,
    u_cell_hbm,
    v_cell_hbm,
    u_frac_hbm,
    v_frac_hbm,
    w_plane_hbm,
    route_hbm,
    taps_hbm,
    gain_hbm,
    tiles_hbm,
    anchors_hbm,
    out,
    meta_out,
    vis,
    u_cell,
    v_cell,
    u_frac,
    v_frac,
    w_plane,
    route,
    taps,
    gain,
    tiles,
    anchors,
    table,
    taper,
    feat,
    dest,
    ordered,
    left,
    right,
    spare,
    partial,
    x_sent,
    x_landed,
    z_sent,
    z_landed,
    meta,
    in_sem,
    meta_send,
    meta_recv,
    x_send,
    x_recv,
    z_send,
    z_recv,
    to_z_send,
    to_z_recv,
    to_x_send,
    to_x_recv,
    to_core_send,
    to_core_recv,
    pass_send,
    pass_recv,
):
    count = out.shape[1]
    height = count // 2
    rows = vis.shape[0]
    channels = u_cell.shape[0]
    chunk = BLK_DEV * slot_cap
    v, t = lax.axis_index("vis"), lax.axis_index("tile")
    z, x = v // 2, v % 2
    c = t % 2
    beside = t + 1 - 2 * c
    each = BLK_DEV // PIECES
    remote = functools.partial(pltpu.make_async_remote_copy, device_id_type=MESH)

    barrier = pltpu.get_barrier_semaphore()
    for k in range(1, count):
        pl.semaphore_signal(barrier, inc=1, device_id=((v + k) % count, t), device_id_type=MESH)
    pl.semaphore_signal(barrier, inc=1, device_id=(v, beside), device_id_type=MESH)
    pairs = (
        (vis_hbm, vis),
        (u_cell_hbm, u_cell),
        (v_cell_hbm, v_cell),
        (u_frac_hbm, u_frac),
        (v_frac_hbm, v_frac),
        (w_plane_hbm, w_plane),
        (route_hbm, route),
        (taps_hbm, taps),
        (gain_hbm, gain),
        (tiles_hbm, tiles),
        (anchors_hbm, anchors),
    )
    loads = [pltpu.make_async_copy(src, dst, in_sem.at[i]) for i, (src, dst) in enumerate(pairs)]
    loads = [loads[6]] + loads[:6] + loads[7:]
    for load in loads:
        load.start()
    table[...] = jnp.zeros_like(table)

    loads[0].wait()
    rank_rows(slot_cap, count * BLK_DEV, route, dest)
    for load in loads[1:]:
        load.wait()
    stack_features(vis, (u_cell, v_cell, u_frac, v_frac, w_plane), feat)
    rest = jnp.zeros((1, LANES - 3 * BLK_DEV), jnp.int32)
    facts = [tiles[...], anchors[pl.ds(0, 1), :], anchors[pl.ds(1, 1), :], rest]
    meta[...] = jnp.concatenate(facts, axis=1)
    table[pl.ds(0, TAPS), :] = taps[...].astype(jnp.bfloat16).astype(jnp.float32)
    cells = lax.broadcasted_iota(jnp.int32, (SUB, SUB * POLC), 0)
    repeat = cells == lax.broadcasted_iota(jnp.int32, (SUB, SUB * POLC), 1) // POLC
    taper[...] = jnp.dot(
        gain[...],
        jnp.where(repeat, 1.0, 0.0),
        precision=lax.Precision.HIGHEST,
        preferred_element_type=jnp.float32,
    )
    pl.semaphore_wait(barrier, count)

    def piece(i):
        return pl.ds(i * each, each)

    def lump(i):
        return pl.ds(i * (BLK_DEV // LUMPS), BLK_DEV // LUMPS)

    def tell(k):
        return remote(
            src_ref=meta,
            dst_ref=meta_out.at[c, v],
            send_sem=meta_send.at[k],
            recv_sem=meta_recv.at[k],
            device_id=((v + k) % count, t),
        )

    def add_x(j, i):
        return remote(
            src_ref=x_sent.at[j, piece(i)],
            dst_ref=x_landed.at[j, piece(i)],
            send_sem=x_send.at[j * PIECES + i],
            recv_sem=x_recv.at[j * PIECES + i],
            device_id=(z * 2 + 1 - x, t),
        )

    def add_z(j, i):
        return remote(
            src_ref=z_sent.at[j - 1, piece(i)],
            dst_ref=z_landed.at[j - 1, piece(i)],
            send_sem=z_send.at[(j - 1) * PIECES + i],
            recv_sem=z_recv.at[(j - 1) * PIECES + i],
            device_id=((z + j) % height * 2 + x, t),
        )

    def hand_z(source, side, i):
        ref = out.at[c, source * 2 + x, lump(i)]
        return remote(
            src_ref=ref,
            dst_ref=ref,
            send_sem=to_z_send.at[((1 + side) // 2 * height + source) * LUMPS + i],
            recv_sem=to_z_recv.at[source * LUMPS + i],
            device_id=((z + side) * 2 + x, t),
        )

    def give_x(j, i):
        ref = out.at[c, j * 2 + x, lump(i)]
        return remote(
            src_ref=ref,
            dst_ref=ref,
            send_sem=to_x_send.at[j * LUMPS + i],
            recv_sem=to_x_recv.at[j * LUMPS + i],
            device_id=(z * 2 + 1 - x, t),
        )

    def give_core(source, column):
        ref = out.at[c, source * 2 + column]
        return remote(
            src_ref=ref,
            dst_ref=ref,
            send_sem=to_core_send.at[source * 2 + column],
            recv_sem=to_core_recv.at[source * 2 + column],
            device_id=(v, beside),
        )

    def pass_meta():
        ref = meta_out.at[c]
        return remote(
            src_ref=ref,
            dst_ref=ref,
            send_sem=pass_send.at[0],
            recv_sem=pass_recv.at[0],
            device_id=(v, beside),
        )

    for k in range(1, count):
        tell(k).start()
    meta_out[c, v] = meta[...]

    cells = lax.broadcasted_iota(jnp.int32, (chunk, rows), 0).astype(jnp.float32)
    cells = cells.astype(jnp.bfloat16)

    def plan(step):
        last = step == count - 1
        mine = jnp.logical_or(jnp.logical_and(step > 0, step % 2 == 0), last)
        j = jnp.where(last, 0, jnp.where(mine, step // 2, (step + 3) // 2 % height))
        return mine, j

    def sort(step, slot):
        mine, j = plan(step)
        owner = (z + j) % height * 2 + jnp.where(mine, x, 1 - x)
        slots = jnp.clip(dest[...] - owner * chunk, -1, chunk).astype(jnp.float32)
        pick = jnp.where(cells == slots.astype(jnp.bfloat16), 1.0, 0.0).astype(jnp.bfloat16)
        ordered[slot] = lax.dot_general(feat[...], pick, NT, preferred_element_type=jnp.float32)

    def grid_step(step, slot):
        mine, j = plan(step)
        sort(step + 1, 1 - slot)
        for d in range(chunk // LANES):
            features = ordered[slot, :, pl.ds(d * LANES, LANES)]
            grids = grid_part(channels, features, table, left, right, spare)
            for b, part in enumerate(grids):
                partial[d * GROUP + b] = part

        @pl.when(jnp.logical_not(mine))
        def _():
            for i in range(PIECES):
                x_sent[j, piece(i)] = partial[piece(i)].astype(jnp.bfloat16)
                add_x(j, i).start()

        @pl.when(mine)
        def _():
            for i in range(PIECES):
                add_x(j, i).wait_recv()
                partial[piece(i)] = partial[piece(i)] + x_landed[j, piece(i)].astype(jnp.float32)

                @pl.when(j > 0)
                def _():
                    z_sent[j - 1, piece(i)] = partial[piece(i)].astype(jnp.bfloat16)
                    add_z(j, i).start()

    def two_steps(half, _):
        grid_step(2 * half, 0)
        grid_step(2 * half + 1, 1)
        return 0

    sort(0, 0)
    lax.fori_loop(0, height, two_steps, 0)
    for i in range(PIECES):
        whole = partial[piece(i)]
        for j in range(1, height):
            add_z(j, i).wait_recv()
            whole = whole + z_landed[j - 1, piece(i)].astype(jnp.float32)
        out[c, v, piece(i)] = (whole * taper[...][None]).astype(jnp.bfloat16)
        if (i + 1) * LUMPS % PIECES:
            continue
        m = (i + 1) * LUMPS // PIECES - 1

        @pl.when(z > 0)
        def _():
            hand_z(z, -1, m).start()

        @pl.when(z < height - 1)
        def _():
            hand_z(z, 1, m).start()

        give_x(z, m).start()
    give_core(z, x).start()
    for k in range(1, count):
        tell(k).wait_recv()
    pass_meta().start()
    for gap in range(1, height):
        for i in range(LUMPS):
            for side in (1, -1):
                origin = z - side * gap

                @pl.when((origin >= 0) & (origin < height))
                def _():
                    hand_z(origin, side, i).wait_recv()

                    @pl.when((z + side >= 0) & (z + side < height))
                    def _():
                        hand_z(origin, side, i).start()

                    give_x(origin, i).start()
                    if i == LUMPS - 1:
                        give_core(origin, x).start()

    for gap in range(height):
        for side in (1, -1)[: 1 + min(gap, 1)]:
            origin = z - side * gap

            @pl.when((origin >= 0) & (origin < height))
            def _():
                for i in range(LUMPS):
                    give_x(origin, i).wait_recv()
                give_core(origin, 1 - x).start()

    for source in range(height):
        for column in range(2):
            give_core(source, column).wait()
    pass_meta().wait_recv()
    pass_meta().wait_send()
    for k in range(1, count):
        tell(k).wait_send()
    for parity in range(2):
        for source in range(count):
            facts = meta_out[parity, source]
            meta_out[parity, source] = placement(facts, tile_rows, v, t)
    for i in range(PIECES):
        for j in range(height):
            add_x(j, i).wait_send()
        for j in range(1, height):
            add_z(j, i).wait_send()
    for i in range(LUMPS):
        for j in range(height):
            give_x(j, i).wait_send()

            @pl.when((j <= z) & (z < height - 1))
            def _():
                hand_z(j, 1, i).wait_send()

            @pl.when((j >= z) & (z > 0))
            def _():
                hand_z(j, -1, i).wait_send()


def canvas_kernel(lane, meta, subs, out, canvas):
    tiles, height, width = out.shape
    span = SUB * POLC
    canvas[:, pl.ds(SUB, height), :] = jnp.zeros((tiles, height, width + LANES), jnp.float32)

    def add_source(source, _):
        for b in range(BLK_DEV):
            low = meta[source, lane + b]

            @pl.when(low > 0)
            def _():
                column = meta[source, 2 * BLK_DEV + b]
                sub = subs[source, b].astype(jnp.float32)
                sub = jnp.concatenate([sub, jnp.zeros((SUB, LANES), jnp.float32)], axis=1)
                sub = pltpu.roll(sub, column % LANES, 1)
                sub = jnp.concatenate([sub, jnp.zeros((ROWS, span + LANES), jnp.float32)], axis=0)
                sub = pltpu.roll(sub, low % ROWS, 0)
                top = pl.multiple_of(low // ROWS * ROWS, ROWS)
                base = pl.multiple_of(column // LANES * LANES, LANES)
                here = (meta[source, b], pl.ds(top, SUB + ROWS), pl.ds(base, span + LANES))
                canvas[here] = canvas[here] + sub

        return 0

    lax.fori_loop(0, subs.shape[0], add_source, 0)
    out[...] = canvas[:, pl.ds(SUB, height), pl.ds(0, width)].astype(out.dtype)


def slot_kernel(tiles, anchors, subs, out, meta):
    slots = out.shape[0]
    out[...] = jnp.zeros_like(out)
    lanes = lax.broadcasted_iota(jnp.int32, meta.shape, 1)
    places = jnp.full(meta.shape, -FAR, jnp.int32)
    for b in range(BLK_DEV):
        slot = tiles[0, b] * SCAP
        for before in range(b):
            slot = slot + jnp.where(tiles[0, before] == tiles[0, b], 1, 0)
        out[slot] = subs[b]
        places = jnp.where(lanes == slot, anchors[0, b], places)
        places = jnp.where(lanes == slots + slot, anchors[1, b], places)
    meta[...] = places


def gather_kernel(subs, meta, out, meta_out, own_sem, near_send, near_recv, far_send, far_recv):
    count = out.shape[0]
    width = out.shape[1]
    v, t = lax.axis_index("vis"), lax.axis_index("tile")
    half = count // 2
    spot = v // 2 * (1 - v % 2) + (count - 1 - v // 2) * (v % 2)

    def member(position):
        position = (position + 2 * count) % count
        back = position // half
        return (1 - back) * 2 * position + back * (2 * (count - 1 - position) + 1)

    barrier = pltpu.get_barrier_semaphore()
    for side in (1, -1):
        pl.semaphore_signal(
            barrier, inc=1, device_id=(member(spot + side), t), device_id_type=MESH
        )
    for k in range(1, width):
        pl.semaphore_signal(barrier, inc=1, device_id=(v, (t + k) % width), device_id_type=MESH)
    pl.semaphore_wait(barrier, 1 + width)

    def near(k):
        chunk = pl.ds((t + k) % width, 1)
        pairs = ((subs.at[chunk], out.at[v, pl.ds(t, 1)]), (meta, meta_out.at[v, t]))
        return [
            pltpu.make_async_remote_copy(
                src_ref=src,
                dst_ref=dst,
                send_sem=near_send.at[2 * k + i],
                recv_sem=near_recv.at[2 * k + i],
                device_id=(v, (t + k) % width),
                device_id_type=MESH,
            )
            for i, (src, dst) in enumerate(pairs)
        ]

    def own():
        pairs = ((subs.at[pl.ds(t, 1)], out.at[v, pl.ds(t, 1)]), (meta, meta_out.at[v, t]))
        return [
            pltpu.make_async_copy(src, dst, own_sem.at[i]) for i, (src, dst) in enumerate(pairs)
        ]

    def far(k, step):
        source = (t + width - k) % width
        cut = out.shape[2] // 2
        copies = []
        for i in range(3):
            side = 1 - 2 * (i % 2)
            origin = member(spot - side * step)
            if i < 2:
                ref = out.at[origin, source, pl.ds(i * cut, cut)]
            else:
                ref = meta_out.at[origin, source]
            copies.append(
                pltpu.make_async_remote_copy(
                    src_ref=ref,
                    dst_ref=ref,
                    send_sem=far_send.at[(step * width + k) * 3 + i],
                    recv_sem=far_recv.at[(step * width + k) * 3 + i],
                    device_id=(member(spot + side), t),
                    device_id_type=MESH,
                )
            )
        return copies

    for copy in own():
        copy.start()
    for k in range(1, width):
        for copy in near(k):
            copy.start()
    for copy in own():
        copy.wait()
    for k in range(width):
        if k:
            for copy in near(k):
                copy.wait_recv()
        for copy in far(k, 0):
            copy.start()

    def forward(step, _):
        for k in range(width):
            for landed, copy in zip(far(k, step - 1), far(k, step)):
                landed.wait_recv()
                copy.start()
        return 0

    lax.fori_loop(1, count - 1, forward, 0)
    for k in range(width):
        for copy in far(k, count - 2):
            copy.wait_recv()
    for k in range(1, width):
        for copy in near(k):
            copy.wait_send()

    def sent(step, _):
        for k in range(width):
            for copy in far(k, step):
                copy.wait_send()
        return 0

    lax.fori_loop(0, count - 1, sent, 0)


def place_kernel(tile_slots, meta, subs, out, canvas):
    v, t = lax.axis_index("vis"), lax.axis_index("tile")
    step = pl.program_id(0)
    slots = subs.shape[1]
    height = out.shape[1]
    width = out.shape[2]
    span = SUB * POLC

    @pl.when(step == 0)
    def _():
        canvas[...] = jnp.zeros_like(canvas)

    def add_source(near, _):
        source = step * (slots // tile_slots) + near
        for slot in range(tile_slots):
            lane = t * tile_slots + slot
            low = meta[source, lane] - v * height + SUB
            column = meta[source, slots + lane] * POLC

            @pl.when((low > 0) & (low < height + SUB))
            def _():
                sub = subs[0, near * tile_slots + slot].astype(jnp.float32)
                sub = jnp.concatenate([sub, jnp.zeros((SUB, LANES), jnp.float32)], axis=1)
                sub = pltpu.roll(sub, column % LANES, 1)
                sub = jnp.concatenate([sub, jnp.zeros((ROWS, span + LANES), jnp.float32)], axis=0)
                sub = pltpu.roll(sub, low % ROWS, 0)
                top = pl.multiple_of(low // ROWS * ROWS, ROWS)
                base = pl.multiple_of(column // LANES * LANES, LANES)
                here = (slot // SCAP, pl.ds(top, SUB + ROWS), pl.ds(base, span + LANES))
                canvas[here] = canvas[here] + sub

        return 0

    lax.fori_loop(0, slots // tile_slots, add_source, 0)

    @pl.when(step == pl.num_programs(0) - 1)
    def _():
        out[...] = canvas[:, pl.ds(SUB, height), pl.ds(0, width)]


def on_device(
    vis_data,
    u_cell,
    v_cell,
    u_frac,
    v_frac,
    w_plane,
    block_route,
    kernel_taps,
    taper_gain,
    sub_tile,
    sub_anchor,
):
    vis_count = lax.axis_size("vis")
    tile_width = lax.axis_size("tile")
    gt_dev = GT // tile_width
    rows, columns = vis_data.shape
    channels = u_cell.shape[0]
    slot_cap = max(2, 2 * rows // (BLK_DEV * vis_count))
    chunk = BLK_DEV * slot_cap
    grouped = (
        slot_cap * GROUP == LANES
        and channels % GROUP == 0
        and vis_count % 2 == 0
        and vis_count > 2
        and tile_width == 4
        and TS // vis_count % 32 == 0
    )
    features = columns + 4 * channels
    per_owner = gt_dev * SCAP
    slots = tile_width * per_owner
    height = TS // vis_count
    width = TS * POLC

    vmem = pl.BlockSpec(memory_space=pltpu.VMEM)
    if grouped:
        layers = vis_count // 2
        block = (SUB, SUB * POLC)
        lanes = channels // GROUP * LANES
        operands = (
            vis_data,
            u_cell,
            v_cell,
            u_frac,
            v_frac,
            w_plane,
            block_route.reshape(1, rows),
            kernel_taps.T,
            taper_gain,
            sub_tile.reshape(1, BLK_DEV),
            sub_anchor.T,
        )
        subs, meta = pl.pallas_call(
            functools.partial(reduce_kernel, slot_cap, height),
            in_specs=[pl.BlockSpec(memory_space=pltpu.HBM)] * len(operands),
            out_specs=[vmem] * 2,
            out_shape=[
                jax.ShapeDtypeStruct((2, vis_count, BLK_DEV) + block, jnp.bfloat16),
                jax.ShapeDtypeStruct((2, vis_count, 1, LANES), jnp.int32),
            ],
            scratch_shapes=[pltpu.VMEM(operand.shape, operand.dtype) for operand in operands]
            + [
                pltpu.VMEM((ROWS, LANES), jnp.float32),
                pltpu.VMEM(block, jnp.float32),
                pltpu.VMEM((features, rows), jnp.bfloat16),
                pltpu.VMEM((1, rows), jnp.int32),
                pltpu.VMEM((2, features, chunk), jnp.float32),
                pltpu.VMEM((GROUP, SUB, lanes), jnp.bfloat16),
                pltpu.VMEM((GROUP, SUB * POLC, lanes), jnp.bfloat16),
                pltpu.VMEM((channels // GROUP, SUB, LANES), jnp.float32),
                pltpu.VMEM((BLK_DEV,) + block, jnp.float32),
                pltpu.VMEM((layers, BLK_DEV) + block, jnp.bfloat16),
                pltpu.VMEM((layers, BLK_DEV) + block, jnp.bfloat16),
                pltpu.VMEM((layers - 1, BLK_DEV) + block, jnp.bfloat16),
                pltpu.VMEM((layers - 1, BLK_DEV) + block, jnp.bfloat16),
                pltpu.VMEM((1, LANES), jnp.int32),
                pltpu.SemaphoreType.DMA((len(operands),)),
            ]
            + [
                pltpu.SemaphoreType.DMA((lots,))
                for lots in [vis_count] * 2
                + [layers * PIECES] * 2
                + [(layers - 1) * PIECES] * 2
                + [2 * layers * LUMPS]
                + [layers * LUMPS] * 3
                + [vis_count] * 2
                + [1] * 2
            ],
            compiler_params=pltpu.CompilerParams(
                collective_id=1, has_side_effects=True, vmem_limit_bytes=VMEM_BYTES
            ),
            name="reduce",
        )(*[pltpu.with_memory_space_constraint(operand, pltpu.HBM) for operand in operands])
        meta = meta.reshape(2 * vis_count, LANES)
        subs = subs.reshape((2 * vis_count, BLK_DEV) + block)

        def canvas(lane, dtype):
            return pl.pallas_call(
                functools.partial(canvas_kernel, lane),
                grid_spec=pltpu.PrefetchScalarGridSpec(
                    num_scalar_prefetch=1,
                    grid=(1,),
                    in_specs=[vmem],
                    out_specs=vmem,
                    scratch_shapes=[
                        pltpu.VMEM((gt_dev, height + 2 * SUB + ROWS, width + LANES), jnp.float32),
                    ],
                ),
                out_shape=jax.ShapeDtypeStruct((gt_dev, height, width), dtype),
                compiler_params=pltpu.CompilerParams(vmem_limit_bytes=VMEM_BYTES),
                cost_estimate=pl.CostEstimate(
                    flops=GT * TS * width, bytes_accessed=8 * subs.size, transcendentals=0
                ),
                name="canvas",
            )(meta, subs)

        across = [(tile, (tile + 2) % tile_width) for tile in range(tile_width)]
        other = lax.ppermute(canvas(3 * BLK_DEV, jnp.bfloat16), "tile", across)
        return canvas(BLK_DEV, jnp.float32) + other.astype(jnp.float32)

    send, table, taper = pl.pallas_call(
        functools.partial(dispatch_kernel, slot_cap),
        out_shape=[
            jax.ShapeDtypeStruct((vis_count, features, chunk), jnp.bfloat16),
            jax.ShapeDtypeStruct((ROWS, LANES), jnp.float32),
            jax.ShapeDtypeStruct((SUB, SUB * POLC), jnp.float32),
        ],
        scratch_shapes=[
            pltpu.VMEM((features, rows), jnp.bfloat16),
            pltpu.VMEM((1, rows), jnp.int32),
        ],
        name="dispatch",
    )(
        vis_data,
        u_cell,
        v_cell,
        u_frac,
        v_frac,
        w_plane,
        block_route.reshape(1, rows),
        kernel_taps.T,
        taper_gain,
    )
    covered = min(BLK_DEV, LANES // slot_cap)
    work = [
        pltpu.VMEM((BLK_DEV * SUB, SUB * POLC), jnp.float32),
        pltpu.VMEM((covered * SUB, channels * LANES), jnp.bfloat16),
        pltpu.VMEM((SUB * POLC, channels * LANES), jnp.bfloat16),
    ]
    gridded = jax.ShapeDtypeStruct((BLK_DEV, SUB, SUB * POLC), jnp.bfloat16)
    moved = lax.all_to_all(send, "vis", split_axis=0, concat_axis=0, tiled=True)
    moved = jnp.transpose(moved, (1, 0, 2)).reshape(1, features, vis_count * chunk)
    subs = pl.pallas_call(
        functools.partial(grid_kernel, slot_cap, chunk, channels),
        grid=(moved.shape[2] // LANES,),
        in_specs=[
            pl.BlockSpec((1, features, LANES), lambda s: (0, 0, s)),
            pl.BlockSpec(table.shape, lambda s: (0, 0)),
            pl.BlockSpec(taper.shape, lambda s: (0, 0)),
        ],
        out_specs=pl.BlockSpec(gridded.shape, lambda s: (0, 0, 0)),
        out_shape=gridded,
        scratch_shapes=work,
        name="grid",
    )(moved, table, taper)
    scalars = pl.BlockSpec(memory_space=pltpu.SMEM)
    subs, meta = pl.pallas_call(
        slot_kernel,
        in_specs=[scalars, scalars, vmem],
        out_specs=[vmem, vmem],
        out_shape=[
            jax.ShapeDtypeStruct((slots, SUB, SUB * POLC), jnp.bfloat16),
            jax.ShapeDtypeStruct((1, LANES), jnp.int32),
        ],
        name="slot",
    )(sub_tile.reshape(1, BLK_DEV), sub_anchor.T, subs)
    hops = (vis_count - 1) * tile_width * 3
    subs, meta = pl.pallas_call(
        gather_kernel,
        in_specs=[vmem, vmem],
        out_specs=[vmem, vmem],
        out_shape=[
            jax.ShapeDtypeStruct(
                (vis_count, tile_width, per_owner, SUB, SUB * POLC), jnp.bfloat16
            ),
            jax.ShapeDtypeStruct((vis_count, tile_width, 1, LANES), jnp.int32),
        ],
        scratch_shapes=[
            pltpu.SemaphoreType.DMA((2,)),
            pltpu.SemaphoreType.DMA((2 * tile_width,)),
            pltpu.SemaphoreType.DMA((2 * tile_width,)),
            pltpu.SemaphoreType.DMA((hops,)),
            pltpu.SemaphoreType.DMA((hops,)),
        ],
        compiler_params=pltpu.CompilerParams(collective_id=0, has_side_effects=True),
        name="gather",
    )(subs.reshape(tile_width, per_owner, SUB, SUB * POLC), meta)
    subs = subs.reshape(vis_count, slots, SUB, SUB * POLC)
    meta = meta.reshape(vis_count * tile_width, LANES)
    return pl.pallas_call(
        functools.partial(place_kernel, per_owner),
        grid_spec=pltpu.PrefetchScalarGridSpec(
            num_scalar_prefetch=1,
            grid=(vis_count,),
            in_specs=[pl.BlockSpec((1, slots, SUB, SUB * POLC), lambda s, *_: (s, 0, 0, 0))],
            out_specs=pl.BlockSpec((gt_dev, height, width), lambda s, *_: (0, 0, 0)),
            scratch_shapes=[
                pltpu.VMEM((gt_dev, -(-height // ROWS) * ROWS + 2 * SUB + ROWS, width + LANES), jnp.float32),
            ],
        ),
        out_shape=jax.ShapeDtypeStruct((gt_dev, height, width), jnp.float32),
        name="place",
    )(meta, subs)


def solution(mesh):
    placed = (
        P(("vis", "tile"), None),
        P(None, ("vis", "tile")),
        P(None, ("vis", "tile")),
        P(None, ("vis", "tile")),
        P(None, ("vis", "tile")),
        P(None, ("vis", "tile")),
        P(("vis", "tile"), None),
        P(),
        P(),
        P(("vis", "tile"), None),
        P(("vis", "tile"), None),
    )
    return jax.shard_map(
        on_device, mesh=mesh, in_specs=placed, out_specs=P("tile", "vis", None), check_vma=False
    )
```

```python
import functools

import jax
import jax.numpy as jnp
from jax import lax
from jax.experimental import pallas as pl
from jax.experimental.pallas import tpu as pltpu
from jax.sharding import PartitionSpec as P

BLK_DEV = 8
SUB = 32
POLC = 8
TAPS = 7
OS = 16
TS = 256
GT = 8
SCAP = 2
LANES = 128
ROWS = 8
GROUP = 4
PIECES = 4
LUMPS = 4
VMEM_BYTES = 24 << 20
FAR = 1 << 20
FLAGS = 8
MESH = pl.DeviceIdType.MESH
NT = (((1,), (1,)), ((), ()))


def dispatch_kernel(
    slot_cap, vis, u_cell, v_cell, u_frac, v_frac, w_plane, route, taps, gain, out, table, taper, feat, dest
):
    rows = vis.shape[0]
    columns = vis.shape[1]
    channels = u_cell.shape[0]
    owners, _, chunk = out.shape
    groups = owners * BLK_DEV
    feat[pl.ds(0, columns), :] = vis[...].astype(jnp.float32).T.astype(jnp.bfloat16)
    plane = w_plane[...] * OS
    codes = (u_cell[...], v_cell[...], plane + u_frac[...], plane + v_frac[...])
    codes = jnp.concatenate(codes, axis=0).astype(jnp.float32).astype(jnp.bfloat16)
    feat[pl.ds(columns, 4 * channels), :] = codes
    names = route[...]
    mine = lax.broadcasted_iota(jnp.int32, (groups, rows), 0) == names
    onehot = jnp.where(mine, 1.0, 0.0)
    earlier = lax.broadcasted_iota(jnp.int32, (rows, rows), 0) < lax.broadcasted_iota(
        jnp.int32, (rows, rows), 1
    )
    before = jnp.dot(
        onehot.astype(jnp.bfloat16),
        jnp.where(earlier, 1.0, 0.0).astype(jnp.bfloat16),
        preferred_element_type=jnp.float32,
    )
    rank = jnp.sum(onehot * before, axis=0, keepdims=True).astype(jnp.int32)
    dest[...] = names * slot_cap + rank

    table[...] = jnp.zeros_like(table)
    table[pl.ds(0, TAPS), :] = taps[...].astype(jnp.bfloat16).astype(jnp.float32)
    cells = lax.broadcasted_iota(jnp.int32, (SUB, SUB * POLC), 0)
    repeat = cells == lax.broadcasted_iota(jnp.int32, (SUB, SUB * POLC), 1) // POLC
    taper[...] = jnp.dot(
        gain[...],
        jnp.where(repeat, 1.0, 0.0),
        precision=lax.Precision.HIGHEST,
        preferred_element_type=jnp.float32,
    )

    def send(owner, _):
        slots = lax.broadcasted_iota(jnp.int32, (chunk, rows), 0) + owner * chunk
        pick = jnp.where(slots == dest[...], 1.0, 0.0).astype(jnp.bfloat16)
        out[owner] = lax.dot_general(
            feat[...], pick, NT, preferred_element_type=jnp.float32
        ).astype(jnp.bfloat16)
        return 0

    lax.fori_loop(0, owners, send, 0)


def spread(cell, taps):
    rows = lax.broadcasted_iota(jnp.int32, taps.shape, 0) - cell
    parts = []
    for start in range(0, SUB, ROWS):
        delta = rows + start
        weight = jnp.take_along_axis(taps, delta & (ROWS - 1), axis=0)
        parts.append(jnp.where((delta >= 0) & (delta < ROWS), weight, 0.0))
    return jnp.concatenate(parts, axis=0)


def grid_chunk(slot_cap, chunk, channels, lane, feat, table, total, left, right):
    covered = min(BLK_DEV, LANES // slot_cap)
    first = lane % chunk // slot_cap
    columns = channels * POLC
    lanes = lax.broadcasted_iota(jnp.int32, (SUB, LANES), 1)
    block = (lane + lanes) % chunk // slot_cap - first
    samples = feat[:columns, :].astype(jnp.float32)
    codes = feat[columns:, :].astype(jnp.float32).astype(jnp.int32)
    lookup = table[...]
    part = jnp.zeros((covered * SUB, SUB * POLC), jnp.float32)
    for h in range(channels):
        sample = samples[h * POLC : (h + 1) * POLC, :]
        cell_u = codes[h : h + 1, :]
        cell_v = codes[channels + h : channels + h + 1, :]
        row_u = codes[2 * channels + h : 2 * channels + h + 1, :]
        row_v = codes[3 * channels + h : 3 * channels + h + 1, :]
        taps_u = jnp.take_along_axis(lookup, jnp.broadcast_to(row_u, (8, LANES)), axis=1)
        taps_v = jnp.take_along_axis(lookup, jnp.broadcast_to(row_v, (8, LANES)), axis=1)
        weight_u = spread(cell_u, taps_u)
        weight_v = spread(cell_v, taps_v)
        here = pl.ds(h * LANES, LANES)
        weighted = weight_u[:, None, :] * sample[None, :, :]
        right[:, here] = weighted.reshape(SUB * POLC, LANES).astype(jnp.bfloat16)
        for b in range(covered):
            left[pl.ds(b * SUB, SUB), here] = jnp.where(block == b, weight_v, 0.0).astype(
                jnp.bfloat16
            )
        if (h + 1) % GROUP == 0:
            group = pl.ds((h + 1 - GROUP) * LANES, GROUP * LANES)
            part = part + lax.dot_general(
                left[:, group], right[:, group], NT, preferred_element_type=jnp.float32
            )
    place = pl.ds(pl.multiple_of(first * SUB, SUB), covered * SUB)
    total[place, :] = total[place, :] + part


def grid_kernel(slot_cap, chunk, channels, feat, table, taper, out, total, left, right):
    step = pl.program_id(0)

    @pl.when(step == 0)
    def _():
        total[...] = jnp.zeros_like(total)

    grid_chunk(
        slot_cap, chunk, channels, step * LANES, feat[0], table, total, left, right
    )

    @pl.when(step == pl.num_programs(0) - 1)
    def _():
        for b in range(BLK_DEV):
            out[b] = (total[pl.ds(b * SUB, SUB), :] * taper[...]).astype(jnp.bfloat16)


def swap(first, second, width):
    low = lax.broadcasted_iota(jnp.int32, first.shape, 1) // width % 2 == 0
    return (
        jnp.where(low, first, pltpu.roll(second, width, 1)),
        jnp.where(low, pltpu.roll(first, LANES - width, 1), second),
    )


def regroup_lanes(parts):
    quarter = LANES // GROUP
    first, second = swap(parts[0], parts[1], quarter)
    third, fourth = swap(parts[2], parts[3], quarter)
    first, third = swap(first, third, 2 * quarter)
    second, fourth = swap(second, fourth, 2 * quarter)
    return first, second, third, fourth


def weights(cell, taps):
    delta = lax.broadcasted_iota(jnp.int32, taps.shape, 0) - cell
    turned = jnp.take_along_axis(taps, delta & (ROWS - 1), axis=0)
    octave = delta >> 3
    return [jnp.where(octave == -g, turned, 0.0) for g in range(SUB // ROWS)]


def grid_part(channels, features, table, left, right, spare):
    width = channels // GROUP
    columns = channels * POLC
    span = width * POLC
    samples = regroup_lanes([features[q * span : (q + 1) * span] for q in range(GROUP)])
    start = [columns + q * 4 * width for q in range(GROUP)]
    codes = regroup_lanes([features[at : at + 4 * width] for at in start])
    lookup = table[...]
    parts = []
    for b in range(GROUP):
        code = codes[b].astype(jnp.int32)
        for g in range(width):
            sample = samples[b][g * POLC : (g + 1) * POLC, :]
            cell_u, cell_v, row_u, row_v = [
                code[kind * width + g : kind * width + g + 1, :] for kind in range(4)
            ]
            taps_u = jnp.take_along_axis(lookup, jnp.broadcast_to(row_u, (8, LANES)), axis=1)
            taps_v = jnp.take_along_axis(lookup, jnp.broadcast_to(row_v, (8, LANES)), axis=1)
            here = pl.ds(g * LANES, LANES)
            for place, weight in enumerate(weights(cell_u, taps_u)):
                spare[g, pl.ds(place * ROWS, ROWS), :] = weight
            for u in range(0, SUB, 2):
                pair = [spare[g, pl.ds(u + i, POLC, stride=0), :] * sample for i in range(2)]
                right[b, pl.ds(u * POLC, 2 * POLC), here] = jnp.concatenate(pair, axis=0).astype(
                    jnp.bfloat16
                )
            left[b, :, here] = jnp.concatenate(weights(cell_v, taps_v), axis=0).astype(jnp.bfloat16)
        parts.append(
            lax.dot_general(left[b], right[b], NT, preferred_element_type=jnp.float32)
        )
    return parts


def rank_rows(slot_cap, groups, route, dest):
    rows = route.shape[1]
    earlier = lax.broadcasted_iota(jnp.int32, (LANES, LANES), 0) < lax.broadcasted_iota(
        jnp.int32, (LANES, LANES), 1
    )
    earlier = jnp.where(earlier, 1.0, 0.0).astype(jnp.bfloat16)
    seen = jnp.zeros((groups, 1), jnp.float32)
    for start in range(0, rows, LANES):
        names = route[:, pl.ds(start, LANES)]
        mine = lax.broadcasted_iota(jnp.int32, (groups, LANES), 0) == names
        onehot = jnp.where(mine, 1.0, 0.0)
        before = seen + jnp.dot(
            onehot.astype(jnp.bfloat16), earlier, preferred_element_type=jnp.float32
        )
        rank = jnp.sum(onehot * before, axis=0, keepdims=True).astype(jnp.int32)
        dest[:, pl.ds(start, LANES)] = names * slot_cap + rank
        seen = seen + jnp.sum(onehot, axis=1, keepdims=True)


def stack_features(vis, codes, feat):
    columns = vis.shape[1]
    feat[pl.ds(0, columns), :] = vis[...].astype(jnp.float32).T.astype(jnp.bfloat16)
    u_cell, v_cell, u_frac, v_frac, w_plane = codes
    channels = u_cell.shape[0]
    plane = w_plane[...] * OS
    codes = (u_cell[...], v_cell[...], plane + u_frac[...], plane + v_frac[...])
    codes = jnp.concatenate(codes, axis=0).astype(jnp.float32).astype(jnp.bfloat16)
    count = 4 * channels
    width = channels // GROUP
    to = lax.broadcasted_iota(jnp.int32, (count, count), 0)
    quarter, rest = to // (4 * width), to % (4 * width)
    source = rest // width * channels + quarter * width + rest % width
    turn = source == lax.broadcasted_iota(jnp.int32, (count, count), 1)
    feat[pl.ds(columns, count), :] = jnp.dot(
        jnp.where(turn, 1.0, 0.0).astype(jnp.bfloat16), codes, preferred_element_type=jnp.float32
    ).astype(jnp.bfloat16)


def placement(facts, height, v, t):
    tiles = GT // 4
    lanes = lax.broadcasted_iota(jnp.int32, facts.shape, 1) // BLK_DEV
    low = facts - v * height + SUB
    low = jnp.where((low > 0) & (low < height + SUB), low, 0)
    tile = pltpu.roll(facts, BLK_DEV, 1)
    placed = jnp.where(lanes == 0, facts % tiles, facts * POLC)
    placed = jnp.where(lanes == 1, jnp.where(tile // tiles == t, low, 0), placed)
    for g in range(tiles):
        across = jnp.where(tile == (t + 2) % 4 * tiles + g, low, 0)
        placed = jnp.where(lanes == 3 + g, pltpu.roll(across, (2 + g) * BLK_DEV, 1), placed)
    for kind in (1, *range(3, 3 + tiles)):
        some = jnp.max(jnp.where(lanes == kind, placed, 0), axis=1, keepdims=True)
        placed = jnp.where(lanes == FLAGS + kind, some, placed)
    return placed


def reduce_kernel(
    slot_cap,
    tile_rows,
    vis_hbm,
    u_cell_hbm,
    v_cell_hbm,
    u_frac_hbm,
    v_frac_hbm,
    w_plane_hbm,
    route_hbm,
    taps_hbm,
    gain_hbm,
    tiles_hbm,
    anchors_hbm,
    out,
    meta_out,
    vis,
    u_cell,
    v_cell,
    u_frac,
    v_frac,
    w_plane,
    route,
    taps,
    gain,
    tiles,
    anchors,
    table,
    taper,
    feat,
    dest,
    ordered,
    left,
    right,
    spare,
    partial,
    x_sent,
    x_landed,
    z_sent,
    z_landed,
    meta,
    in_sem,
    meta_send,
    meta_recv,
    x_send,
    x_recv,
    z_send,
    z_recv,
    to_z_send,
    to_z_recv,
    to_x_send,
    to_x_recv,
    to_core_send,
    to_core_recv,
    pass_send,
    pass_recv,
):
    count = out.shape[1]
    height = count // 2
    rows = vis.shape[0]
    channels = u_cell.shape[0]
    chunk = BLK_DEV * slot_cap
    v, t = lax.axis_index("vis"), lax.axis_index("tile")
    z, x = v // 2, v % 2
    c = t % 2
    beside = t + 1 - 2 * c
    each = BLK_DEV // PIECES
    remote = functools.partial(pltpu.make_async_remote_copy, device_id_type=MESH)

    pairs = (
        (vis_hbm, vis),
        (u_cell_hbm, u_cell),
        (v_cell_hbm, v_cell),
        (u_frac_hbm, u_frac),
        (v_frac_hbm, v_frac),
        (w_plane_hbm, w_plane),
        (route_hbm, route),
        (taps_hbm, taps),
        (gain_hbm, gain),
        (tiles_hbm, tiles),
        (anchors_hbm, anchors),
    )
    loads = [pltpu.make_async_copy(src, dst, in_sem.at[i]) for i, (src, dst) in enumerate(pairs)]
    loads = [loads[6]] + loads[:6] + loads[7:]
    for load in loads[:7]:
        load.start()
    barrier = pltpu.get_barrier_semaphore()
    for k in range(1, count):
        pl.semaphore_signal(barrier, inc=1, device_id=((v + k) % count, t), device_id_type=MESH)
    pl.semaphore_signal(barrier, inc=1, device_id=(v, beside), device_id_type=MESH)
    for load in loads[7:]:
        load.start()
    table[...] = jnp.zeros_like(table)

    loads[0].wait()
    rank_rows(slot_cap, count * BLK_DEV, route, dest)
    for load in loads[1:]:
        load.wait()
    stack_features(vis, (u_cell, v_cell, u_frac, v_frac, w_plane), feat)
    table[pl.ds(0, TAPS), :] = taps[...].astype(jnp.bfloat16).astype(jnp.float32)
    pl.semaphore_wait(barrier, count)

    def piece(i):
        return pl.ds(i * each, each)

    def lump(i):
        return pl.ds(i * (BLK_DEV // LUMPS), BLK_DEV // LUMPS)

    def tell(k):
        return remote(
            src_ref=meta,
            dst_ref=meta_out.at[c, v],
            send_sem=meta_send.at[k],
            recv_sem=meta_recv.at[k],
            device_id=((v + k) % count, t),
        )

    def add_x(j, i):
        return remote(
            src_ref=x_sent.at[j, piece(i)],
            dst_ref=x_landed.at[j, piece(i)],
            send_sem=x_send.at[j * PIECES + i],
            recv_sem=x_recv.at[j * PIECES + i],
            device_id=(z * 2 + 1 - x, t),
        )

    def add_z(j, i):
        return remote(
            src_ref=z_sent.at[j - 1, piece(i)],
            dst_ref=z_landed.at[j - 1, piece(i)],
            send_sem=z_send.at[(j - 1) * PIECES + i],
            recv_sem=z_recv.at[(j - 1) * PIECES + i],
            device_id=((z + j) % height * 2 + x, t),
        )

    def hand_z(source, side, i):
        ref = out.at[c, source * 2 + x, lump(i)]
        return remote(
            src_ref=ref,
            dst_ref=ref,
            send_sem=to_z_send.at[((1 + side) // 2 * height + source) * LUMPS + i],
            recv_sem=to_z_recv.at[source * LUMPS + i],
            device_id=((z + side) * 2 + x, t),
        )

    def give_x(j, i):
        ref = out.at[c, j * 2 + x, lump(i)]
        return remote(
            src_ref=ref,
            dst_ref=ref,
            send_sem=to_x_send.at[j * LUMPS + i],
            recv_sem=to_x_recv.at[j * LUMPS + i],
            device_id=(z * 2 + 1 - x, t),
        )

    def give_core(source, column):
        ref = out.at[c, source * 2 + column]
        return remote(
            src_ref=ref,
            dst_ref=ref,
            send_sem=to_core_send.at[source * 2 + column],
            recv_sem=to_core_recv.at[source * 2 + column],
            device_id=(v, beside),
        )

    def pass_meta():
        ref = meta_out.at[c]
        return remote(
            src_ref=ref,
            dst_ref=ref,
            send_sem=pass_send.at[0],
            recv_sem=pass_recv.at[0],
            device_id=(v, beside),
        )


    cells = lax.broadcasted_iota(jnp.int32, (chunk, rows), 0).astype(jnp.float32)
    cells = cells.astype(jnp.bfloat16)

    def plan(step):
        last = step == count - 1
        mine = jnp.logical_or(jnp.logical_and(step > 0, step % 2 == 0), last)
        j = jnp.where(last, 0, jnp.where(mine, step // 2, (step + 3) // 2 % height))
        return mine, j

    def sort(step, slot):
        mine, j = plan(step)
        owner = (z + j) % height * 2 + jnp.where(mine, x, 1 - x)
        slots = jnp.clip(dest[...] - owner * chunk, -1, chunk).astype(jnp.float32)
        pick = jnp.where(cells == slots.astype(jnp.bfloat16), 1.0, 0.0).astype(jnp.bfloat16)
        ordered[slot] = lax.dot_general(feat[...], pick, NT, preferred_element_type=jnp.float32)

    def grid_step(step, slot):
        mine, j = plan(step)
        sort(step + 1, 1 - slot)
        for d in range(chunk // LANES):
            features = ordered[slot, :, pl.ds(d * LANES, LANES)]
            grids = grid_part(channels, features, table, left, right, spare)
            for b, part in enumerate(grids):
                partial[d * GROUP + b] = part

        @pl.when(jnp.logical_not(mine))
        def _():
            for i in range(PIECES):
                x_sent[j, piece(i)] = partial[piece(i)].astype(jnp.bfloat16)
                add_x(j, i).start()

        @pl.when(mine)
        def _():
            for i in range(PIECES):
                add_x(j, i).wait_recv()
                partial[piece(i)] = partial[piece(i)] + x_landed[j, piece(i)].astype(jnp.float32)

                @pl.when(j > 0)
                def _():
                    z_sent[j - 1, piece(i)] = partial[piece(i)].astype(jnp.bfloat16)
                    add_z(j, i).start()

    def two_steps(half, _):
        grid_step(2 * half, 0)
        grid_step(2 * half + 1, 1)
        return 0

    sort(0, 0)
    lax.fori_loop(0, height, two_steps, 0)
    rest = jnp.zeros((1, LANES - 3 * BLK_DEV), jnp.int32)
    facts = [tiles[...], anchors[pl.ds(0, 1), :], anchors[pl.ds(1, 1), :], rest]
    meta[...] = jnp.concatenate(facts, axis=1)
    for k in range(1, count):
        tell(k).start()
    meta_out[c, v] = meta[...]
    cells = lax.broadcasted_iota(jnp.int32, (SUB, SUB * POLC), 0)
    repeat = cells == lax.broadcasted_iota(jnp.int32, (SUB, SUB * POLC), 1) // POLC
    taper[...] = jnp.dot(
        gain[...],
        jnp.where(repeat, 1.0, 0.0),
        precision=lax.Precision.HIGHEST,
        preferred_element_type=jnp.float32,
    )
    for i in range(PIECES):
        whole = partial[piece(i)]
        for j in range(1, height):
            add_z(j, i).wait_recv()
            whole = whole + z_landed[j - 1, piece(i)].astype(jnp.float32)
        out[c, v, piece(i)] = (whole * taper[...][None]).astype(jnp.bfloat16)
        if (i + 1) * LUMPS % PIECES:
            continue
        m = (i + 1) * LUMPS // PIECES - 1

        @pl.when(z > 0)
        def _():
            hand_z(z, -1, m).start()

        @pl.when(z < height - 1)
        def _():
            hand_z(z, 1, m).start()

        give_x(z, m).start()
    give_core(z, x).start()
    for k in range(1, count):
        tell(k).wait_recv()
    pass_meta().start()
    for gap in range(1, height):
        for i in range(LUMPS):
            for side in (1, -1):
                origin = z - side * gap

                @pl.when((origin >= 0) & (origin < height))
                def _():
                    hand_z(origin, side, i).wait_recv()

                    @pl.when((z + side >= 0) & (z + side < height))
                    def _():
                        hand_z(origin, side, i).start()

                    give_x(origin, i).start()
                    if i == LUMPS - 1:
                        give_core(origin, x).start()

    for gap in range(height):
        for side in (1, -1)[: 1 + min(gap, 1)]:
            origin = z - side * gap

            @pl.when((origin >= 0) & (origin < height))
            def _():
                for i in range(LUMPS):
                    give_x(origin, i).wait_recv()
                give_core(origin, 1 - x).start()

    for source in range(height):
        for column in range(2):
            give_core(source, column).wait()
    pass_meta().wait_recv()
    pass_meta().wait_send()
    for k in range(1, count):
        tell(k).wait_send()
    facts = meta_out[...].reshape(2 * count, LANES)
    meta_out[...] = placement(facts, tile_rows, v, t).reshape(2, count, 1, LANES)
    for i in range(PIECES):
        for j in range(height):
            add_x(j, i).wait_send()
        for j in range(1, height):
            add_z(j, i).wait_send()
    for i in range(LUMPS):
        for j in range(height):
            give_x(j, i).wait_send()

            @pl.when((j <= z) & (z < height - 1))
            def _():
                hand_z(j, 1, i).wait_send()

            @pl.when((j >= z) & (z > 0))
            def _():
                hand_z(j, -1, i).wait_send()


def canvas_kernel(lane, meta, subs, out, canvas):
    tiles, height, width = out.shape
    span = SUB * POLC
    canvas[:, pl.ds(SUB, height), :] = jnp.zeros((tiles, height, width + LANES), jnp.float32)

    def add_source(source, _):
        @pl.when(meta[source, FLAGS * BLK_DEV + lane] > 0)
        def _():
            add_blocks(source)

        return 0

    def add_blocks(source):
        for b in range(BLK_DEV):
            low = meta[source, lane + b]

            @pl.when(low > 0)
            def _():
                column = meta[source, 2 * BLK_DEV + b]
                sub = subs[source, b].astype(jnp.float32)
                sub = jnp.concatenate([sub, jnp.zeros((SUB, LANES), jnp.float32)], axis=1)
                sub = pltpu.roll(sub, column % LANES, 1)
                sub = jnp.concatenate([sub, jnp.zeros((ROWS, span + LANES), jnp.float32)], axis=0)
                sub = pltpu.roll(sub, low % ROWS, 0)
                top = pl.multiple_of(low // ROWS * ROWS, ROWS)
                base = pl.multiple_of(column // LANES * LANES, LANES)
                place = meta[source, b] if tiles > 1 else 0
                here = (place, pl.ds(top, SUB + ROWS), pl.ds(base, span + LANES))
                canvas[here] = canvas[here] + sub


    lax.fori_loop(0, subs.shape[0], add_source, 0)
    out[...] = canvas[:, pl.ds(SUB, height), pl.ds(0, width)].astype(out.dtype)


def slot_kernel(tiles, anchors, subs, out, meta):
    slots = out.shape[0]
    out[...] = jnp.zeros_like(out)
    lanes = lax.broadcasted_iota(jnp.int32, meta.shape, 1)
    places = jnp.full(meta.shape, -FAR, jnp.int32)
    for b in range(BLK_DEV):
        slot = tiles[0, b] * SCAP
        for before in range(b):
            slot = slot + jnp.where(tiles[0, before] == tiles[0, b], 1, 0)
        out[slot] = subs[b]
        places = jnp.where(lanes == slot, anchors[0, b], places)
        places = jnp.where(lanes == slots + slot, anchors[1, b], places)
    meta[...] = places


def gather_kernel(subs, meta, out, meta_out, own_sem, near_send, near_recv, far_send, far_recv):
    count = out.shape[0]
    width = out.shape[1]
    v, t = lax.axis_index("vis"), lax.axis_index("tile")
    half = count // 2
    spot = v // 2 * (1 - v % 2) + (count - 1 - v // 2) * (v % 2)

    def member(position):
        position = (position + 2 * count) % count
        back = position // half
        return (1 - back) * 2 * position + back * (2 * (count - 1 - position) + 1)

    barrier = pltpu.get_barrier_semaphore()
    for side in (1, -1):
        pl.semaphore_signal(
            barrier, inc=1, device_id=(member(spot + side), t), device_id_type=MESH
        )
    for k in range(1, width):
        pl.semaphore_signal(barrier, inc=1, device_id=(v, (t + k) % width), device_id_type=MESH)
    pl.semaphore_wait(barrier, 1 + width)

    def near(k):
        chunk = pl.ds((t + k) % width, 1)
        pairs = ((subs.at[chunk], out.at[v, pl.ds(t, 1)]), (meta, meta_out.at[v, t]))
        return [
            pltpu.make_async_remote_copy(
                src_ref=src,
                dst_ref=dst,
                send_sem=near_send.at[2 * k + i],
                recv_sem=near_recv.at[2 * k + i],
                device_id=(v, (t + k) % width),
                device_id_type=MESH,
            )
            for i, (src, dst) in enumerate(pairs)
        ]

    def own():
        pairs = ((subs.at[pl.ds(t, 1)], out.at[v, pl.ds(t, 1)]), (meta, meta_out.at[v, t]))
        return [
            pltpu.make_async_copy(src, dst, own_sem.at[i]) for i, (src, dst) in enumerate(pairs)
        ]

    def far(k, step):
        source = (t + width - k) % width
        cut = out.shape[2] // 2
        copies = []
        for i in range(3):
            side = 1 - 2 * (i % 2)
            origin = member(spot - side * step)
            if i < 2:
                ref = out.at[origin, source, pl.ds(i * cut, cut)]
            else:
                ref = meta_out.at[origin, source]
            copies.append(
                pltpu.make_async_remote_copy(
                    src_ref=ref,
                    dst_ref=ref,
                    send_sem=far_send.at[(step * width + k) * 3 + i],
                    recv_sem=far_recv.at[(step * width + k) * 3 + i],
                    device_id=(member(spot + side), t),
                    device_id_type=MESH,
                )
            )
        return copies

    for copy in own():
        copy.start()
    for k in range(1, width):
        for copy in near(k):
            copy.start()
    for copy in own():
        copy.wait()
    for k in range(width):
        if k:
            for copy in near(k):
                copy.wait_recv()
        for copy in far(k, 0):
            copy.start()

    def forward(step, _):
        for k in range(width):
            for landed, copy in zip(far(k, step - 1), far(k, step)):
                landed.wait_recv()
                copy.start()
        return 0

    lax.fori_loop(1, count - 1, forward, 0)
    for k in range(width):
        for copy in far(k, count - 2):
            copy.wait_recv()
    for k in range(1, width):
        for copy in near(k):
            copy.wait_send()

    def sent(step, _):
        for k in range(width):
            for copy in far(k, step):
                copy.wait_send()
        return 0

    lax.fori_loop(0, count - 1, sent, 0)


def place_kernel(tile_slots, meta, subs, out, canvas):
    v, t = lax.axis_index("vis"), lax.axis_index("tile")
    step = pl.program_id(0)
    slots = subs.shape[1]
    height = out.shape[1]
    width = out.shape[2]
    span = SUB * POLC

    @pl.when(step == 0)
    def _():
        canvas[...] = jnp.zeros_like(canvas)

    def add_source(near, _):
        source = step * (slots // tile_slots) + near
        for slot in range(tile_slots):
            lane = t * tile_slots + slot
            low = meta[source, lane] - v * height + SUB
            column = meta[source, slots + lane] * POLC

            @pl.when((low > 0) & (low < height + SUB))
            def _():
                sub = subs[0, near * tile_slots + slot].astype(jnp.float32)
                sub = jnp.concatenate([sub, jnp.zeros((SUB, LANES), jnp.float32)], axis=1)
                sub = pltpu.roll(sub, column % LANES, 1)
                sub = jnp.concatenate([sub, jnp.zeros((ROWS, span + LANES), jnp.float32)], axis=0)
                sub = pltpu.roll(sub, low % ROWS, 0)
                top = pl.multiple_of(low // ROWS * ROWS, ROWS)
                base = pl.multiple_of(column // LANES * LANES, LANES)
                here = (slot // SCAP, pl.ds(top, SUB + ROWS), pl.ds(base, span + LANES))
                canvas[here] = canvas[here] + sub

        return 0

    lax.fori_loop(0, slots // tile_slots, add_source, 0)

    @pl.when(step == pl.num_programs(0) - 1)
    def _():
        out[...] = canvas[:, pl.ds(SUB, height), pl.ds(0, width)]


def on_device(
    vis_data,
    u_cell,
    v_cell,
    u_frac,
    v_frac,
    w_plane,
    block_route,
    kernel_taps,
    taper_gain,
    sub_tile,
    sub_anchor,
):
    vis_count = lax.axis_size("vis")
    tile_width = lax.axis_size("tile")
    gt_dev = GT // tile_width
    rows, columns = vis_data.shape
    channels = u_cell.shape[0]
    slot_cap = max(2, 2 * rows // (BLK_DEV * vis_count))
    chunk = BLK_DEV * slot_cap
    grouped = (
        slot_cap * GROUP == LANES
        and channels % GROUP == 0
        and vis_count % 2 == 0
        and vis_count > 2
        and tile_width == 4
        and TS // vis_count % 32 == 0
    )
    features = columns + 4 * channels
    per_owner = gt_dev * SCAP
    slots = tile_width * per_owner
    height = TS // vis_count
    width = TS * POLC

    vmem = pl.BlockSpec(memory_space=pltpu.VMEM)
    if grouped:
        layers = vis_count // 2
        block = (SUB, SUB * POLC)
        lanes = channels // GROUP * LANES
        operands = (
            vis_data,
            u_cell,
            v_cell,
            u_frac,
            v_frac,
            w_plane,
            block_route.reshape(1, rows),
            kernel_taps.T,
            taper_gain,
            sub_tile.reshape(1, BLK_DEV),
            sub_anchor.T,
        )
        subs, meta = pl.pallas_call(
            functools.partial(reduce_kernel, slot_cap, height),
            in_specs=[pl.BlockSpec(memory_space=pltpu.HBM)] * len(operands),
            out_specs=[vmem] * 2,
            out_shape=[
                jax.ShapeDtypeStruct((2, vis_count, BLK_DEV) + block, jnp.bfloat16),
                jax.ShapeDtypeStruct((2, vis_count, 1, LANES), jnp.int32),
            ],
            scratch_shapes=[pltpu.VMEM(operand.shape, operand.dtype) for operand in operands]
            + [
                pltpu.VMEM((ROWS, LANES), jnp.float32),
                pltpu.VMEM(block, jnp.float32),
                pltpu.VMEM((features, rows), jnp.bfloat16),
                pltpu.VMEM((1, rows), jnp.int32),
                pltpu.VMEM((2, features, chunk), jnp.float32),
                pltpu.VMEM((GROUP, SUB, lanes), jnp.bfloat16),
                pltpu.VMEM((GROUP, SUB * POLC, lanes), jnp.bfloat16),
                pltpu.VMEM((channels // GROUP, SUB, LANES), jnp.float32),
                pltpu.VMEM((BLK_DEV,) + block, jnp.float32),
                pltpu.VMEM((layers, BLK_DEV) + block, jnp.bfloat16),
                pltpu.VMEM((layers, BLK_DEV) + block, jnp.bfloat16),
                pltpu.VMEM((layers - 1, BLK_DEV) + block, jnp.bfloat16),
                pltpu.VMEM((layers - 1, BLK_DEV) + block, jnp.bfloat16),
                pltpu.VMEM((1, LANES), jnp.int32),
                pltpu.SemaphoreType.DMA((len(operands),)),
            ]
            + [
                pltpu.SemaphoreType.DMA((lots,))
                for lots in [vis_count] * 2
                + [layers * PIECES] * 2
                + [(layers - 1) * PIECES] * 2
                + [2 * layers * LUMPS]
                + [layers * LUMPS] * 3
                + [vis_count] * 2
                + [1] * 2
            ],
            compiler_params=pltpu.CompilerParams(
                collective_id=1, has_side_effects=True, vmem_limit_bytes=VMEM_BYTES
            ),
            name="reduce",
        )(*[pltpu.with_memory_space_constraint(operand, pltpu.HBM) for operand in operands])
        meta = meta.reshape(2 * vis_count, LANES)
        subs = subs.reshape((2 * vis_count, BLK_DEV) + block)

        def canvas(lane, tiles, dtype):
            return pl.pallas_call(
                functools.partial(canvas_kernel, lane),
                grid_spec=pltpu.PrefetchScalarGridSpec(
                    num_scalar_prefetch=1,
                    grid=(1,),
                    in_specs=[vmem],
                    out_specs=vmem,
                    scratch_shapes=[
                        pltpu.VMEM((tiles, height + 2 * SUB + ROWS, width + LANES), jnp.float32),
                    ],
                ),
                out_shape=jax.ShapeDtypeStruct((tiles, height, width), dtype),
                compiler_params=pltpu.CompilerParams(vmem_limit_bytes=VMEM_BYTES),
                cost_estimate=pl.CostEstimate(
                    flops=GT * TS * width, bytes_accessed=8 * subs.size, transcendentals=0
                ),
                name="canvas",
            )(meta, subs)

        across = [(tile, (tile + 2) % tile_width) for tile in range(tile_width)]
        others = [
            lax.ppermute(canvas((3 + g) * BLK_DEV, 1, jnp.bfloat16), "tile", across)
            for g in range(gt_dev)
        ]
        own = canvas(BLK_DEV, gt_dev, jnp.float32)
        return own + jnp.concatenate(others, axis=0).astype(jnp.float32)

    send, table, taper = pl.pallas_call(
        functools.partial(dispatch_kernel, slot_cap),
        out_shape=[
            jax.ShapeDtypeStruct((vis_count, features, chunk), jnp.bfloat16),
            jax.ShapeDtypeStruct((ROWS, LANES), jnp.float32),
            jax.ShapeDtypeStruct((SUB, SUB * POLC), jnp.float32),
        ],
        scratch_shapes=[
            pltpu.VMEM((features, rows), jnp.bfloat16),
            pltpu.VMEM((1, rows), jnp.int32),
        ],
        name="dispatch",
    )(
        vis_data,
        u_cell,
        v_cell,
        u_frac,
        v_frac,
        w_plane,
        block_route.reshape(1, rows),
        kernel_taps.T,
        taper_gain,
    )
    covered = min(BLK_DEV, LANES // slot_cap)
    work = [
        pltpu.VMEM((BLK_DEV * SUB, SUB * POLC), jnp.float32),
        pltpu.VMEM((covered * SUB, channels * LANES), jnp.bfloat16),
        pltpu.VMEM((SUB * POLC, channels * LANES), jnp.bfloat16),
    ]
    gridded = jax.ShapeDtypeStruct((BLK_DEV, SUB, SUB * POLC), jnp.bfloat16)
    moved = lax.all_to_all(send, "vis", split_axis=0, concat_axis=0, tiled=True)
    moved = jnp.transpose(moved, (1, 0, 2)).reshape(1, features, vis_count * chunk)
    subs = pl.pallas_call(
        functools.partial(grid_kernel, slot_cap, chunk, channels),
        grid=(moved.shape[2] // LANES,),
        in_specs=[
            pl.BlockSpec((1, features, LANES), lambda s: (0, 0, s)),
            pl.BlockSpec(table.shape, lambda s: (0, 0)),
            pl.BlockSpec(taper.shape, lambda s: (0, 0)),
        ],
        out_specs=pl.BlockSpec(gridded.shape, lambda s: (0, 0, 0)),
        out_shape=gridded,
        scratch_shapes=work,
        name="grid",
    )(moved, table, taper)
    scalars = pl.BlockSpec(memory_space=pltpu.SMEM)
    subs, meta = pl.pallas_call(
        slot_kernel,
        in_specs=[scalars, scalars, vmem],
        out_specs=[vmem, vmem],
        out_shape=[
            jax.ShapeDtypeStruct((slots, SUB, SUB * POLC), jnp.bfloat16),
            jax.ShapeDtypeStruct((1, LANES), jnp.int32),
        ],
        name="slot",
    )(sub_tile.reshape(1, BLK_DEV), sub_anchor.T, subs)
    hops = (vis_count - 1) * tile_width * 3
    subs, meta = pl.pallas_call(
        gather_kernel,
        in_specs=[vmem, vmem],
        out_specs=[vmem, vmem],
        out_shape=[
            jax.ShapeDtypeStruct(
                (vis_count, tile_width, per_owner, SUB, SUB * POLC), jnp.bfloat16
            ),
            jax.ShapeDtypeStruct((vis_count, tile_width, 1, LANES), jnp.int32),
        ],
        scratch_shapes=[
            pltpu.SemaphoreType.DMA((2,)),
            pltpu.SemaphoreType.DMA((2 * tile_width,)),
            pltpu.SemaphoreType.DMA((2 * tile_width,)),
            pltpu.SemaphoreType.DMA((hops,)),
            pltpu.SemaphoreType.DMA((hops,)),
        ],
        compiler_params=pltpu.CompilerParams(collective_id=0, has_side_effects=True),
        name="gather",
    )(subs.reshape(tile_width, per_owner, SUB, SUB * POLC), meta)
    subs = subs.reshape(vis_count, slots, SUB, SUB * POLC)
    meta = meta.reshape(vis_count * tile_width, LANES)
    return pl.pallas_call(
        functools.partial(place_kernel, per_owner),
        grid_spec=pltpu.PrefetchScalarGridSpec(
            num_scalar_prefetch=1,
            grid=(vis_count,),
            in_specs=[pl.BlockSpec((1, slots, SUB, SUB * POLC), lambda s, *_: (s, 0, 0, 0))],
            out_specs=pl.BlockSpec((gt_dev, height, width), lambda s, *_: (0, 0, 0)),
            scratch_shapes=[
                pltpu.VMEM((gt_dev, -(-height // ROWS) * ROWS + 2 * SUB + ROWS, width + LANES), jnp.float32),
            ],
        ),
        out_shape=jax.ShapeDtypeStruct((gt_dev, height, width), jnp.float32),
        name="place",
    )(meta, subs)


def solution(mesh):
    placed = (
        P(("vis", "tile"), None),
        P(None, ("vis", "tile")),
        P(None, ("vis", "tile")),
        P(None, ("vis", "tile")),
        P(None, ("vis", "tile")),
        P(None, ("vis", "tile")),
        P(("vis", "tile"), None),
        P(),
        P(),
        P(("vis", "tile"), None),
        P(("vis", "tile"), None),
    )
    return jax.shard_map(
        on_device, mesh=mesh, in_specs=placed, out_specs=P("tile", "vis", None), check_vma=False
    )
```

```python
import functools

import jax
import jax.numpy as jnp
from jax import lax
from jax.experimental import pallas as pl
from jax.experimental.pallas import tpu as pltpu
from jax.sharding import PartitionSpec as P

BLK_DEV = 8
SUB = 32
POLC = 8
TAPS = 7
OS = 16
TS = 256
GT = 8
SCAP = 2
LANES = 128
ROWS = 8
GROUP = 4
PIECES = 4
LUMPS = 4
VMEM_BYTES = 24 << 20
FAR = 1 << 20
FLAGS = 8
MESH = pl.DeviceIdType.MESH
NT = (((1,), (1,)), ((), ()))


def dispatch_kernel(
    slot_cap, vis, u_cell, v_cell, u_frac, v_frac, w_plane, route, taps, gain, out, table, taper, feat, dest
):
    rows = vis.shape[0]
    columns = vis.shape[1]
    channels = u_cell.shape[0]
    owners, _, chunk = out.shape
    groups = owners * BLK_DEV
    feat[pl.ds(0, columns), :] = vis[...].astype(jnp.float32).T.astype(jnp.bfloat16)
    plane = w_plane[...] * OS
    codes = (u_cell[...], v_cell[...], plane + u_frac[...], plane + v_frac[...])
    codes = jnp.concatenate(codes, axis=0).astype(jnp.float32).astype(jnp.bfloat16)
    feat[pl.ds(columns, 4 * channels), :] = codes
    names = route[...]
    mine = lax.broadcasted_iota(jnp.int32, (groups, rows), 0) == names
    onehot = jnp.where(mine, 1.0, 0.0)
    earlier = lax.broadcasted_iota(jnp.int32, (rows, rows), 0) < lax.broadcasted_iota(
        jnp.int32, (rows, rows), 1
    )
    before = jnp.dot(
        onehot.astype(jnp.bfloat16),
        jnp.where(earlier, 1.0, 0.0).astype(jnp.bfloat16),
        preferred_element_type=jnp.float32,
    )
    rank = jnp.sum(onehot * before, axis=0, keepdims=True).astype(jnp.int32)
    dest[...] = names * slot_cap + rank

    table[...] = jnp.zeros_like(table)
    table[pl.ds(0, TAPS), :] = taps[...].astype(jnp.bfloat16).astype(jnp.float32)
    cells = lax.broadcasted_iota(jnp.int32, (SUB, SUB * POLC), 0)
    repeat = cells == lax.broadcasted_iota(jnp.int32, (SUB, SUB * POLC), 1) // POLC
    taper[...] = jnp.dot(
        gain[...],
        jnp.where(repeat, 1.0, 0.0),
        precision=lax.Precision.HIGHEST,
        preferred_element_type=jnp.float32,
    )

    def send(owner, _):
        slots = lax.broadcasted_iota(jnp.int32, (chunk, rows), 0) + owner * chunk
        pick = jnp.where(slots == dest[...], 1.0, 0.0).astype(jnp.bfloat16)
        out[owner] = lax.dot_general(
            feat[...], pick, NT, preferred_element_type=jnp.float32
        ).astype(jnp.bfloat16)
        return 0

    lax.fori_loop(0, owners, send, 0)


def spread(cell, taps):
    rows = lax.broadcasted_iota(jnp.int32, taps.shape, 0) - cell
    parts = []
    for start in range(0, SUB, ROWS):
        delta = rows + start
        weight = jnp.take_along_axis(taps, delta & (ROWS - 1), axis=0)
        parts.append(jnp.where((delta >= 0) & (delta < ROWS), weight, 0.0))
    return jnp.concatenate(parts, axis=0)


def grid_chunk(slot_cap, chunk, channels, lane, feat, table, total, left, right):
    covered = min(BLK_DEV, LANES // slot_cap)
    first = lane % chunk // slot_cap
    columns = channels * POLC
    lanes = lax.broadcasted_iota(jnp.int32, (SUB, LANES), 1)
    block = (lane + lanes) % chunk // slot_cap - first
    samples = feat[:columns, :].astype(jnp.float32)
    codes = feat[columns:, :].astype(jnp.float32).astype(jnp.int32)
    lookup = table[...]
    part = jnp.zeros((covered * SUB, SUB * POLC), jnp.float32)
    for h in range(channels):
        sample = samples[h * POLC : (h + 1) * POLC, :]
        cell_u = codes[h : h + 1, :]
        cell_v = codes[channels + h : channels + h + 1, :]
        row_u = codes[2 * channels + h : 2 * channels + h + 1, :]
        row_v = codes[3 * channels + h : 3 * channels + h + 1, :]
        taps_u = jnp.take_along_axis(lookup, jnp.broadcast_to(row_u, (8, LANES)), axis=1)
        taps_v = jnp.take_along_axis(lookup, jnp.broadcast_to(row_v, (8, LANES)), axis=1)
        weight_u = spread(cell_u, taps_u)
        weight_v = spread(cell_v, taps_v)
        here = pl.ds(h * LANES, LANES)
        weighted = weight_u[:, None, :] * sample[None, :, :]
        right[:, here] = weighted.reshape(SUB * POLC, LANES).astype(jnp.bfloat16)
        for b in range(covered):
            left[pl.ds(b * SUB, SUB), here] = jnp.where(block == b, weight_v, 0.0).astype(
                jnp.bfloat16
            )
        if (h + 1) % GROUP == 0:
            group = pl.ds((h + 1 - GROUP) * LANES, GROUP * LANES)
            part = part + lax.dot_general(
                left[:, group], right[:, group], NT, preferred_element_type=jnp.float32
            )
    place = pl.ds(pl.multiple_of(first * SUB, SUB), covered * SUB)
    total[place, :] = total[place, :] + part


def grid_kernel(slot_cap, chunk, channels, feat, table, taper, out, total, left, right):
    step = pl.program_id(0)

    @pl.when(step == 0)
    def _():
        total[...] = jnp.zeros_like(total)

    grid_chunk(
        slot_cap, chunk, channels, step * LANES, feat[0], table, total, left, right
    )

    @pl.when(step == pl.num_programs(0) - 1)
    def _():
        for b in range(BLK_DEV):
            out[b] = (total[pl.ds(b * SUB, SUB), :] * taper[...]).astype(jnp.bfloat16)


def swap(first, second, width):
    low = lax.broadcasted_iota(jnp.int32, first.shape, 1) // width % 2 == 0
    return (
        jnp.where(low, first, pltpu.roll(second, width, 1)),
        jnp.where(low, pltpu.roll(first, LANES - width, 1), second),
    )


def regroup_lanes(parts):
    quarter = LANES // GROUP
    first, second = swap(parts[0], parts[1], quarter)
    third, fourth = swap(parts[2], parts[3], quarter)
    first, third = swap(first, third, 2 * quarter)
    second, fourth = swap(second, fourth, 2 * quarter)
    return first, second, third, fourth


def weights(cell, taps):
    delta = lax.broadcasted_iota(jnp.int32, taps.shape, 0) - cell
    turned = jnp.take_along_axis(taps, delta & (ROWS - 1), axis=0)
    octave = delta >> 3
    return [jnp.where(octave == -g, turned, 0.0) for g in range(SUB // ROWS)]


def grid_part(channels, features, table, left, right, spare):
    width = channels // GROUP
    columns = channels * POLC
    span = width * POLC
    samples = regroup_lanes([features[q * span : (q + 1) * span] for q in range(GROUP)])
    start = [columns + q * 4 * width for q in range(GROUP)]
    codes = regroup_lanes([features[at : at + 4 * width] for at in start])
    lookup = table[...]
    parts = []
    for b in range(GROUP):
        code = codes[b].astype(jnp.int32)
        for g in range(width):
            sample = samples[b][g * POLC : (g + 1) * POLC, :]
            cell_u, cell_v, row_u, row_v = [
                code[kind * width + g : kind * width + g + 1, :] for kind in range(4)
            ]
            taps_u = jnp.take_along_axis(lookup, jnp.broadcast_to(row_u, (8, LANES)), axis=1)
            taps_v = jnp.take_along_axis(lookup, jnp.broadcast_to(row_v, (8, LANES)), axis=1)
            here = pl.ds(g * LANES, LANES)
            for place, weight in enumerate(weights(cell_u, taps_u)):
                spare[g, pl.ds(place * ROWS, ROWS), :] = weight
            for u in range(0, SUB, 2):
                pair = [spare[g, pl.ds(u + i, POLC, stride=0), :] * sample for i in range(2)]
                right[b, pl.ds(u * POLC, 2 * POLC), here] = jnp.concatenate(pair, axis=0).astype(
                    jnp.bfloat16
                )
            left[b, :, here] = jnp.concatenate(weights(cell_v, taps_v), axis=0).astype(jnp.bfloat16)
        parts.append(
            lax.dot_general(left[b], right[b], NT, preferred_element_type=jnp.float32)
        )
    return parts


def rank_rows(slot_cap, groups, route, dest):
    rows = route.shape[1]
    earlier = lax.broadcasted_iota(jnp.int32, (LANES, LANES), 0) < lax.broadcasted_iota(
        jnp.int32, (LANES, LANES), 1
    )
    earlier = jnp.where(earlier, 1.0, 0.0).astype(jnp.bfloat16)
    seen = jnp.zeros((groups, 1), jnp.float32)
    for start in range(0, rows, LANES):
        names = route[:, pl.ds(start, LANES)]
        mine = lax.broadcasted_iota(jnp.int32, (groups, LANES), 0) == names
        onehot = jnp.where(mine, 1.0, 0.0)
        before = seen + jnp.dot(
            onehot.astype(jnp.bfloat16), earlier, preferred_element_type=jnp.float32
        )
        rank = jnp.sum(onehot * before, axis=0, keepdims=True).astype(jnp.int32)
        dest[:, pl.ds(start, LANES)] = names * slot_cap + rank
        seen = seen + jnp.sum(onehot, axis=1, keepdims=True)


def stack_features(vis, codes, feat):
    columns = vis.shape[1]
    feat[pl.ds(0, columns), :] = vis[...].astype(jnp.float32).T.astype(jnp.bfloat16)
    u_cell, v_cell, u_frac, v_frac, w_plane = codes
    channels = u_cell.shape[0]
    plane = w_plane[...] * OS
    codes = (u_cell[...], v_cell[...], plane + u_frac[...], plane + v_frac[...])
    codes = jnp.concatenate(codes, axis=0).astype(jnp.float32).astype(jnp.bfloat16)
    count = 4 * channels
    width = channels // GROUP
    to = lax.broadcasted_iota(jnp.int32, (count, count), 0)
    quarter, rest = to // (4 * width), to % (4 * width)
    source = rest // width * channels + quarter * width + rest % width
    turn = source == lax.broadcasted_iota(jnp.int32, (count, count), 1)
    feat[pl.ds(columns, count), :] = jnp.dot(
        jnp.where(turn, 1.0, 0.0).astype(jnp.bfloat16), codes, preferred_element_type=jnp.float32
    ).astype(jnp.bfloat16)


def placement(facts, height, v, t):
    tiles = GT // 4
    lanes = lax.broadcasted_iota(jnp.int32, facts.shape, 1) // BLK_DEV
    low = facts - v * height + SUB
    low = jnp.where((low > 0) & (low < height + SUB), low, 0)
    tile = pltpu.roll(facts, BLK_DEV, 1)
    placed = jnp.where(lanes == 0, facts % tiles, facts * POLC)
    placed = jnp.where(lanes == 1, jnp.where(tile // tiles == t, low, 0), placed)
    for g in range(tiles):
        across = jnp.where(tile == (t + 2) % 4 * tiles + g, low, 0)
        placed = jnp.where(lanes == 3 + g, pltpu.roll(across, (2 + g) * BLK_DEV, 1), placed)
    for kind in (1, *range(3, 3 + tiles)):
        some = jnp.max(jnp.where(lanes == kind, placed, 0), axis=1, keepdims=True)
        placed = jnp.where(lanes == FLAGS + kind, some, placed)
    return placed


def reduce_kernel(
    slot_cap,
    tile_rows,
    vis_hbm,
    u_cell_hbm,
    v_cell_hbm,
    u_frac_hbm,
    v_frac_hbm,
    w_plane_hbm,
    route_hbm,
    taps_hbm,
    gain_hbm,
    tiles_hbm,
    anchors_hbm,
    out,
    meta_out,
    vis,
    u_cell,
    v_cell,
    u_frac,
    v_frac,
    w_plane,
    route,
    taps,
    gain,
    tiles,
    anchors,
    table,
    taper,
    feat,
    dest,
    ordered,
    left,
    right,
    spare,
    partial,
    x_sent,
    x_landed,
    z_sent,
    z_landed,
    meta,
    in_sem,
    meta_send,
    meta_recv,
    x_send,
    x_recv,
    z_send,
    z_recv,
    to_z_send,
    to_z_recv,
    to_x_send,
    to_x_recv,
    to_core_send,
    to_core_recv,
    pass_send,
    pass_recv,
):
    count = out.shape[1]
    height = count // 2
    rows = vis.shape[0]
    channels = u_cell.shape[0]
    chunk = BLK_DEV * slot_cap
    v, t = lax.axis_index("vis"), lax.axis_index("tile")
    z, x = v // 2, v % 2
    c = t % 2
    beside = t + 1 - 2 * c
    each = BLK_DEV // PIECES
    remote = functools.partial(pltpu.make_async_remote_copy, device_id_type=MESH)

    pairs = (
        (vis_hbm, vis),
        (u_cell_hbm, u_cell),
        (v_cell_hbm, v_cell),
        (u_frac_hbm, u_frac),
        (v_frac_hbm, v_frac),
        (w_plane_hbm, w_plane),
        (route_hbm, route),
        (taps_hbm, taps),
        (gain_hbm, gain),
        (tiles_hbm, tiles),
        (anchors_hbm, anchors),
    )
    loads = [pltpu.make_async_copy(src, dst, in_sem.at[i]) for i, (src, dst) in enumerate(pairs)]
    loads = [loads[6]] + loads[:6] + loads[7:]
    for load in loads[:7]:
        load.start()
    barrier = pltpu.get_barrier_semaphore()
    for k in range(1, count):
        pl.semaphore_signal(barrier, inc=1, device_id=((v + k) % count, t), device_id_type=MESH)
    pl.semaphore_signal(barrier, inc=1, device_id=(v, beside), device_id_type=MESH)
    for load in loads[7:]:
        load.start()
    table[...] = jnp.zeros_like(table)

    loads[0].wait()
    rank_rows(slot_cap, count * BLK_DEV, route, dest)
    for load in loads[1:]:
        load.wait()
    stack_features(vis, (u_cell, v_cell, u_frac, v_frac, w_plane), feat)
    table[pl.ds(0, TAPS), :] = taps[...].astype(jnp.bfloat16).astype(jnp.float32)
    pl.semaphore_wait(barrier, count)

    def piece(i):
        return pl.ds(i * each, each)

    def lump(i):
        return pl.ds(i * (BLK_DEV // LUMPS), BLK_DEV // LUMPS)

    def tell(k):
        return remote(
            src_ref=meta,
            dst_ref=meta_out.at[c, v],
            send_sem=meta_send.at[k],
            recv_sem=meta_recv.at[k],
            device_id=((v + k) % count, t),
        )

    def add_x(j, i):
        return remote(
            src_ref=x_sent.at[j, piece(i)],
            dst_ref=x_landed.at[j, piece(i)],
            send_sem=x_send.at[j * PIECES + i],
            recv_sem=x_recv.at[j * PIECES + i],
            device_id=(z * 2 + 1 - x, t),
        )

    def add_z(j, i):
        return remote(
            src_ref=z_sent.at[j - 1, piece(i)],
            dst_ref=z_landed.at[j - 1, piece(i)],
            send_sem=z_send.at[(j - 1) * PIECES + i],
            recv_sem=z_recv.at[(j - 1) * PIECES + i],
            device_id=((z + j) % height * 2 + x, t),
        )

    def hand_z(source, side, i):
        ref = out.at[c, source * 2 + x, lump(i)]
        return remote(
            src_ref=ref,
            dst_ref=ref,
            send_sem=to_z_send.at[((1 + side) // 2 * height + source) * LUMPS + i],
            recv_sem=to_z_recv.at[source * LUMPS + i],
            device_id=((z + side) * 2 + x, t),
        )

    def give_x(j, i):
        ref = out.at[c, j * 2 + x, lump(i)]
        return remote(
            src_ref=ref,
            dst_ref=ref,
            send_sem=to_x_send.at[j * LUMPS + i],
            recv_sem=to_x_recv.at[j * LUMPS + i],
            device_id=(z * 2 + 1 - x, t),
        )

    def give_core(source, column):
        ref = out.at[c, source * 2 + column]
        return remote(
            src_ref=ref,
            dst_ref=ref,
            send_sem=to_core_send.at[source * 2 + column],
            recv_sem=to_core_recv.at[source * 2 + column],
            device_id=(v, beside),
        )

    def pass_meta():
        ref = meta_out.at[c]
        return remote(
            src_ref=ref,
            dst_ref=ref,
            send_sem=pass_send.at[0],
            recv_sem=pass_recv.at[0],
            device_id=(v, beside),
        )


    cells = lax.broadcasted_iota(jnp.int32, (chunk, rows), 0).astype(jnp.float32)
    cells = cells.astype(jnp.bfloat16)

    def plan(step):
        last = step == count - 1
        mine = jnp.logical_or(jnp.logical_and(step > 0, step % 2 == 0), last)
        j = jnp.where(last, 0, jnp.where(mine, step // 2, (step + 3) // 2 % height))
        return mine, j

    def sort(step, slot):
        mine, j = plan(step)
        owner = (z + j) % height * 2 + jnp.where(mine, x, 1 - x)
        slots = jnp.clip(dest[...] - owner * chunk, -1, chunk).astype(jnp.float32)
        pick = jnp.where(cells == slots.astype(jnp.bfloat16), 1.0, 0.0).astype(jnp.bfloat16)
        ordered[slot] = lax.dot_general(feat[...], pick, NT, preferred_element_type=jnp.float32)

    def grid_step(step, slot):
        mine, j = plan(step)
        sort(step + 1, 1 - slot)
        for d in range(chunk // LANES):
            features = ordered[slot, :, pl.ds(d * LANES, LANES)]
            grids = grid_part(channels, features, table, left, right, spare)
            for b, part in enumerate(grids):
                partial[d * GROUP + b] = part

        @pl.when(jnp.logical_not(mine))
        def _():
            for i in range(PIECES):
                x_sent[j, piece(i)] = partial[piece(i)].astype(jnp.bfloat16)
                add_x(j, i).start()

        @pl.when(mine)
        def _():
            for i in range(PIECES):
                add_x(j, i).wait_recv()
                partial[piece(i)] = partial[piece(i)] + x_landed[j, piece(i)].astype(jnp.float32)

                @pl.when(j > 0)
                def _():
                    z_sent[j - 1, piece(i)] = partial[piece(i)].astype(jnp.bfloat16)
                    add_z(j, i).start()

    def two_steps(half, _):
        grid_step(2 * half, 0)
        grid_step(2 * half + 1, 1)
        return 0

    sort(0, 0)
    lax.fori_loop(0, height, two_steps, 0)
    rest = jnp.zeros((1, LANES - 3 * BLK_DEV), jnp.int32)
    facts = [tiles[...], anchors[pl.ds(0, 1), :], anchors[pl.ds(1, 1), :], rest]
    meta[...] = jnp.concatenate(facts, axis=1)
    for k in range(1, count):
        tell(k).start()
    meta_out[c, v] = meta[...]
    cells = lax.broadcasted_iota(jnp.int32, (SUB, SUB * POLC), 0)
    repeat = cells == lax.broadcasted_iota(jnp.int32, (SUB, SUB * POLC), 1) // POLC
    taper[...] = jnp.dot(
        gain[...],
        jnp.where(repeat, 1.0, 0.0),
        precision=lax.Precision.HIGHEST,
        preferred_element_type=jnp.float32,
    )
    for i in range(PIECES):
        whole = partial[piece(i)]
        for j in range(1, height):
            add_z(j, i).wait_recv()
            whole = whole + z_landed[j - 1, piece(i)].astype(jnp.float32)
        out[c, v, piece(i)] = (whole * taper[...][None]).astype(jnp.bfloat16)
        if (i + 1) * LUMPS % PIECES:
            continue
        m = (i + 1) * LUMPS // PIECES - 1

        @pl.when(z > 0)
        def _():
            hand_z(z, -1, m).start()

        @pl.when(z < height - 1)
        def _():
            hand_z(z, 1, m).start()

        give_x(z, m).start()
    give_core(z, x).start()
    for k in range(1, count):
        tell(k).wait_recv()
    pass_meta().start()
    for gap in range(1, height):
        for i in range(LUMPS):
            for side in (1, -1):
                origin = z - side * gap

                @pl.when((origin >= 0) & (origin < height))
                def _():
                    hand_z(origin, side, i).wait_recv()

                    @pl.when((z + side >= 0) & (z + side < height))
                    def _():
                        hand_z(origin, side, i).start()

                    give_x(origin, i).start()
                    if i == LUMPS - 1:
                        give_core(origin, x).start()

    for gap in range(height):
        for side in (1, -1)[: 1 + min(gap, 1)]:
            origin = z - side * gap

            @pl.when((origin >= 0) & (origin < height))
            def _():
                for i in range(LUMPS):
                    give_x(origin, i).wait_recv()
                give_core(origin, 1 - x).start()

    for source in range(height):
        for column in range(2):
            give_core(source, column).wait()
    pass_meta().wait_recv()
    pass_meta().wait_send()
    for k in range(1, count):
        tell(k).wait_send()
    facts = meta_out[...].reshape(2 * count, LANES)
    meta_out[...] = placement(facts, tile_rows, v, t).reshape(2, count, 1, LANES)
    for i in range(PIECES):
        for j in range(height):
            add_x(j, i).wait_send()
        for j in range(1, height):
            add_z(j, i).wait_send()
    for i in range(LUMPS):
        for j in range(height):
            give_x(j, i).wait_send()

            @pl.when((j <= z) & (z < height - 1))
            def _():
                hand_z(j, 1, i).wait_send()

            @pl.when((j >= z) & (z > 0))
            def _():
                hand_z(j, -1, i).wait_send()


def canvas_kernel(lane, meta, subs, out, canvas):
    tiles, height, width = out.shape
    span = SUB * POLC
    canvas[:, pl.ds(SUB, height), :] = jnp.zeros((tiles, height, width + LANES), jnp.float32)

    def add_source(source, _):
        @pl.when(meta[source, FLAGS * BLK_DEV + lane] > 0)
        def _():
            add_blocks(source)

        return 0

    def add_blocks(source):
        for b in range(BLK_DEV):
            low = meta[source, lane + b]

            @pl.when(low > 0)
            def _():
                column = meta[source, 2 * BLK_DEV + b]
                sub = subs[source, b].astype(jnp.float32)
                sub = jnp.concatenate([sub, jnp.zeros((SUB, LANES), jnp.float32)], axis=1)
                sub = pltpu.roll(sub, column % LANES, 1)
                sub = jnp.concatenate([sub, jnp.zeros((ROWS, span + LANES), jnp.float32)], axis=0)
                sub = pltpu.roll(sub, low % ROWS, 0)
                top = pl.multiple_of(low // ROWS * ROWS, ROWS)
                base = pl.multiple_of(column // LANES * LANES, LANES)
                place = meta[source, b] if tiles > 1 else 0
                here = (place, pl.ds(top, SUB + ROWS), pl.ds(base, span + LANES))
                canvas[here] = canvas[here] + sub


    lax.fori_loop(0, subs.shape[0], add_source, 0, unroll=2)
    out[...] = canvas[:, pl.ds(SUB, height), pl.ds(0, width)].astype(out.dtype)


def slot_kernel(tiles, anchors, subs, out, meta):
    slots = out.shape[0]
    out[...] = jnp.zeros_like(out)
    lanes = lax.broadcasted_iota(jnp.int32, meta.shape, 1)
    places = jnp.full(meta.shape, -FAR, jnp.int32)
    for b in range(BLK_DEV):
        slot = tiles[0, b] * SCAP
        for before in range(b):
            slot = slot + jnp.where(tiles[0, before] == tiles[0, b], 1, 0)
        out[slot] = subs[b]
        places = jnp.where(lanes == slot, anchors[0, b], places)
        places = jnp.where(lanes == slots + slot, anchors[1, b], places)
    meta[...] = places


def gather_kernel(subs, meta, out, meta_out, own_sem, near_send, near_recv, far_send, far_recv):
    count = out.shape[0]
    width = out.shape[1]
    v, t = lax.axis_index("vis"), lax.axis_index("tile")
    half = count // 2
    spot = v // 2 * (1 - v % 2) + (count - 1 - v // 2) * (v % 2)

    def member(position):
        position = (position + 2 * count) % count
        back = position // half
        return (1 - back) * 2 * position + back * (2 * (count - 1 - position) + 1)

    barrier = pltpu.get_barrier_semaphore()
    for side in (1, -1):
        pl.semaphore_signal(
            barrier, inc=1, device_id=(member(spot + side), t), device_id_type=MESH
        )
    for k in range(1, width):
        pl.semaphore_signal(barrier, inc=1, device_id=(v, (t + k) % width), device_id_type=MESH)
    pl.semaphore_wait(barrier, 1 + width)

    def near(k):
        chunk = pl.ds((t + k) % width, 1)
        pairs = ((subs.at[chunk], out.at[v, pl.ds(t, 1)]), (meta, meta_out.at[v, t]))
        return [
            pltpu.make_async_remote_copy(
                src_ref=src,
                dst_ref=dst,
                send_sem=near_send.at[2 * k + i],
                recv_sem=near_recv.at[2 * k + i],
                device_id=(v, (t + k) % width),
                device_id_type=MESH,
            )
            for i, (src, dst) in enumerate(pairs)
        ]

    def own():
        pairs = ((subs.at[pl.ds(t, 1)], out.at[v, pl.ds(t, 1)]), (meta, meta_out.at[v, t]))
        return [
            pltpu.make_async_copy(src, dst, own_sem.at[i]) for i, (src, dst) in enumerate(pairs)
        ]

    def far(k, step):
        source = (t + width - k) % width
        cut = out.shape[2] // 2
        copies = []
        for i in range(3):
            side = 1 - 2 * (i % 2)
            origin = member(spot - side * step)
            if i < 2:
                ref = out.at[origin, source, pl.ds(i * cut, cut)]
            else:
                ref = meta_out.at[origin, source]
            copies.append(
                pltpu.make_async_remote_copy(
                    src_ref=ref,
                    dst_ref=ref,
                    send_sem=far_send.at[(step * width + k) * 3 + i],
                    recv_sem=far_recv.at[(step * width + k) * 3 + i],
                    device_id=(member(spot + side), t),
                    device_id_type=MESH,
                )
            )
        return copies

    for copy in own():
        copy.start()
    for k in range(1, width):
        for copy in near(k):
            copy.start()
    for copy in own():
        copy.wait()
    for k in range(width):
        if k:
            for copy in near(k):
                copy.wait_recv()
        for copy in far(k, 0):
            copy.start()

    def forward(step, _):
        for k in range(width):
            for landed, copy in zip(far(k, step - 1), far(k, step)):
                landed.wait_recv()
                copy.start()
        return 0

    lax.fori_loop(1, count - 1, forward, 0)
    for k in range(width):
        for copy in far(k, count - 2):
            copy.wait_recv()
    for k in range(1, width):
        for copy in near(k):
            copy.wait_send()

    def sent(step, _):
        for k in range(width):
            for copy in far(k, step):
                copy.wait_send()
        return 0

    lax.fori_loop(0, count - 1, sent, 0)


def place_kernel(tile_slots, meta, subs, out, canvas):
    v, t = lax.axis_index("vis"), lax.axis_index("tile")
    step = pl.program_id(0)
    slots = subs.shape[1]
    height = out.shape[1]
    width = out.shape[2]
    span = SUB * POLC

    @pl.when(step == 0)
    def _():
        canvas[...] = jnp.zeros_like(canvas)

    def add_source(near, _):
        source = step * (slots // tile_slots) + near
        for slot in range(tile_slots):
            lane = t * tile_slots + slot
            low = meta[source, lane] - v * height + SUB
            column = meta[source, slots + lane] * POLC

            @pl.when((low > 0) & (low < height + SUB))
            def _():
                sub = subs[0, near * tile_slots + slot].astype(jnp.float32)
                sub = jnp.concatenate([sub, jnp.zeros((SUB, LANES), jnp.float32)], axis=1)
                sub = pltpu.roll(sub, column % LANES, 1)
                sub = jnp.concatenate([sub, jnp.zeros((ROWS, span + LANES), jnp.float32)], axis=0)
                sub = pltpu.roll(sub, low % ROWS, 0)
                top = pl.multiple_of(low // ROWS * ROWS, ROWS)
                base = pl.multiple_of(column // LANES * LANES, LANES)
                here = (slot // SCAP, pl.ds(top, SUB + ROWS), pl.ds(base, span + LANES))
                canvas[here] = canvas[here] + sub

        return 0

    lax.fori_loop(0, slots // tile_slots, add_source, 0)

    @pl.when(step == pl.num_programs(0) - 1)
    def _():
        out[...] = canvas[:, pl.ds(SUB, height), pl.ds(0, width)]


def on_device(
    vis_data,
    u_cell,
    v_cell,
    u_frac,
    v_frac,
    w_plane,
    block_route,
    kernel_taps,
    taper_gain,
    sub_tile,
    sub_anchor,
):
    vis_count = lax.axis_size("vis")
    tile_width = lax.axis_size("tile")
    gt_dev = GT // tile_width
    rows, columns = vis_data.shape
    channels = u_cell.shape[0]
    slot_cap = max(2, 2 * rows // (BLK_DEV * vis_count))
    chunk = BLK_DEV * slot_cap
    grouped = (
        slot_cap * GROUP == LANES
        and channels % GROUP == 0
        and vis_count % 2 == 0
        and vis_count > 2
        and tile_width == 4
        and TS // vis_count % 32 == 0
    )
    features = columns + 4 * channels
    per_owner = gt_dev * SCAP
    slots = tile_width * per_owner
    height = TS // vis_count
    width = TS * POLC

    vmem = pl.BlockSpec(memory_space=pltpu.VMEM)
    if grouped:
        layers = vis_count // 2
        block = (SUB, SUB * POLC)
        lanes = channels // GROUP * LANES
        operands = (
            vis_data,
            u_cell,
            v_cell,
            u_frac,
            v_frac,
            w_plane,
            block_route.reshape(1, rows),
            kernel_taps.T,
            taper_gain,
            sub_tile.reshape(1, BLK_DEV),
            sub_anchor.T,
        )
        subs, meta = pl.pallas_call(
            functools.partial(reduce_kernel, slot_cap, height),
            in_specs=[pl.BlockSpec(memory_space=pltpu.HBM)] * len(operands),
            out_specs=[vmem] * 2,
            out_shape=[
                jax.ShapeDtypeStruct((2, vis_count, BLK_DEV) + block, jnp.bfloat16),
                jax.ShapeDtypeStruct((2, vis_count, 1, LANES), jnp.int32),
            ],
            scratch_shapes=[pltpu.VMEM(operand.shape, operand.dtype) for operand in operands]
            + [
                pltpu.VMEM((ROWS, LANES), jnp.float32),
                pltpu.VMEM(block, jnp.float32),
                pltpu.VMEM((features, rows), jnp.bfloat16),
                pltpu.VMEM((1, rows), jnp.int32),
                pltpu.VMEM((2, features, chunk), jnp.float32),
                pltpu.VMEM((GROUP, SUB, lanes), jnp.bfloat16),
                pltpu.VMEM((GROUP, SUB * POLC, lanes), jnp.bfloat16),
                pltpu.VMEM((channels // GROUP, SUB, LANES), jnp.float32),
                pltpu.VMEM((BLK_DEV,) + block, jnp.float32),
                pltpu.VMEM((layers, BLK_DEV) + block, jnp.bfloat16),
                pltpu.VMEM((layers, BLK_DEV) + block, jnp.bfloat16),
                pltpu.VMEM((layers - 1, BLK_DEV) + block, jnp.bfloat16),
                pltpu.VMEM((layers - 1, BLK_DEV) + block, jnp.bfloat16),
                pltpu.VMEM((1, LANES), jnp.int32),
                pltpu.SemaphoreType.DMA((len(operands),)),
            ]
            + [
                pltpu.SemaphoreType.DMA((lots,))
                for lots in [vis_count] * 2
                + [layers * PIECES] * 2
                + [(layers - 1) * PIECES] * 2
                + [2 * layers * LUMPS]
                + [layers * LUMPS] * 3
                + [vis_count] * 2
                + [1] * 2
            ],
            compiler_params=pltpu.CompilerParams(
                collective_id=1, has_side_effects=True, vmem_limit_bytes=VMEM_BYTES
            ),
            name="reduce",
        )(*[pltpu.with_memory_space_constraint(operand, pltpu.HBM) for operand in operands])
        meta = meta.reshape(2 * vis_count, LANES)
        subs = subs.reshape((2 * vis_count, BLK_DEV) + block)

        def canvas(lane, tiles, dtype):
            return pl.pallas_call(
                functools.partial(canvas_kernel, lane),
                grid_spec=pltpu.PrefetchScalarGridSpec(
                    num_scalar_prefetch=1,
                    grid=(1,),
                    in_specs=[vmem],
                    out_specs=vmem,
                    scratch_shapes=[
                        pltpu.VMEM((tiles, height + 2 * SUB + ROWS, width + LANES), jnp.float32),
                    ],
                ),
                out_shape=jax.ShapeDtypeStruct((tiles, height, width), dtype),
                compiler_params=pltpu.CompilerParams(vmem_limit_bytes=VMEM_BYTES),
                cost_estimate=pl.CostEstimate(
                    flops=GT * TS * width, bytes_accessed=8 * subs.size, transcendentals=0
                ),
                name="canvas",
            )(meta, subs)

        across = [(tile, (tile + 2) % tile_width) for tile in range(tile_width)]
        others = [
            lax.ppermute(canvas((3 + g) * BLK_DEV, 1, jnp.bfloat16), "tile", across)
            for g in range(gt_dev)
        ]
        own = canvas(BLK_DEV, gt_dev, jnp.float32)
        return own + jnp.concatenate(others, axis=0).astype(jnp.float32)

    send, table, taper = pl.pallas_call(
        functools.partial(dispatch_kernel, slot_cap),
        out_shape=[
            jax.ShapeDtypeStruct((vis_count, features, chunk), jnp.bfloat16),
            jax.ShapeDtypeStruct((ROWS, LANES), jnp.float32),
            jax.ShapeDtypeStruct((SUB, SUB * POLC), jnp.float32),
        ],
        scratch_shapes=[
            pltpu.VMEM((features, rows), jnp.bfloat16),
            pltpu.VMEM((1, rows), jnp.int32),
        ],
        name="dispatch",
    )(
        vis_data,
        u_cell,
        v_cell,
        u_frac,
        v_frac,
        w_plane,
        block_route.reshape(1, rows),
        kernel_taps.T,
        taper_gain,
    )
    covered = min(BLK_DEV, LANES // slot_cap)
    work = [
        pltpu.VMEM((BLK_DEV * SUB, SUB * POLC), jnp.float32),
        pltpu.VMEM((covered * SUB, channels * LANES), jnp.bfloat16),
        pltpu.VMEM((SUB * POLC, channels * LANES), jnp.bfloat16),
    ]
    gridded = jax.ShapeDtypeStruct((BLK_DEV, SUB, SUB * POLC), jnp.bfloat16)
    moved = lax.all_to_all(send, "vis", split_axis=0, concat_axis=0, tiled=True)
    moved = jnp.transpose(moved, (1, 0, 2)).reshape(1, features, vis_count * chunk)
    subs = pl.pallas_call(
        functools.partial(grid_kernel, slot_cap, chunk, channels),
        grid=(moved.shape[2] // LANES,),
        in_specs=[
            pl.BlockSpec((1, features, LANES), lambda s: (0, 0, s)),
            pl.BlockSpec(table.shape, lambda s: (0, 0)),
            pl.BlockSpec(taper.shape, lambda s: (0, 0)),
        ],
        out_specs=pl.BlockSpec(gridded.shape, lambda s: (0, 0, 0)),
        out_shape=gridded,
        scratch_shapes=work,
        name="grid",
    )(moved, table, taper)
    scalars = pl.BlockSpec(memory_space=pltpu.SMEM)
    subs, meta = pl.pallas_call(
        slot_kernel,
        in_specs=[scalars, scalars, vmem],
        out_specs=[vmem, vmem],
        out_shape=[
            jax.ShapeDtypeStruct((slots, SUB, SUB * POLC), jnp.bfloat16),
            jax.ShapeDtypeStruct((1, LANES), jnp.int32),
        ],
        name="slot",
    )(sub_tile.reshape(1, BLK_DEV), sub_anchor.T, subs)
    hops = (vis_count - 1) * tile_width * 3
    subs, meta = pl.pallas_call(
        gather_kernel,
        in_specs=[vmem, vmem],
        out_specs=[vmem, vmem],
        out_shape=[
            jax.ShapeDtypeStruct(
                (vis_count, tile_width, per_owner, SUB, SUB * POLC), jnp.bfloat16
            ),
            jax.ShapeDtypeStruct((vis_count, tile_width, 1, LANES), jnp.int32),
        ],
        scratch_shapes=[
            pltpu.SemaphoreType.DMA((2,)),
            pltpu.SemaphoreType.DMA((2 * tile_width,)),
            pltpu.SemaphoreType.DMA((2 * tile_width,)),
            pltpu.SemaphoreType.DMA((hops,)),
            pltpu.SemaphoreType.DMA((hops,)),
        ],
        compiler_params=pltpu.CompilerParams(collective_id=0, has_side_effects=True),
        name="gather",
    )(subs.reshape(tile_width, per_owner, SUB, SUB * POLC), meta)
    subs = subs.reshape(vis_count, slots, SUB, SUB * POLC)
    meta = meta.reshape(vis_count * tile_width, LANES)
    return pl.pallas_call(
        functools.partial(place_kernel, per_owner),
        grid_spec=pltpu.PrefetchScalarGridSpec(
            num_scalar_prefetch=1,
            grid=(vis_count,),
            in_specs=[pl.BlockSpec((1, slots, SUB, SUB * POLC), lambda s, *_: (s, 0, 0, 0))],
            out_specs=pl.BlockSpec((gt_dev, height, width), lambda s, *_: (0, 0, 0)),
            scratch_shapes=[
                pltpu.VMEM((gt_dev, -(-height // ROWS) * ROWS + 2 * SUB + ROWS, width + LANES), jnp.float32),
            ],
        ),
        out_shape=jax.ShapeDtypeStruct((gt_dev, height, width), jnp.float32),
        name="place",
    )(meta, subs)


def solution(mesh):
    placed = (
        P(("vis", "tile"), None),
        P(None, ("vis", "tile")),
        P(None, ("vis", "tile")),
        P(None, ("vis", "tile")),
        P(None, ("vis", "tile")),
        P(None, ("vis", "tile")),
        P(("vis", "tile"), None),
        P(),
        P(),
        P(("vis", "tile"), None),
        P(("vis", "tile"), None),
    )
    return jax.shard_map(
        on_device, mesh=mesh, in_specs=placed, out_specs=P("tile", "vis", None), check_vma=False
    )
```
